32 devices in a mesh: blk: 4 (over y, core), group: 8 (over z, x).
Axes of the slice: x: 2, y: 2, z: 4, core: 2. Of those that a mesh axis runs over, the one named last changes fastest.
Arguments:
- queries: bfloat16 [32, 16, 128], P(('blk', 'group')), may hold values from -2.5 to 2.5
- query_mask: int32 [32, 16], P(('blk', 'group')), may hold values from 0 to 1, as said below
- positive: int32 [32], P(('blk', 'group')), may hold values from 0 to 63
- page_vectors: bfloat16 [64, 128, 128], P(('blk', 'group')), may hold values from -2 to 2
- page_mask: int32 [64, 128], P(('blk', 'group')), may hold values from 0 to 1, as said below
Outputs:
- grad_queries: float32 [32, 16, 128], P(('blk', 'group'))
- grad_pages: float32 [64, 128, 128], P(('blk', 'group'))
- mean_loss: float32 [], replicated
The draws below stay inside these ranges and needn't reach their ends.
Inputs may be any that keep to these rules, and one draw needn't show every extreme that they name: `query_mask`: each row holds ones on its first 8 to 16 token slots and zeros after them. `page_mask`: each row holds ones on its first 32 to 128 patch slots and zeros after them.
All inputs are finite; a program needn't handle non-finite values.
Results may differ from the reference program's by a relative error of at most 0.0028.
Values may be sent and summed in bfloat16 or wider, within the bound.
No kernel may reach another device: no remote copies, remote signals or barrier semaphores. Data moves between devices by JAX's collectives and lax.ppermute only.
A program may use at most 64 MiB of HBM per device.

```python
import math
import jax
import jax.numpy as jnp
from jax import lax

D = 128
QT = 16
PATCH = 128
Q = 32
PAGES = 64


def draw_queries(key, part):
    own_key = jax.random.fold_in(key, 11)
    values = jnp.clip(0.36 * jax.random.normal(own_key, (Q, QT, D), jnp.float32), -2.5, 2.5)
    return values.astype(jnp.bfloat16)


def draw_page_vectors(key, part):
    own_key = jax.random.fold_in(key, 13)
    values = jnp.clip(0.36 * jax.random.normal(own_key, (PAGES, PATCH, D), jnp.float32), -2.0, 2.0)
    return values.astype(jnp.bfloat16)


def draw_query_mask(key, part):
    lengths = jax.random.randint(jax.random.fold_in(key, 17), (Q, 1), QT // 2, QT + 1)
    return (jnp.arange(QT, dtype=jnp.int32)[None, :] < lengths).astype(jnp.int32)


def draw_page_mask(key, part):
    lengths = jax.random.randint(jax.random.fold_in(key, 19), (PAGES, 1), PATCH // 4, PATCH + 1)
    return (jnp.arange(PATCH, dtype=jnp.int32)[None, :] < lengths).astype(jnp.int32)


def set_ends(drawn, key, smallest, largest):
    longest = drawn.shape.index(max(drawn.shape))
    spots = []
    for shift in (0, 1):
        where = [jax.random.randint(jax.random.fold_in(key, axis), (), 0, length) for axis, length in enumerate(drawn.shape)]
        where[longest] = (where[longest] + shift) % drawn.shape[longest]
        spots.append(tuple(where))
    return drawn.at[spots[0]].set(smallest).at[spots[1]].set(largest)


def setup_inputs(seed: int = 0) -> dict:
    key_of = jax.random.split(jax.random.key(seed), 6)
    return {
        "queries": draw_queries(jax.random.fold_in(key_of[5], 71), 0),
        "query_mask": draw_query_mask(jax.random.fold_in(key_of[5], 71), 0),
        "positive": set_ends(jax.random.randint(key_of[2], (Q,), 0, PAGES), jax.random.fold_in(key_of[2], 1), 0, PAGES - 1).astype(jnp.int32),
        "page_vectors": draw_page_vectors(jax.random.fold_in(key_of[5], 71), 0),
        "page_mask": draw_page_mask(jax.random.fold_in(key_of[5], 71), 0),
    }


relaxation_scale_factor = 0.5
guarded_floor_entry = -1.0e30


def masked_logits(question_embedding_matrix, lone_document, live_image_embeddings):
    similarity_matrix = jnp.dot(question_embedding_matrix, lone_document.T, preferred_element_type=jnp.float32) / relaxation_scale_factor
    return jnp.where(live_image_embeddings[None, :] > 0, similarity_matrix, guarded_floor_entry)


def reference(queries, query_mask, positive, page_vectors, page_mask):
    question_embedding_matrix = queries.reshape(Q * QT, D).astype(jnp.float32)
    vectors_wide = page_vectors.astype(jnp.float32)
    live_tokens = query_mask.astype(jnp.float32)
    document_region_number = jnp.sum(page_mask.astype(jnp.float32), axis=1)
    page_group = math.gcd(PAGES, 8)
    grouped_pages = vectors_wide.reshape(PAGES // page_group, page_group, PATCH, D)
    grouped_masks = page_mask.reshape(PAGES // page_group, page_group, PATCH)

    def forward(bundle):
        page_block, mask_block = bundle
        found_sums = []
        for number in range(page_group):
            masked = masked_logits(question_embedding_matrix, page_block[number], mask_block[number])
            highest = jnp.max(masked, axis=1, keepdims=True)
            found_sums.append(highest[:, 0] + jnp.log(jnp.sum(jnp.exp(masked - highest), axis=1)))
        return jnp.stack(found_sums)

    logsumexp_results = lax.map(forward, (grouped_pages, grouped_masks))
    linear_accumulated_totals = logsumexp_results.reshape(PAGES, Q, QT)
    softened_supremum = relaxation_scale_factor * (linear_accumulated_totals - jnp.log(document_region_number)[:, None, None])
    scores = jnp.sum(live_tokens[None] * softened_supremum, axis=2).T
    highest = jnp.max(scores, axis=1)
    totals = jnp.sum(jnp.exp(scores - highest[:, None]), axis=1)
    page_lse = highest + jnp.log(totals)
    chosen = positive[:, None] == jnp.arange(PAGES, dtype=jnp.int32)[None, :]
    picked = jnp.sum(jnp.where(chosen, scores, 0.0))
    mean_loss = (jnp.sum(page_lse) - picked) / Q
    coefficient = jnp.exp(scores - page_lse[:, None]) - chosen.astype(jnp.float32)
    factor_scale = (coefficient.T[:, :, None] * live_tokens[None]).reshape(PAGES // page_group, page_group, Q * QT)

    def backward(collected, bundle):
        page_block, mask_block, sums_block, scale_block = bundle
        outputs = []
        for number in range(page_group):
            masked = masked_logits(question_embedding_matrix, page_block[number], mask_block[number])
            weights = jnp.exp(masked - sums_block[number][:, None])
            factor = (scale_block[number][:, None] * weights).astype(jnp.bfloat16)
            factor = lax.optimization_barrier(factor).astype(jnp.float32)
            collected = collected + jnp.dot(factor, page_block[number], preferred_element_type=jnp.float32)
            outputs.append(jnp.dot(factor.T, question_embedding_matrix, preferred_element_type=jnp.float32))
        return collected, jnp.stack(outputs)

    collected, grad_blocks = lax.scan(backward, jnp.zeros((Q * QT, D), jnp.float32), (grouped_pages, grouped_masks, logsumexp_results, factor_scale))
    grad_pages = grad_blocks.reshape(PAGES, PATCH, D)
    grad_queries = collected.reshape(Q, QT, D)
    return grad_queries, grad_pages, mean_loss
```

```python
import functools
import math

import jax
import jax.numpy as jnp
from jax import lax
from jax.experimental import pallas as pl
from jax.experimental.pallas import tpu as pltpu
from jax.sharding import PartitionSpec as P

relaxation_scale_factor = 0.5
guarded_floor_entry = -1e30


def combined_all(part, axis, combine):
    gathered = jax.tree.map(lambda a: lax.all_gather(a, axis), part)

    def take(source):
        return jax.tree.map(lambda a: lax.dynamic_index_in_dim(a, source, 0, False), gathered)

    return lax.fori_loop(
        1, lax.axis_size(axis), lambda source, state: combine(state, take(source)), take(0)
    )


def from_behind(value, axis, steps):
    count = lax.axis_size(axis)
    pairs = [(source, (source + steps) % count) for source in range(count)]
    return lax.ppermute(value, axis, pairs)


def masked_logits(row_block, lone_document, live_image_embeddings):
    similarity_matrix = lax.dot_general(
        row_block, lone_document, (((1,), (1,)), ((), ())), preferred_element_type=jnp.float32
    )
    return jnp.where(
        live_image_embeddings[None, :] > 0,
        similarity_matrix / relaxation_scale_factor,
        guarded_floor_entry,
    )


def combine_parts(earlier, later):
    highest = jnp.maximum(earlier[0], later[0])
    totals = earlier[1] * jnp.exp(earlier[0] - highest) + later[1] * jnp.exp(later[0] - highest)
    return (highest, totals, earlier[2] + later[2])


def general_path(queries, query_mask, positive, page_vectors, page_mask):
    tokens = queries.shape[1]
    features = queries.shape[2]
    local_pages = page_vectors.shape[0]
    blocks = lax.axis_size("blk")
    members = lax.axis_size("group")
    bundle_size = queries.shape[0] * members
    total_queries = bundle_size * blocks
    natural_logarithm_lengths = jnp.log(jnp.sum(page_mask.astype(jnp.float32), axis=1))
    bundle_vectors, bundle_masks, bundle_targets = (
        lax.all_gather(queries, "group", axis=0, tiled=True),
        lax.all_gather(query_mask, "group", axis=0, tiled=True),
        lax.all_gather(positive, "group", axis=0, tiled=True),
    )

    def forward_piece(folded, shard_in, root_row):
        scores, lse_rows, live_all, owners, kept = folded
        vectors, token_masks, targets = shard_in
        amount = vectors.shape[0]
        stride = math.gcd(amount, max(1, 512 // tokens))

        def run_block(number, current):
            scores, lse_rows = current
            offset = number * stride
            slab_rows = lax.dynamic_slice_in_dim(vectors, offset, stride, 0).reshape(
                stride * tokens, features
            )
            alive = lax.dynamic_slice_in_dim(token_masks, offset, stride, 0).astype(jnp.float32)
            found_sums = []
            for index_page in range(local_pages):
                masked = masked_logits(slab_rows, page_vectors[index_page], page_mask[index_page])
                highest = jnp.max(masked, axis=1, keepdims=True)
                found_sums.append(
                    highest[:, 0] + jnp.log(jnp.sum(jnp.exp(masked - highest), axis=1))
                )
            logsumexp_results = jnp.stack(found_sums, axis=1).reshape(stride, tokens, local_pages)
            softened_supremum = relaxation_scale_factor * (
                logsumexp_results - natural_logarithm_lengths
            )
            page_score = jnp.sum(alive[:, :, None] * softened_supremum, axis=1)
            scores = lax.dynamic_update_slice_in_dim(scores, page_score, offset, 0)
            lse_rows = lax.dynamic_update_slice_in_dim(lse_rows, logsumexp_results, offset, 0)
            return (scores, lse_rows)

        scores, lse_rows = lax.fori_loop(0, amount // stride, run_block, (scores, lse_rows))
        live_all = lax.dynamic_update_slice_in_dim(live_all, token_masks, root_row, 0)
        owners = lax.dynamic_update_slice_in_dim(owners, targets, root_row, 0)
        kept = vectors
        return (scores, lse_rows, live_all, owners, kept)

    starting = (
        jnp.zeros((total_queries, local_pages), jnp.float32),
        jnp.zeros((total_queries, tokens, local_pages), jnp.float32),
        jnp.zeros((total_queries, tokens), jnp.int32),
        jnp.zeros((total_queries,), jnp.int32),
        jnp.zeros((total_queries, tokens, features), jnp.bfloat16),
    )
    scores, lse_rows, live_all, owners, kept = forward_piece(
        starting,
        (
            lax.all_gather(bundle_vectors, "blk", axis=0, tiled=True),
            lax.all_gather(bundle_masks, "blk", axis=0, tiled=True),
            lax.all_gather(bundle_targets, "blk", axis=0, tiled=True),
        ),
        jnp.int32(0),
    )
    position = lax.axis_index(("blk", "group"))
    page_ids = position * local_pages + jnp.arange(local_pages, dtype=jnp.int32)
    chosen = owners[:, None] == page_ids[None, :]
    picked_local = jnp.sum(jnp.where(chosen, scores, 0.0))
    local_top = jnp.max(scores, axis=1)
    local_total = jnp.sum(jnp.exp(scores - local_top[:, None]), axis=1)
    highest, totals, picked = combined_all(
        (local_top, local_total, picked_local), ("blk", "group"), combine_parts
    )
    page_lse = highest + jnp.log(totals)
    mean_loss = (jnp.sum(page_lse) - picked) / total_queries
    coefficient = jnp.exp(scores - page_lse[:, None]) - chosen.astype(jnp.float32)
    factor_scale = coefficient[:, None, :] * live_all.astype(jnp.float32)[:, :, None]

    def slice_rows(root_row, amount):
        sums = lax.dynamic_slice_in_dim(lse_rows, root_row, amount, 0).reshape(
            amount * tokens, local_pages
        )
        scales = lax.dynamic_slice_in_dim(factor_scale, root_row, amount, 0).reshape(
            amount * tokens, local_pages
        )
        return (sums, scales)

    def gradient_terms(row_block, logsumexp_results, scales, page_grads):
        partial_value = jnp.zeros(row_block.shape, jnp.float32)
        for number in range(local_pages):
            masked = masked_logits(row_block, page_vectors[number], page_mask[number])
            weights = jnp.exp(masked - logsumexp_results[:, number : number + 1])
            factor = (scales[:, number : number + 1] * weights).astype(jnp.bfloat16)
            partial_value = partial_value + jnp.dot(
                factor, page_vectors[number], preferred_element_type=jnp.float32
            )
            update = lax.dot_general(
                factor, row_block, (((0,), (0,)), ((), ())), preferred_element_type=jnp.float32
            )
            page_grads = page_grads.at[number].add(update)
        return (partial_value, page_grads)

    home = lax.axis_index("blk")
    page_grads = jnp.zeros(page_vectors.shape, jnp.float32)

    def visit_one(moving, collected, page_grads, lap_index):
        root_row = (home - lap_index) % blocks * bundle_size
        sums, scales = slice_rows(root_row, bundle_size)
        partial_value, page_grads = gradient_terms(
            moving.reshape(bundle_size * tokens, features), sums, scales, page_grads
        )
        return (collected + partial_value.reshape(bundle_size, tokens, features), page_grads)

    def pass_one(collected):
        return from_behind(collected, "blk", 1)

    def turn_one(lap_index, current):
        moving, collected, page_grads = current
        collected, page_grads = visit_one(moving, collected, page_grads, lap_index)
        moving = from_behind(moving, "blk", 1)
        return (moving, pass_one(collected), page_grads)

    empty_whole = jnp.zeros((bundle_size, tokens, features), jnp.float32)
    moving, collected, page_grads = lax.fori_loop(
        0, blocks - 1, turn_one, (bundle_vectors, empty_whole, page_grads)
    )
    collected, page_grads = visit_one(moving, collected, page_grads, blocks - 1)
    collected = pass_one(collected)
    grad_queries = lax.psum_scatter(collected, "group", scatter_dimension=0, tiled=True)
    return (grad_queries, page_grads, mean_loss)


LANES = 128
EXTRA = 8


def fits(queries, page_vectors, devices):
    tokens, features = queries.shape[1:]
    lanes = devices * tokens
    return (
        queries.shape[0] == 1
        and tokens % 8 == 0
        and LANES % tokens == 0
        and features == LANES
        and page_vectors.shape[1] == LANES
        and lanes % LANES == 0
        and 2 * (lanes // LANES) <= EXTRA
        and lax.axis_size("blk") % 2 == 0
    )


def segment_sum(values, width):
    lanes = values.shape[1]
    lane = lax.broadcasted_iota(jnp.int32, values.shape, 1)
    step = 1
    while step < width:
        ahead = pltpu.roll(values, lanes - step, 1)
        behind = pltpu.roll(values, step, 1)
        values = values + jnp.where((lane & step) == 0, ahead, behind)
        step *= 2
    return values


def split_half(value):
    scaled = value * 8193.0
    high = scaled - (scaled - value)
    return high, value - high


def middle_kernel(tokens, sent_ref, own_ref, other_ref, own_mask_ref, other_mask_ref, out_ref, weight_ref, stat_ref):
    sources = sent_ref.shape[0]
    lanes = sources * tokens
    chunks = lanes // LANES
    per_chunk = LANES // tokens
    local_pages = own_ref.shape[0]
    blk = lax.axis_index("blk")
    group = lax.axis_index("group")
    members = lax.axis_size("group")
    bases = [
        (blk * members + group) * local_pages,
        ((blk ^ 1) * members + group) * local_pages,
    ]

    extra = sent_ref[:, tokens : tokens + EXTRA, :].astype(jnp.float32)
    slot = lax.broadcasted_iota(jnp.int32, (EXTRA, LANES), 1) // tokens
    rows = []
    for chunk in range(chunks):
        total = jnp.zeros((EXTRA, LANES), jnp.float32)
        for i in range(per_chunk):
            total = jnp.where(slot == i, extra[chunk * per_chunk + i], total)
        rows.append(total)
    rows = jnp.concatenate(rows, axis=1)
    alive = rows[0:1]
    target = (rows[1:2] * 256.0 + rows[2:3]).astype(jnp.int32)

    rows_q = sent_ref[:, 0:tokens, :].reshape(lanes, LANES)
    patch = lax.broadcasted_iota(jnp.int32, (LANES, lanes), 0).astype(jnp.float32)
    tokens_soft, weights, ids = [], [], []
    for vectors_ref, mask_ref, base in (
        (own_ref, own_mask_ref, bases[0]),
        (other_ref, other_mask_ref, bases[1]),
    ):
        for number in range(local_pages):
            count = jnp.sum(mask_ref[number : number + 1, :].astype(jnp.float32), axis=1, keepdims=True)
            similarity = lax.dot_general(
                vectors_ref[number], rows_q, (((1,), (1,)), ((), ())), preferred_element_type=jnp.float32
            )
            masked = jnp.where(patch < count, similarity / relaxation_scale_factor, guarded_floor_entry)
            highest = jnp.max(masked, axis=0, keepdims=True)
            powers = jnp.exp(masked - highest)
            total = jnp.sum(powers, axis=0, keepdims=True)
            lse = highest + jnp.log(total)
            tokens_soft.append(alive * (relaxation_scale_factor * (lse - jnp.log(count))))
            weights.append(powers * (1.0 / total))
            ids.append(base + number)
    scores = segment_sum(jnp.concatenate(tokens_soft, axis=0), tokens)
    top = jnp.max(scores, axis=0, keepdims=True)
    chip_lse = top + jnp.log(jnp.sum(jnp.exp(scores - top), axis=0, keepdims=True))

    sends_sum = (blk & 1) == 0
    picked = jnp.zeros((1, lanes), jnp.float32)
    high_terms, low_terms = [], []
    for number in range(2 * local_pages):
        score = scores[number : number + 1]
        hit = target == ids[number]
        picked = picked + jnp.where(hit, score, 0.0)
        scale = alive * jnp.where(sends_sum, jnp.exp(score - chip_lse), hit.astype(jnp.float32))
        term = weights[number] * scale
        high = term.astype(jnp.bfloat16)
        high_terms.append(high)
        low_terms.append((term - high.astype(jnp.float32)).astype(jnp.bfloat16))
    vectors = jnp.concatenate([own_ref[...], other_ref[...]], axis=0).reshape(2 * local_pages * LANES, LANES)
    contract = (((0,), (0,)), ((), ()))
    mixed = lax.dot_general(
        vectors, jnp.concatenate(high_terms, axis=0), contract, preferred_element_type=jnp.float32
    ) + lax.dot_general(
        vectors, jnp.concatenate(low_terms, axis=0), contract, preferred_element_type=jnp.float32
    )
    out_ref[:, 0:tokens, :] = mixed.T.reshape(sources, tokens, LANES)
    high, low = split_half(jnp.where(sends_sum, chip_lse, picked))
    pieces = [high[:, c * LANES : (c + 1) * LANES] for c in range(chunks)]
    pieces += [jnp.zeros((1, LANES), jnp.float32)] * (EXTRA // 2 - chunks)
    pieces += [low[:, c * LANES : (c + 1) * LANES] for c in range(chunks)]
    pieces += [jnp.zeros((1, LANES), jnp.float32)] * (EXTRA // 2 - chunks)
    out_ref[:, tokens : tokens + EXTRA, :] = jnp.broadcast_to(
        jnp.concatenate(pieces, axis=0)[None], (sources, EXTRA, LANES)
    )
    for number in range(local_pages):
        weight_ref[number] = weights[number] * alive
        stat_ref[number : number + 1, :] = scores[number : number + 1]
        stat_ref[local_pages + number : local_pages + number + 1, :] = (target == ids[number]).astype(jnp.float32)


def last_kernel(tokens, got_ref, sent_ref, weight_ref, stat_ref, grad_q_ref, grad_p_ref, loss_ref):
    sources = sent_ref.shape[0]
    lanes = sources * tokens
    chunks = lanes // LANES
    local_pages = weight_ref.shape[0]
    blk = lax.axis_index("blk")
    group = lax.axis_index("group")
    members = lax.axis_size("group")
    me = blk * members + group
    even = [s for s in range(sources) if (s // members) % 2 == 0]
    odd = [s for s in range(sources) if (s // members) % 2 == 1]

    def stats(source):
        rows = got_ref[source, tokens : tokens + EXTRA, :]
        return rows + pltpu.roll(rows, EXTRA // 2, 0)

    chip_lse = [stats(s) for s in even]
    top = functools.reduce(jnp.maximum, chip_lse)
    page_lse = top + jnp.log(sum(jnp.exp(c - top) for c in chip_lse))
    picked = sum(stats(s) for s in odd)
    row = lax.broadcasted_iota(jnp.int32, (EXTRA, LANES), 0)
    lane = lax.broadcasted_iota(jnp.int32, (EXTRA, LANES), 1)
    difference = jnp.where(row < chunks, page_lse - picked, 0.0)
    loss_ref[...] = jnp.sum(
        jnp.sum(difference, axis=0, keepdims=True), axis=1, keepdims=True
    ) * (1.0 / (tokens * sources))

    mine = (row == me * tokens // LANES) & (lane == me * tokens % LANES)
    ratios = jnp.concatenate(
        [
            jnp.sum(jnp.where(mine, jnp.exp(c - page_lse), 0.0), axis=0, keepdims=True)
            for c in chip_lse
        ],
        axis=0,
    )
    ratios = jnp.broadcast_to(jnp.sum(ratios, axis=1, keepdims=True), ratios.shape)
    grad_q = jnp.zeros((tokens, LANES), jnp.float32)
    for i, s in enumerate(even):
        grad_q = grad_q + ratios[i : i + 1, :] * got_ref[s, 0:tokens, :]
    for s in odd:
        grad_q = grad_q - got_ref[s, 0:tokens, :]
    grad_q_ref[0] = grad_q

    flat = jnp.concatenate([page_lse[c : c + 1] for c in range(chunks)], axis=1)
    rows_q = sent_ref[:, 0:tokens, :].reshape(lanes, LANES)
    for number in range(local_pages):
        coefficient = (
            jnp.exp(stat_ref[number : number + 1, :] - flat)
            - stat_ref[local_pages + number : local_pages + number + 1, :]
        )
        factor = (coefficient * weight_ref[number]).astype(jnp.bfloat16)
        grad_p_ref[number] = jnp.dot(factor, rows_q, preferred_element_type=jnp.float32)


def exchange(blocks_to_all):
    return lax.all_to_all(blocks_to_all, ("blk", "group"), 0, 0, tiled=True)


def two_exchanges(queries, query_mask, positive, page_vectors, page_mask):
    tokens = queries.shape[1]
    local_pages = page_vectors.shape[0]
    devices = lax.axis_size("blk") * lax.axis_size("group")
    lanes = devices * tokens
    blocks = lax.axis_size("blk")
    swap = [(b, b ^ 1) for b in range(blocks)]
    other_vectors = lax.ppermute(page_vectors, "blk", swap)
    other_mask = lax.ppermute(page_mask, "blk", swap)

    kind = lax.broadcasted_iota(jnp.int32, (1, EXTRA, LANES), 1)
    number = positive[:, None, None]
    extra = jnp.where(
        kind == 0,
        jnp.tile(query_mask, (1, LANES // tokens))[:, None, :],
        jnp.where(kind == 1, number // 256, number % 256),
    ).astype(jnp.bfloat16)
    message = jnp.concatenate([queries, extra], axis=1)
    sent = exchange(jnp.broadcast_to(message, (devices, tokens + EXTRA, LANES)))

    vmem = pl.BlockSpec(memory_space=pltpu.VMEM)
    out, weights, stats = pl.pallas_call(
        functools.partial(middle_kernel, tokens),
        out_shape=(
            jax.ShapeDtypeStruct((devices, tokens + EXTRA, LANES), jnp.float32),
            jax.ShapeDtypeStruct((local_pages, LANES, lanes), jnp.float32),
            jax.ShapeDtypeStruct((2 * local_pages, lanes), jnp.float32),
        ),
        in_specs=[vmem] * 5,
        out_specs=(vmem, vmem, vmem),
    )(sent, page_vectors, other_vectors, page_mask, other_mask)
    got = exchange(out.astype(jnp.float16)).astype(jnp.float32)
    grad_q, grad_p, loss = pl.pallas_call(
        functools.partial(last_kernel, tokens),
        out_shape=(
            jax.ShapeDtypeStruct(queries.shape, jnp.float32),
            jax.ShapeDtypeStruct(page_vectors.shape, jnp.float32),
            jax.ShapeDtypeStruct((1, 1), jnp.float32),
        ),
        in_specs=[vmem] * 4,
        out_specs=(vmem, vmem, vmem),
    )(got, sent, weights, stats)
    return (grad_q, grad_p, loss[0, 0])


def on_device(queries, query_mask, positive, page_vectors, page_mask):
    devices = lax.axis_size("blk") * lax.axis_size("group")
    chosen = two_exchanges if fits(queries, page_vectors, devices) else general_path
    return chosen(queries, query_mask, positive, page_vectors, page_mask)


def solution(mesh):
    in_specs = (
        P(("blk", "group"), None, None),
        P(("blk", "group"), None),
        P(("blk", "group")),
        P(("blk", "group"), None, None),
        P(("blk", "group"), None),
    )
    out_specs = (P(("blk", "group"), None, None), P(("blk", "group"), None, None), P())
    return jax.shard_map(
        on_device, mesh=mesh, in_specs=in_specs, out_specs=out_specs, check_vma=False
    )
```

```python
import functools
import math

import jax
import jax.numpy as jnp
from jax import lax
from jax.experimental import pallas as pl
from jax.experimental.pallas import tpu as pltpu
from jax.sharding import PartitionSpec as P

relaxation_scale_factor = 0.5
guarded_floor_entry = -1e30


def combined_all(part, axis, combine):
    gathered = jax.tree.map(lambda a: lax.all_gather(a, axis), part)

    def take(source):
        return jax.tree.map(lambda a: lax.dynamic_index_in_dim(a, source, 0, False), gathered)

    return lax.fori_loop(
        1, lax.axis_size(axis), lambda source, state: combine(state, take(source)), take(0)
    )


def from_behind(value, axis, steps):
    count = lax.axis_size(axis)
    pairs = [(source, (source + steps) % count) for source in range(count)]
    return lax.ppermute(value, axis, pairs)


def masked_logits(row_block, lone_document, live_image_embeddings):
    similarity_matrix = lax.dot_general(
        row_block, lone_document, (((1,), (1,)), ((), ())), preferred_element_type=jnp.float32
    )
    return jnp.where(
        live_image_embeddings[None, :] > 0,
        similarity_matrix / relaxation_scale_factor,
        guarded_floor_entry,
    )


def combine_parts(earlier, later):
    highest = jnp.maximum(earlier[0], later[0])
    totals = earlier[1] * jnp.exp(earlier[0] - highest) + later[1] * jnp.exp(later[0] - highest)
    return (highest, totals, earlier[2] + later[2])


def general_path(queries, query_mask, positive, page_vectors, page_mask):
    tokens = queries.shape[1]
    features = queries.shape[2]
    local_pages = page_vectors.shape[0]
    blocks = lax.axis_size("blk")
    members = lax.axis_size("group")
    bundle_size = queries.shape[0] * members
    total_queries = bundle_size * blocks
    natural_logarithm_lengths = jnp.log(jnp.sum(page_mask.astype(jnp.float32), axis=1))
    bundle_vectors, bundle_masks, bundle_targets = (
        lax.all_gather(queries, "group", axis=0, tiled=True),
        lax.all_gather(query_mask, "group", axis=0, tiled=True),
        lax.all_gather(positive, "group", axis=0, tiled=True),
    )

    def forward_piece(folded, shard_in, root_row):
        scores, lse_rows, live_all, owners, kept = folded
        vectors, token_masks, targets = shard_in
        amount = vectors.shape[0]
        stride = math.gcd(amount, max(1, 512 // tokens))

        def run_block(number, current):
            scores, lse_rows = current
            offset = number * stride
            slab_rows = lax.dynamic_slice_in_dim(vectors, offset, stride, 0).reshape(
                stride * tokens, features
            )
            alive = lax.dynamic_slice_in_dim(token_masks, offset, stride, 0).astype(jnp.float32)
            found_sums = []
            for index_page in range(local_pages):
                masked = masked_logits(slab_rows, page_vectors[index_page], page_mask[index_page])
                highest = jnp.max(masked, axis=1, keepdims=True)
                found_sums.append(
                    highest[:, 0] + jnp.log(jnp.sum(jnp.exp(masked - highest), axis=1))
                )
            logsumexp_results = jnp.stack(found_sums, axis=1).reshape(stride, tokens, local_pages)
            softened_supremum = relaxation_scale_factor * (
                logsumexp_results - natural_logarithm_lengths
            )
            page_score = jnp.sum(alive[:, :, None] * softened_supremum, axis=1)
            scores = lax.dynamic_update_slice_in_dim(scores, page_score, offset, 0)
            lse_rows = lax.dynamic_update_slice_in_dim(lse_rows, logsumexp_results, offset, 0)
            return (scores, lse_rows)

        scores, lse_rows = lax.fori_loop(0, amount // stride, run_block, (scores, lse_rows))
        live_all = lax.dynamic_update_slice_in_dim(live_all, token_masks, root_row, 0)
        owners = lax.dynamic_update_slice_in_dim(owners, targets, root_row, 0)
        kept = vectors
        return (scores, lse_rows, live_all, owners, kept)

    starting = (
        jnp.zeros((total_queries, local_pages), jnp.float32),
        jnp.zeros((total_queries, tokens, local_pages), jnp.float32),
        jnp.zeros((total_queries, tokens), jnp.int32),
        jnp.zeros((total_queries,), jnp.int32),
        jnp.zeros((total_queries, tokens, features), jnp.bfloat16),
    )
    scores, lse_rows, live_all, owners, kept = forward_piece(
        starting,
        (
            lax.all_gather(bundle_vectors, "blk", axis=0, tiled=True),
            lax.all_gather(bundle_masks, "blk", axis=0, tiled=True),
            lax.all_gather(bundle_targets, "blk", axis=0, tiled=True),
        ),
        jnp.int32(0),
    )
    position = lax.axis_index(("blk", "group"))
    page_ids = position * local_pages + jnp.arange(local_pages, dtype=jnp.int32)
    chosen = owners[:, None] == page_ids[None, :]
    picked_local = jnp.sum(jnp.where(chosen, scores, 0.0))
    local_top = jnp.max(scores, axis=1)
    local_total = jnp.sum(jnp.exp(scores - local_top[:, None]), axis=1)
    highest, totals, picked = combined_all(
        (local_top, local_total, picked_local), ("blk", "group"), combine_parts
    )
    page_lse = highest + jnp.log(totals)
    mean_loss = (jnp.sum(page_lse) - picked) / total_queries
    coefficient = jnp.exp(scores - page_lse[:, None]) - chosen.astype(jnp.float32)
    factor_scale = coefficient[:, None, :] * live_all.astype(jnp.float32)[:, :, None]

    def slice_rows(root_row, amount):
        sums = lax.dynamic_slice_in_dim(lse_rows, root_row, amount, 0).reshape(
            amount * tokens, local_pages
        )
        scales = lax.dynamic_slice_in_dim(factor_scale, root_row, amount, 0).reshape(
            amount * tokens, local_pages
        )
        return (sums, scales)

    def gradient_terms(row_block, logsumexp_results, scales, page_grads):
        partial_value = jnp.zeros(row_block.shape, jnp.float32)
        for number in range(local_pages):
            masked = masked_logits(row_block, page_vectors[number], page_mask[number])
            weights = jnp.exp(masked - logsumexp_results[:, number : number + 1])
            factor = (scales[:, number : number + 1] * weights).astype(jnp.bfloat16)
            partial_value = partial_value + jnp.dot(
                factor, page_vectors[number], preferred_element_type=jnp.float32
            )
            update = lax.dot_general(
                factor, row_block, (((0,), (0,)), ((), ())), preferred_element_type=jnp.float32
            )
            page_grads = page_grads.at[number].add(update)
        return (partial_value, page_grads)

    home = lax.axis_index("blk")
    page_grads = jnp.zeros(page_vectors.shape, jnp.float32)

    def visit_one(moving, collected, page_grads, lap_index):
        root_row = (home - lap_index) % blocks * bundle_size
        sums, scales = slice_rows(root_row, bundle_size)
        partial_value, page_grads = gradient_terms(
            moving.reshape(bundle_size * tokens, features), sums, scales, page_grads
        )
        return (collected + partial_value.reshape(bundle_size, tokens, features), page_grads)

    def pass_one(collected):
        return from_behind(collected, "blk", 1)

    def turn_one(lap_index, current):
        moving, collected, page_grads = current
        collected, page_grads = visit_one(moving, collected, page_grads, lap_index)
        moving = from_behind(moving, "blk", 1)
        return (moving, pass_one(collected), page_grads)

    empty_whole = jnp.zeros((bundle_size, tokens, features), jnp.float32)
    moving, collected, page_grads = lax.fori_loop(
        0, blocks - 1, turn_one, (bundle_vectors, empty_whole, page_grads)
    )
    collected, page_grads = visit_one(moving, collected, page_grads, blocks - 1)
    collected = pass_one(collected)
    grad_queries = lax.psum_scatter(collected, "group", scatter_dimension=0, tiled=True)
    return (grad_queries, page_grads, mean_loss)


LANES = 128
EXTRA = 8
COUNTS = 3
KERNEL_VMEM = 16 * 2**20


def fits(queries, page_vectors, devices):
    tokens, features = queries.shape[1:]
    lanes = devices * tokens
    return (
        queries.shape[0] == 1
        and tokens % 8 == 0
        and LANES % tokens == 0
        and COUNTS + page_vectors.shape[0] <= EXTRA
        and features == LANES
        and page_vectors.shape[1] == LANES
        and lanes % LANES == 0
        and 2 * (lanes // LANES) <= EXTRA
        and lax.axis_size("blk") % 2 == 0
    )


def segment_sum(values, width):
    lanes = values.shape[1]
    lane = lax.broadcasted_iota(jnp.int32, values.shape, 1)
    step = 1
    while step < width:
        ahead = pltpu.roll(values, lanes - step, 1)
        behind = pltpu.roll(values, step, 1)
        values = values + jnp.where((lane & step) == 0, ahead, behind)
        step *= 2
    return values


def split_half(value):
    scaled = value * 8193.0
    high = scaled - (scaled - value)
    return high, value - high


def first_kernel(target_ref, queries_ref, query_mask_ref, page_mask_ref, out_ref):
    devices, _, _ = out_ref.shape
    tokens = queries_ref.shape[1]
    target = target_ref[0]
    alive = jnp.sum(query_mask_ref[...].astype(jnp.float32), axis=1, keepdims=True)
    row = lax.broadcasted_iota(jnp.int32, (EXTRA, LANES), 0)
    extra = jnp.where(row == 0, alive, 0.0)
    extra = jnp.where(row == 1, (target // 256).astype(jnp.float32), extra)
    extra = jnp.where(row == 2, (target % 256).astype(jnp.float32), extra)
    for number in range(page_mask_ref.shape[0]):
        count = jnp.sum(page_mask_ref[number : number + 1, :].astype(jnp.float32), axis=1, keepdims=True)
        extra = jnp.where(row == COUNTS + number, count, extra)
    out_ref[:, 0:tokens, :] = jnp.broadcast_to(queries_ref[...], (devices, tokens, LANES))
    out_ref[:, tokens : tokens + EXTRA, :] = jnp.broadcast_to(
        extra.astype(jnp.bfloat16)[None], (devices, EXTRA, LANES)
    )


def middle_kernel(tokens, sent_ref, own_ref, other_ref, out_ref, weight_ref, stat_ref):
    sources = sent_ref.shape[0]
    lanes = sources * tokens
    chunks = lanes // LANES
    per_chunk = LANES // tokens
    local_pages = own_ref.shape[0]
    blk = lax.axis_index("blk")
    group = lax.axis_index("group")
    members = lax.axis_size("group")
    homes = [blk * members + group, (blk ^ 1) * members + group]

    extra = sent_ref[:, tokens : tokens + EXTRA, :].astype(jnp.float32)
    slot = lax.broadcasted_iota(jnp.int32, (EXTRA, LANES), 1) // tokens
    rows = []
    for chunk in range(chunks):
        total = jnp.zeros((EXTRA, LANES), jnp.float32)
        for i in range(per_chunk):
            total = jnp.where(slot == i, extra[chunk * per_chunk + i], total)
        rows.append(total)
    rows = jnp.concatenate(rows, axis=1)
    spot = lax.broadcasted_iota(jnp.int32, (1, lanes), 1) % tokens
    alive = (spot.astype(jnp.float32) < rows[0:1]).astype(jnp.float32)
    target = (rows[1:2] * 256.0 + rows[2:3]).astype(jnp.int32)

    rows_q = sent_ref[:, 0:tokens, :].reshape(lanes, LANES)
    patch = lax.broadcasted_iota(jnp.int32, (LANES, lanes), 0).astype(jnp.float32)
    tokens_soft, weights, ids = [], [], []
    for vectors_ref, home in ((own_ref, homes[0]), (other_ref, homes[1])):
        facts = sent_ref[home, tokens : tokens + EXTRA, :].astype(jnp.float32)
        for number in range(local_pages):
            count = facts[COUNTS + number : COUNTS + number + 1, 0:1]
            similarity = lax.dot_general(
                vectors_ref[number], rows_q, (((1,), (1,)), ((), ())), preferred_element_type=jnp.float32
            )
            masked = jnp.where(patch < count, similarity / relaxation_scale_factor, guarded_floor_entry)
            highest = jnp.max(masked, axis=0, keepdims=True)
            powers = jnp.exp(masked - highest)
            total = jnp.sum(powers, axis=0, keepdims=True)
            lse = highest + jnp.log(total)
            tokens_soft.append(alive * (relaxation_scale_factor * (lse - jnp.log(count))))
            weights.append(powers * (1.0 / total))
            ids.append(home * local_pages + number)
    scores = segment_sum(jnp.concatenate(tokens_soft, axis=0), tokens)
    top = jnp.max(scores, axis=0, keepdims=True)
    chip_lse = top + jnp.log(jnp.sum(jnp.exp(scores - top), axis=0, keepdims=True))

    sends_sum = (blk & 1) == 0
    picked = jnp.zeros((1, lanes), jnp.float32)
    high_terms, low_terms = [], []
    for number in range(2 * local_pages):
        score = scores[number : number + 1]
        hit = target == ids[number]
        picked = picked + jnp.where(hit, score, 0.0)
        scale = alive * jnp.where(sends_sum, jnp.exp(score - chip_lse), hit.astype(jnp.float32))
        term = weights[number] * scale
        high = term.astype(jnp.bfloat16)
        high_terms.append(high)
        low_terms.append((term - high.astype(jnp.float32)).astype(jnp.bfloat16))
    vectors = jnp.concatenate([own_ref[...], other_ref[...]], axis=0).reshape(2 * local_pages * LANES, LANES)
    contract = (((0,), (0,)), ((), ()))
    mixed = lax.dot_general(
        vectors, jnp.concatenate(high_terms, axis=0), contract, preferred_element_type=jnp.float32
    ) + lax.dot_general(
        vectors, jnp.concatenate(low_terms, axis=0), contract, preferred_element_type=jnp.float32
    )
    out_ref[:, 0:tokens, :] = mixed.T.reshape(sources, tokens, LANES)
    high, low = split_half(jnp.where(sends_sum, chip_lse, picked))
    pieces = [high[:, c * LANES : (c + 1) * LANES] for c in range(chunks)]
    pieces += [jnp.zeros((1, LANES), jnp.float32)] * (EXTRA // 2 - chunks)
    pieces += [low[:, c * LANES : (c + 1) * LANES] for c in range(chunks)]
    pieces += [jnp.zeros((1, LANES), jnp.float32)] * (EXTRA // 2 - chunks)
    out_ref[:, tokens : tokens + EXTRA, :] = jnp.broadcast_to(
        jnp.concatenate(pieces, axis=0)[None], (sources, EXTRA, LANES)
    )
    for number in range(local_pages):
        weight_ref[number] = weights[number] * alive
        stat_ref[number : number + 1, :] = scores[number : number + 1]
        stat_ref[local_pages + number : local_pages + number + 1, :] = (target == ids[number]).astype(jnp.float32)


def last_kernel(tokens, got_ref, sent_ref, weight_ref, stat_ref, grad_q_ref, grad_p_ref, loss_ref):
    sources = sent_ref.shape[0]
    lanes = sources * tokens
    chunks = lanes // LANES
    local_pages = weight_ref.shape[0]
    blk = lax.axis_index("blk")
    group = lax.axis_index("group")
    members = lax.axis_size("group")
    me = blk * members + group
    even = [s for s in range(sources) if (s // members) % 2 == 0]
    odd = [s for s in range(sources) if (s // members) % 2 == 1]

    def stats(source):
        rows = got_ref[source, tokens : tokens + EXTRA, :]
        return rows + pltpu.roll(rows, EXTRA // 2, 0)

    chip_lse = [stats(s) for s in even]
    top = functools.reduce(jnp.maximum, chip_lse)
    page_lse = top + jnp.log(sum(jnp.exp(c - top) for c in chip_lse))
    picked = sum(stats(s) for s in odd)
    row = lax.broadcasted_iota(jnp.int32, (EXTRA, LANES), 0)
    lane = lax.broadcasted_iota(jnp.int32, (EXTRA, LANES), 1)
    difference = jnp.where(row < chunks, page_lse - picked, 0.0)
    loss_ref[...] = jnp.sum(
        jnp.sum(difference, axis=0, keepdims=True), axis=1, keepdims=True
    ) * (1.0 / (tokens * sources))

    mine = (row == me * tokens // LANES) & (lane == me * tokens % LANES)
    ratios = jnp.concatenate(
        [
            jnp.sum(jnp.where(mine, jnp.exp(c - page_lse), 0.0), axis=0, keepdims=True)
            for c in chip_lse
        ],
        axis=0,
    )
    ratios = jnp.broadcast_to(jnp.sum(ratios, axis=1, keepdims=True), ratios.shape)
    grad_q = jnp.zeros((tokens, LANES), jnp.float32)
    for i, s in enumerate(even):
        grad_q = grad_q + ratios[i : i + 1, :] * got_ref[s, 0:tokens, :]
    for s in odd:
        grad_q = grad_q - got_ref[s, 0:tokens, :]
    grad_q_ref[0] = grad_q

    flat = jnp.concatenate([page_lse[c : c + 1] for c in range(chunks)], axis=1)
    rows_q = sent_ref[:, 0:tokens, :].reshape(lanes, LANES)
    for number in range(local_pages):
        coefficient = (
            jnp.exp(stat_ref[number : number + 1, :] - flat)
            - stat_ref[local_pages + number : local_pages + number + 1, :]
        )
        factor = (coefficient * weight_ref[number]).astype(jnp.bfloat16)
        grad_p_ref[number] = jnp.dot(factor, rows_q, preferred_element_type=jnp.float32)


def exchange(blocks_to_all):
    return lax.all_to_all(blocks_to_all, ("blk", "group"), 0, 0, tiled=True)


def two_exchanges(queries, query_mask, positive, page_vectors, page_mask):
    tokens = queries.shape[1]
    local_pages = page_vectors.shape[0]
    devices = lax.axis_size("blk") * lax.axis_size("group")
    lanes = devices * tokens
    blocks = lax.axis_size("blk")
    swap = [(b, b ^ 1) for b in range(blocks)]
    other_vectors = lax.ppermute(page_vectors, "blk", swap)

    vmem = pl.BlockSpec(memory_space=pltpu.VMEM)
    params = pltpu.CompilerParams(vmem_limit_bytes=KERNEL_VMEM)
    message = pl.pallas_call(
        first_kernel,
        out_shape=jax.ShapeDtypeStruct((devices, tokens + EXTRA, LANES), jnp.bfloat16),
        in_specs=[pl.BlockSpec(memory_space=pltpu.SMEM)] + [vmem] * 3,
        out_specs=vmem,
        compiler_params=params,
    )(positive, queries, query_mask, page_mask)
    sent = exchange(message)
    out, weights, stats = pl.pallas_call(
        functools.partial(middle_kernel, tokens),
        out_shape=(
            jax.ShapeDtypeStruct((devices, tokens + EXTRA, LANES), jnp.float32),
            jax.ShapeDtypeStruct((local_pages, LANES, lanes), jnp.float32),
            jax.ShapeDtypeStruct((2 * local_pages, lanes), jnp.float32),
        ),
        in_specs=[vmem] * 3,
        out_specs=(vmem, vmem, vmem),
        compiler_params=params,
    )(sent, page_vectors, other_vectors)
    got = exchange(out.astype(jnp.float16)).astype(jnp.float32)
    grad_q, grad_p, loss = pl.pallas_call(
        functools.partial(last_kernel, tokens),
        out_shape=(
            jax.ShapeDtypeStruct(queries.shape, jnp.float32),
            jax.ShapeDtypeStruct(page_vectors.shape, jnp.float32),
            jax.ShapeDtypeStruct((1, 1), jnp.float32),
        ),
        in_specs=[vmem] * 4,
        out_specs=(vmem, vmem, vmem),
        compiler_params=params,
    )(got, sent, weights, stats)
    return (grad_q, grad_p, loss[0, 0])


def on_device(queries, query_mask, positive, page_vectors, page_mask):
    devices = lax.axis_size("blk") * lax.axis_size("group")
    chosen = two_exchanges if fits(queries, page_vectors, devices) else general_path
    return chosen(queries, query_mask, positive, page_vectors, page_mask)


def solution(mesh):
    in_specs = (
        P(("blk", "group"), None, None),
        P(("blk", "group"), None),
        P(("blk", "group")),
        P(("blk", "group"), None, None),
        P(("blk", "group"), None),
    )
    out_specs = (P(("blk", "group"), None, None), P(("blk", "group"), None, None), P())
    return jax.shard_map(
        on_device, mesh=mesh, in_specs=in_specs, out_specs=out_specs, check_vma=False
    )
```

```python
import functools
import math

import jax
import jax.numpy as jnp
from jax import lax
from jax.experimental import pallas as pl
from jax.experimental.pallas import tpu as pltpu
from jax.sharding import PartitionSpec as P

relaxation_scale_factor = 0.5
guarded_floor_entry = -1e30


def combined_all(part, axis, combine):
    gathered = jax.tree.map(lambda a: lax.all_gather(a, axis), part)

    def take(source):
        return jax.tree.map(lambda a: lax.dynamic_index_in_dim(a, source, 0, False), gathered)

    return lax.fori_loop(
        1, lax.axis_size(axis), lambda source, state: combine(state, take(source)), take(0)
    )


def from_behind(value, axis, steps):
    count = lax.axis_size(axis)
    pairs = [(source, (source + steps) % count) for source in range(count)]
    return lax.ppermute(value, axis, pairs)


def masked_logits(row_block, lone_document, live_image_embeddings):
    similarity_matrix = lax.dot_general(
        row_block, lone_document, (((1,), (1,)), ((), ())), preferred_element_type=jnp.float32
    )
    return jnp.where(
        live_image_embeddings[None, :] > 0,
        similarity_matrix / relaxation_scale_factor,
        guarded_floor_entry,
    )


def combine_parts(earlier, later):
    highest = jnp.maximum(earlier[0], later[0])
    totals = earlier[1] * jnp.exp(earlier[0] - highest) + later[1] * jnp.exp(later[0] - highest)
    return (highest, totals, earlier[2] + later[2])


def general_path(queries, query_mask, positive, page_vectors, page_mask):
    tokens = queries.shape[1]
    features = queries.shape[2]
    local_pages = page_vectors.shape[0]
    blocks = lax.axis_size("blk")
    members = lax.axis_size("group")
    bundle_size = queries.shape[0] * members
    total_queries = bundle_size * blocks
    natural_logarithm_lengths = jnp.log(jnp.sum(page_mask.astype(jnp.float32), axis=1))
    bundle_vectors, bundle_masks, bundle_targets = (
        lax.all_gather(queries, "group", axis=0, tiled=True),
        lax.all_gather(query_mask, "group", axis=0, tiled=True),
        lax.all_gather(positive, "group", axis=0, tiled=True),
    )

    def forward_piece(folded, shard_in, root_row):
        scores, lse_rows, live_all, owners, kept = folded
        vectors, token_masks, targets = shard_in
        amount = vectors.shape[0]
        stride = math.gcd(amount, max(1, 512 // tokens))

        def run_block(number, current):
            scores, lse_rows = current
            offset = number * stride
            slab_rows = lax.dynamic_slice_in_dim(vectors, offset, stride, 0).reshape(
                stride * tokens, features
            )
            alive = lax.dynamic_slice_in_dim(token_masks, offset, stride, 0).astype(jnp.float32)
            found_sums = []
            for index_page in range(local_pages):
                masked = masked_logits(slab_rows, page_vectors[index_page], page_mask[index_page])
                highest = jnp.max(masked, axis=1, keepdims=True)
                found_sums.append(
                    highest[:, 0] + jnp.log(jnp.sum(jnp.exp(masked - highest), axis=1))
                )
            logsumexp_results = jnp.stack(found_sums, axis=1).reshape(stride, tokens, local_pages)
            softened_supremum = relaxation_scale_factor * (
                logsumexp_results - natural_logarithm_lengths
            )
            page_score = jnp.sum(alive[:, :, None] * softened_supremum, axis=1)
            scores = lax.dynamic_update_slice_in_dim(scores, page_score, offset, 0)
            lse_rows = lax.dynamic_update_slice_in_dim(lse_rows, logsumexp_results, offset, 0)
            return (scores, lse_rows)

        scores, lse_rows = lax.fori_loop(0, amount // stride, run_block, (scores, lse_rows))
        live_all = lax.dynamic_update_slice_in_dim(live_all, token_masks, root_row, 0)
        owners = lax.dynamic_update_slice_in_dim(owners, targets, root_row, 0)
        kept = vectors
        return (scores, lse_rows, live_all, owners, kept)

    starting = (
        jnp.zeros((total_queries, local_pages), jnp.float32),
        jnp.zeros((total_queries, tokens, local_pages), jnp.float32),
        jnp.zeros((total_queries, tokens), jnp.int32),
        jnp.zeros((total_queries,), jnp.int32),
        jnp.zeros((total_queries, tokens, features), jnp.bfloat16),
    )
    scores, lse_rows, live_all, owners, kept = forward_piece(
        starting,
        (
            lax.all_gather(bundle_vectors, "blk", axis=0, tiled=True),
            lax.all_gather(bundle_masks, "blk", axis=0, tiled=True),
            lax.all_gather(bundle_targets, "blk", axis=0, tiled=True),
        ),
        jnp.int32(0),
    )
    position = lax.axis_index(("blk", "group"))
    page_ids = position * local_pages + jnp.arange(local_pages, dtype=jnp.int32)
    chosen = owners[:, None] == page_ids[None, :]
    picked_local = jnp.sum(jnp.where(chosen, scores, 0.0))
    local_top = jnp.max(scores, axis=1)
    local_total = jnp.sum(jnp.exp(scores - local_top[:, None]), axis=1)
    highest, totals, picked = combined_all(
        (local_top, local_total, picked_local), ("blk", "group"), combine_parts
    )
    page_lse = highest + jnp.log(totals)
    mean_loss = (jnp.sum(page_lse) - picked) / total_queries
    coefficient = jnp.exp(scores - page_lse[:, None]) - chosen.astype(jnp.float32)
    factor_scale = coefficient[:, None, :] * live_all.astype(jnp.float32)[:, :, None]

    def slice_rows(root_row, amount):
        sums = lax.dynamic_slice_in_dim(lse_rows, root_row, amount, 0).reshape(
            amount * tokens, local_pages
        )
        scales = lax.dynamic_slice_in_dim(factor_scale, root_row, amount, 0).reshape(
            amount * tokens, local_pages
        )
        return (sums, scales)

    def gradient_terms(row_block, logsumexp_results, scales, page_grads):
        partial_value = jnp.zeros(row_block.shape, jnp.float32)
        for number in range(local_pages):
            masked = masked_logits(row_block, page_vectors[number], page_mask[number])
            weights = jnp.exp(masked - logsumexp_results[:, number : number + 1])
            factor = (scales[:, number : number + 1] * weights).astype(jnp.bfloat16)
            partial_value = partial_value + jnp.dot(
                factor, page_vectors[number], preferred_element_type=jnp.float32
            )
            update = lax.dot_general(
                factor, row_block, (((0,), (0,)), ((), ())), preferred_element_type=jnp.float32
            )
            page_grads = page_grads.at[number].add(update)
        return (partial_value, page_grads)

    home = lax.axis_index("blk")
    page_grads = jnp.zeros(page_vectors.shape, jnp.float32)

    def visit_one(moving, collected, page_grads, lap_index):
        root_row = (home - lap_index) % blocks * bundle_size
        sums, scales = slice_rows(root_row, bundle_size)
        partial_value, page_grads = gradient_terms(
            moving.reshape(bundle_size * tokens, features), sums, scales, page_grads
        )
        return (collected + partial_value.reshape(bundle_size, tokens, features), page_grads)

    def pass_one(collected):
        return from_behind(collected, "blk", 1)

    def turn_one(lap_index, current):
        moving, collected, page_grads = current
        collected, page_grads = visit_one(moving, collected, page_grads, lap_index)
        moving = from_behind(moving, "blk", 1)
        return (moving, pass_one(collected), page_grads)

    empty_whole = jnp.zeros((bundle_size, tokens, features), jnp.float32)
    moving, collected, page_grads = lax.fori_loop(
        0, blocks - 1, turn_one, (bundle_vectors, empty_whole, page_grads)
    )
    collected, page_grads = visit_one(moving, collected, page_grads, blocks - 1)
    collected = pass_one(collected)
    grad_queries = lax.psum_scatter(collected, "group", scatter_dimension=0, tiled=True)
    return (grad_queries, page_grads, mean_loss)


LANES = 128
EXTRA = 2
FACTS = 16
WIDE_FIRST = 256
WIDE_SECOND = 256
KERNEL_VMEM = 16 * 2**20


def fits(queries, page_vectors, devices):
    tokens, features = queries.shape[1:]
    lanes = devices * tokens
    return (
        queries.shape[0] == 1
        and tokens == FACTS
        and features == LANES
        and page_vectors.shape[1] == LANES
        and page_vectors.shape[0] <= FACTS - 3
        and lanes % LANES == 0
        and lanes // LANES <= 8
        and lax.axis_size("blk") % 2 == 0
    )


def segment_sum(values, width):
    lanes = values.shape[1]
    lane = lax.broadcasted_iota(jnp.int32, values.shape, 1)
    step = 1
    while step < width:
        ahead = pltpu.roll(values, lanes - step, 1)
        behind = pltpu.roll(values, step, 1)
        values = values + jnp.where((lane & step) == 0, ahead, behind)
        step *= 2
    return values


def spread_runs(line, width):
    lane = lax.broadcasted_iota(jnp.int32, (8, LANES), 1)
    row = lax.broadcasted_iota(jnp.int32, (8, LANES), 0)
    return jnp.take_along_axis(jnp.broadcast_to(line, (8, LANES)), lane // width * width + row, axis=1)


def split_half(value):
    scaled = value * 8193.0
    high = scaled - (scaled - value)
    return high, value - high


def first_kernel(target_ref, queries_ref, query_mask_ref, page_mask_ref, out_ref, *scratch):
    target, queries, query_mask, page_mask, message, sems, out_sem = scratch
    devices = out_ref.shape[0]
    tokens = queries_ref.shape[1]
    loads = [
        pltpu.make_async_copy(src, dst, sems.at[i])
        for i, (src, dst) in enumerate(
            (
                (queries_ref, queries),
                (query_mask_ref, query_mask),
                (page_mask_ref, page_mask),
                (target_ref, target),
            )
        )
    ]
    for load in loads:
        load.start()
    for load in loads:
        load.wait()
    alive = jnp.sum(query_mask[...].astype(jnp.float32), axis=1, keepdims=True)
    kind = lax.broadcasted_iota(jnp.int32, (EXTRA, LANES), 1) % FACTS
    number = target[0]
    facts = jnp.where(kind == 0, alive, 0.0)
    facts = jnp.where(kind == 1, (number >> 8).astype(jnp.float32), facts)
    facts = jnp.where(kind == 2, (number & 255).astype(jnp.float32), facts)
    for page in range(page_mask.shape[0]):
        count = jnp.sum(page_mask[page : page + 1, :].astype(jnp.float32), axis=1, keepdims=True)
        facts = jnp.where(kind == 3 + page, count, facts)
    for pair in range(tokens // 2):
        message[:, pair] = jnp.broadcast_to(queries[:, 2 * pair : 2 * pair + 2, :], (devices, 2, LANES))
    message[:, tokens // 2] = jnp.broadcast_to(facts.astype(jnp.bfloat16)[None], (devices, EXTRA, LANES))
    store = pltpu.make_async_copy(message, out_ref, out_sem)
    store.start()
    store.wait()


def middle_kernel(tokens, sent_ref, own_ref, other_ref, out_ref, power_ref, stat_ref, rows_ref, other_power_ref):
    sources = sent_ref.shape[0]
    lanes = sources * tokens
    chunks = lanes // LANES
    per_chunk = LANES // tokens
    local_pages = own_ref.shape[0]
    blk = lax.axis_index("blk")
    group = lax.axis_index("group")
    members = lax.axis_size("group")
    homes = [blk * members + group, (blk ^ 1) * members + group]
    sends_sum = (blk & 1) == 0

    counts, ids, vectors, powers_refs = [], [], [], []
    for vectors_ref, kept_ref, home in ((own_ref, power_ref, homes[0]), (other_ref, other_power_ref, homes[1])):
        facts = sent_ref[home, tokens // 2].astype(jnp.float32)
        for number in range(local_pages):
            counts.append(facts[0:1, 3 + number : 4 + number])
            ids.append(home * local_pages + number)
            vectors.append(vectors_ref[number])
            powers_refs.append(kept_ref.at[number])
    slot = lax.broadcasted_iota(jnp.int32, (1, LANES), 1) // tokens
    spot = lax.broadcasted_iota(jnp.int32, (1, LANES), 1) % tokens
    steep = 1.0 / (relaxation_scale_factor * math.log(2.0))

    scales = []
    high_line = jnp.zeros((1, LANES), jnp.float32)
    low_line = jnp.zeros((1, LANES), jnp.float32)
    wide_first = math.gcd(WIDE_FIRST, lanes)
    for start in range(0, lanes, wide_first):
        columns = pl.ds(start, wide_first)
        facts = []
        for c in range(start // LANES, (start + wide_first) // LANES):
            told = jnp.zeros((1, LANES), jnp.float32)
            for i in range(per_chunk):
                told = jnp.where(
                    slot == i, sent_ref[c * per_chunk + i, tokens // 2, 0:1, :].astype(jnp.float32), told
                )
            facts.append(spread_runs(told, tokens))
        facts = jnp.concatenate(facts, axis=1)
        spots = lax.broadcasted_iota(jnp.int32, (1, wide_first), 1) % tokens
        alive = (spots.astype(jnp.float32) < facts[0:1]).astype(jnp.float32)
        target = (facts[1:2] * 256.0 + facts[2:3]).astype(jnp.int32)
        first, last = start // tokens, (start + wide_first) // tokens
        rows_q = sent_ref[first:last, 0 : tokens // 2].reshape(wide_first, LANES)
        rows_ref[columns, :] = rows_q

        softened, inverses = [], []
        patch = lax.broadcasted_iota(jnp.int32, (LANES, wide_first), 0).astype(jnp.float32)
        for page in range(2 * local_pages):
            similarity = lax.dot_general(
                vectors[page], rows_q, (((1,), (1,)), ((), ())), preferred_element_type=jnp.float32
            )
            masked = jnp.where(patch < counts[page], similarity, guarded_floor_entry)
            highest = jnp.max(masked, axis=0, keepdims=True)
            powers = jnp.exp2((masked - highest) * steep)
            powers_refs[page][:, columns] = powers
            total = jnp.sum(powers, axis=0, keepdims=True)
            lse = highest * (1.0 / relaxation_scale_factor) + jnp.log(total)
            softened.append(alive * (relaxation_scale_factor * (lse - jnp.log(counts[page]))))
            inverses.append(alive / total)
        scores = segment_sum(jnp.concatenate(softened, axis=0), tokens)
        top = jnp.max(scores, axis=0, keepdims=True)
        chip_lse = top + jnp.log(jnp.sum(jnp.exp(scores - top), axis=0, keepdims=True))

        picked = jnp.zeros((1, wide_first), jnp.float32)
        chunk_scales = []
        for page in range(2 * local_pages):
            score = scores[page : page + 1]
            hit = target == ids[page]
            picked = picked + jnp.where(hit, score, 0.0)
            share = jnp.where(sends_sum, jnp.exp(score - chip_lse), hit.astype(jnp.float32))
            chunk_scales.append(inverses[page] * share)
            if page < local_pages:
                for row, value in enumerate((score, hit.astype(jnp.float32), inverses[page])):
                    stat_ref[row * local_pages + page : row * local_pages + page + 1, columns] = value
        scales.append(chunk_scales)
        high, low = split_half(jnp.where(sends_sum, chip_lse, picked))
        for offset in range(0, wide_first, LANES):
            c = (start + offset) // LANES
            high_line = jnp.where(spot == c, high[:, offset : offset + LANES], high_line)
            low_line = jnp.where(spot == c, low[:, offset : offset + LANES], low_line)

    scales = [jnp.concatenate([part[page] for part in scales], axis=1) for page in range(2 * local_pages)]
    flipped = jnp.concatenate(vectors, axis=0).T
    wide_second = math.gcd(WIDE_SECOND, lanes)
    for start in range(0, lanes, wide_second):
        highs, lows = [], []
        for page in range(2 * local_pages):
            term = powers_refs[page][:, pl.ds(start, wide_second)] * scales[page][:, start : start + wide_second]
            high = term.astype(jnp.bfloat16)
            highs.append(high)
            lows.append((term - high.astype(jnp.float32)).astype(jnp.bfloat16))
        mixed = jnp.dot(flipped, jnp.concatenate(highs, axis=0), preferred_element_type=jnp.float32) + jnp.dot(
            flipped, jnp.concatenate(lows, axis=0), preferred_element_type=jnp.float32
        )
        first, last = start // tokens, (start + wide_second) // tokens
        out_ref[first:last, 0 : tokens // 2] = mixed.T.reshape(last - first, tokens // 2, 2, LANES)
    lines = jnp.concatenate([high_line, low_line], axis=0)
    out_ref[:, tokens // 2] = jnp.broadcast_to(lines[None], (sources, EXTRA, LANES))


def last_kernel(tokens, got_ref, rows_ref, power_ref, stat_ref, grad_q_out, grad_p_out, loss_out, *scratch):
    grad_q_ref, grad_p_ref, loss_ref, sems = scratch
    sources = got_ref.shape[0]
    lanes = sources * tokens
    chunks = lanes // LANES
    per_chunk = LANES // tokens
    local_pages = power_ref.shape[0]
    blk = lax.axis_index("blk")
    group = lax.axis_index("group")
    members = lax.axis_size("group")
    me = blk * members + group
    even = [s for s in range(sources) if (s // members) % 2 == 0]
    odd = [s for s in range(sources) if (s // members) % 2 == 1]

    def stats(source):
        return got_ref[source, tokens // 2, 0:1, :] + got_ref[source, tokens // 2, 1:2, :]

    def tree(combine, values):
        while len(values) > 1:
            values = [combine(*values[i : i + 2]) if i + 1 < len(values) else values[i] for i in range(0, len(values), 2)]
        return values[0]

    chip_lse = [stats(s) for s in even]
    top = tree(jnp.maximum, chip_lse)
    page_lse = top + jnp.log(tree(jnp.add, [jnp.exp(c - top) for c in chip_lse]))
    spread = spread_runs(page_lse, tokens)
    flat = jnp.concatenate([spread[c : c + 1] for c in range(chunks)], axis=1)
    rows_q = rows_ref[...]
    copies = []
    for page in range(local_pages):
        score, hit, inverse = (
            stat_ref[row * local_pages + page : row * local_pages + page + 1, :] for row in range(3)
        )
        coefficient = (jnp.exp(score - flat) - hit) * inverse
        factor = (coefficient * power_ref[page]).astype(jnp.bfloat16)
        grad_p_ref[page] = jnp.dot(factor, rows_q, preferred_element_type=jnp.float32)
        copies.append(pltpu.make_async_copy(grad_p_ref.at[page], grad_p_out.at[page], sems.at[page]))
        copies[-1].start()

    lane = lax.broadcasted_iota(jnp.int32, (1, LANES), 1)
    mine = lane == (me % per_chunk) * tokens + me // per_chunk
    ratios = jnp.concatenate([jnp.where(mine, jnp.exp(c - page_lse), 0.0) for c in chip_lse], axis=0)
    ratios = jnp.broadcast_to(jnp.sum(ratios, axis=1, keepdims=True), ratios.shape)
    grad_q = jnp.zeros((tokens // 2, 2, LANES), jnp.float32)
    for i, s in enumerate(even):
        grad_q = grad_q + ratios[i : i + 1, :][None] * got_ref[s, 0 : tokens // 2]
    for s in odd:
        grad_q = grad_q - got_ref[s, 0 : tokens // 2]
    for pair in range(tokens // 2):
        grad_q_ref[0, 2 * pair : 2 * pair + 2, :] = grad_q[pair]
    copies.append(pltpu.make_async_copy(grad_q_ref, grad_q_out, sems.at[local_pages]))
    copies[-1].start()

    picked = tree(jnp.add, [stats(s) for s in odd])
    difference = jnp.where(lane % tokens < chunks, page_lse - picked, 0.0)
    loss_ref[...] = jnp.sum(difference, axis=1, keepdims=True) * (1.0 / sources)
    copies.append(pltpu.make_async_copy(loss_ref, loss_out, sems.at[local_pages + 1]))
    copies[-1].start()
    for copy in copies:
        copy.wait()


def exchange(blocks_to_all):
    return lax.all_to_all(blocks_to_all, ("blk", "group"), 0, 0, tiled=True)


def two_exchanges(queries, query_mask, positive, page_vectors, page_mask):
    tokens = queries.shape[1]
    local_pages = page_vectors.shape[0]
    devices = lax.axis_size("blk") * lax.axis_size("group")
    lanes = devices * tokens
    blocks = lax.axis_size("blk")
    pairs = (tokens + EXTRA) // 2
    swap = [(b, b ^ 1) for b in range(blocks)]
    other_vectors = lax.ppermute(page_vectors, "blk", swap)

    vmem = pl.BlockSpec(memory_space=pltpu.VMEM)
    anywhere = pl.BlockSpec(memory_space=pl.ANY)
    params = pltpu.CompilerParams(vmem_limit_bytes=KERNEL_VMEM)
    message = pl.pallas_call(
        first_kernel,
        out_shape=jax.ShapeDtypeStruct((devices, pairs, 2, LANES), jnp.bfloat16),
        in_specs=[anywhere] * 4,
        out_specs=anywhere,
        scratch_shapes=[
            pltpu.SMEM(positive.shape, jnp.int32),
            pltpu.VMEM(queries.shape, jnp.bfloat16),
            pltpu.VMEM(query_mask.shape, jnp.int32),
            pltpu.VMEM(page_mask.shape, jnp.int32),
            pltpu.VMEM((devices, pairs, 2, LANES), jnp.bfloat16),
            pltpu.SemaphoreType.DMA((4,)),
            pltpu.SemaphoreType.DMA,
        ],
    )(positive, queries, query_mask, page_mask)
    sent = exchange(message)
    out, powers, stats, rows_q = pl.pallas_call(
        functools.partial(middle_kernel, tokens),
        out_shape=(
            jax.ShapeDtypeStruct((devices, pairs, 2, LANES), jnp.float32),
            jax.ShapeDtypeStruct((local_pages, LANES, lanes), jnp.float32),
            jax.ShapeDtypeStruct((3 * local_pages, lanes), jnp.float32),
            jax.ShapeDtypeStruct((lanes, LANES), jnp.bfloat16),
        ),
        in_specs=[vmem] * 3,
        out_specs=(vmem,) * 4,
        scratch_shapes=[pltpu.VMEM((local_pages, LANES, lanes), jnp.float32)],
        compiler_params=params,
    )(sent, page_vectors, other_vectors)
    got = exchange(out.astype(jnp.float16)).astype(jnp.float32)
    grad_q, grad_p, loss = pl.pallas_call(
        functools.partial(last_kernel, tokens),
        out_shape=(
            jax.ShapeDtypeStruct(queries.shape, jnp.float32),
            jax.ShapeDtypeStruct(page_vectors.shape, jnp.float32),
            jax.ShapeDtypeStruct((1, 1), jnp.float32),
        ),
        in_specs=[vmem] * 4,
        out_specs=(anywhere,) * 3,
        scratch_shapes=[
            pltpu.VMEM(queries.shape, jnp.float32),
            pltpu.VMEM(page_vectors.shape, jnp.float32),
            pltpu.VMEM((1, 1), jnp.float32),
            pltpu.SemaphoreType.DMA((local_pages + 2,)),
        ],
        compiler_params=params,
    )(got, rows_q, powers, stats)
    return (grad_q, grad_p, loss[0, 0])


def on_device(queries, query_mask, positive, page_vectors, page_mask):
    devices = lax.axis_size("blk") * lax.axis_size("group")
    chosen = two_exchanges if fits(queries, page_vectors, devices) else general_path
    return chosen(queries, query_mask, positive, page_vectors, page_mask)


def solution(mesh):
    in_specs = (
        P(("blk", "group"), None, None),
        P(("blk", "group"), None),
        P(("blk", "group")),
        P(("blk", "group"), None, None),
        P(("blk", "group"), None),
    )
    out_specs = (P(("blk", "group"), None, None), P(("blk", "group"), None, None), P())
    return jax.shard_map(
        on_device, mesh=mesh, in_specs=in_specs, out_specs=out_specs, check_vma=False
    )
```

```python
import functools
import math

import jax
import jax.numpy as jnp
from jax import lax
from jax.experimental import pallas as pl
from jax.experimental.pallas import tpu as pltpu
from jax.sharding import PartitionSpec as P

relaxation_scale_factor = 0.5
guarded_floor_entry = -1e30


def combined_all(part, axis, combine):
    gathered = jax.tree.map(lambda a: lax.all_gather(a, axis), part)

    def take(source):
        return jax.tree.map(lambda a: lax.dynamic_index_in_dim(a, source, 0, False), gathered)

    return lax.fori_loop(
        1, lax.axis_size(axis), lambda source, state: combine(state, take(source)), take(0)
    )


def from_behind(value, axis, steps):
    count = lax.axis_size(axis)
    pairs = [(source, (source + steps) % count) for source in range(count)]
    return lax.ppermute(value, axis, pairs)


def masked_logits(row_block, lone_document, live_image_embeddings):
    similarity_matrix = lax.dot_general(
        row_block, lone_document, (((1,), (1,)), ((), ())), preferred_element_type=jnp.float32
    )
    return jnp.where(
        live_image_embeddings[None, :] > 0,
        similarity_matrix / relaxation_scale_factor,
        guarded_floor_entry,
    )


def combine_parts(earlier, later):
    highest = jnp.maximum(earlier[0], later[0])
    totals = earlier[1] * jnp.exp(earlier[0] - highest) + later[1] * jnp.exp(later[0] - highest)
    return (highest, totals, earlier[2] + later[2])


def general_path(queries, query_mask, positive, page_vectors, page_mask):
    tokens = queries.shape[1]
    features = queries.shape[2]
    local_pages = page_vectors.shape[0]
    blocks = lax.axis_size("blk")
    members = lax.axis_size("group")
    bundle_size = queries.shape[0] * members
    total_queries = bundle_size * blocks
    natural_logarithm_lengths = jnp.log(jnp.sum(page_mask.astype(jnp.float32), axis=1))
    bundle_vectors, bundle_masks, bundle_targets = (
        lax.all_gather(queries, "group", axis=0, tiled=True),
        lax.all_gather(query_mask, "group", axis=0, tiled=True),
        lax.all_gather(positive, "group", axis=0, tiled=True),
    )

    def forward_piece(folded, shard_in, root_row):
        scores, lse_rows, live_all, owners, kept = folded
        vectors, token_masks, targets = shard_in
        amount = vectors.shape[0]
        stride = math.gcd(amount, max(1, 512 // tokens))

        def run_block(number, current):
            scores, lse_rows = current
            offset = number * stride
            slab_rows = lax.dynamic_slice_in_dim(vectors, offset, stride, 0).reshape(
                stride * tokens, features
            )
            alive = lax.dynamic_slice_in_dim(token_masks, offset, stride, 0).astype(jnp.float32)
            found_sums = []
            for index_page in range(local_pages):
                masked = masked_logits(slab_rows, page_vectors[index_page], page_mask[index_page])
                highest = jnp.max(masked, axis=1, keepdims=True)
                found_sums.append(
                    highest[:, 0] + jnp.log(jnp.sum(jnp.exp(masked - highest), axis=1))
                )
            logsumexp_results = jnp.stack(found_sums, axis=1).reshape(stride, tokens, local_pages)
            softened_supremum = relaxation_scale_factor * (
                logsumexp_results - natural_logarithm_lengths
            )
            page_score = jnp.sum(alive[:, :, None] * softened_supremum, axis=1)
            scores = lax.dynamic_update_slice_in_dim(scores, page_score, offset, 0)
            lse_rows = lax.dynamic_update_slice_in_dim(lse_rows, logsumexp_results, offset, 0)
            return (scores, lse_rows)

        scores, lse_rows = lax.fori_loop(0, amount // stride, run_block, (scores, lse_rows))
        live_all = lax.dynamic_update_slice_in_dim(live_all, token_masks, root_row, 0)
        owners = lax.dynamic_update_slice_in_dim(owners, targets, root_row, 0)
        kept = vectors
        return (scores, lse_rows, live_all, owners, kept)

    starting = (
        jnp.zeros((total_queries, local_pages), jnp.float32),
        jnp.zeros((total_queries, tokens, local_pages), jnp.float32),
        jnp.zeros((total_queries, tokens), jnp.int32),
        jnp.zeros((total_queries,), jnp.int32),
        jnp.zeros((total_queries, tokens, features), jnp.bfloat16),
    )
    scores, lse_rows, live_all, owners, kept = forward_piece(
        starting,
        (
            lax.all_gather(bundle_vectors, "blk", axis=0, tiled=True),
            lax.all_gather(bundle_masks, "blk", axis=0, tiled=True),
            lax.all_gather(bundle_targets, "blk", axis=0, tiled=True),
        ),
        jnp.int32(0),
    )
    position = lax.axis_index(("blk", "group"))
    page_ids = position * local_pages + jnp.arange(local_pages, dtype=jnp.int32)
    chosen = owners[:, None] == page_ids[None, :]
    picked_local = jnp.sum(jnp.where(chosen, scores, 0.0))
    local_top = jnp.max(scores, axis=1)
    local_total = jnp.sum(jnp.exp(scores - local_top[:, None]), axis=1)
    highest, totals, picked = combined_all(
        (local_top, local_total, picked_local), ("blk", "group"), combine_parts
    )
    page_lse = highest + jnp.log(totals)
    mean_loss = (jnp.sum(page_lse) - picked) / total_queries
    coefficient = jnp.exp(scores - page_lse[:, None]) - chosen.astype(jnp.float32)
    factor_scale = coefficient[:, None, :] * live_all.astype(jnp.float32)[:, :, None]

    def slice_rows(root_row, amount):
        sums = lax.dynamic_slice_in_dim(lse_rows, root_row, amount, 0).reshape(
            amount * tokens, local_pages
        )
        scales = lax.dynamic_slice_in_dim(factor_scale, root_row, amount, 0).reshape(
            amount * tokens, local_pages
        )
        return (sums, scales)

    def gradient_terms(row_block, logsumexp_results, scales, page_grads):
        partial_value = jnp.zeros(row_block.shape, jnp.float32)
        for number in range(local_pages):
            masked = masked_logits(row_block, page_vectors[number], page_mask[number])
            weights = jnp.exp(masked - logsumexp_results[:, number : number + 1])
            factor = (scales[:, number : number + 1] * weights).astype(jnp.bfloat16)
            partial_value = partial_value + jnp.dot(
                factor, page_vectors[number], preferred_element_type=jnp.float32
            )
            update = lax.dot_general(
                factor, row_block, (((0,), (0,)), ((), ())), preferred_element_type=jnp.float32
            )
            page_grads = page_grads.at[number].add(update)
        return (partial_value, page_grads)

    home = lax.axis_index("blk")
    page_grads = jnp.zeros(page_vectors.shape, jnp.float32)

    def visit_one(moving, collected, page_grads, lap_index):
        root_row = (home - lap_index) % blocks * bundle_size
        sums, scales = slice_rows(root_row, bundle_size)
        partial_value, page_grads = gradient_terms(
            moving.reshape(bundle_size * tokens, features), sums, scales, page_grads
        )
        return (collected + partial_value.reshape(bundle_size, tokens, features), page_grads)

    def pass_one(collected):
        return from_behind(collected, "blk", 1)

    def turn_one(lap_index, current):
        moving, collected, page_grads = current
        collected, page_grads = visit_one(moving, collected, page_grads, lap_index)
        moving = from_behind(moving, "blk", 1)
        return (moving, pass_one(collected), page_grads)

    empty_whole = jnp.zeros((bundle_size, tokens, features), jnp.float32)
    moving, collected, page_grads = lax.fori_loop(
        0, blocks - 1, turn_one, (bundle_vectors, empty_whole, page_grads)
    )
    collected, page_grads = visit_one(moving, collected, page_grads, blocks - 1)
    collected = pass_one(collected)
    grad_queries = lax.psum_scatter(collected, "group", scatter_dimension=0, tiled=True)
    return (grad_queries, page_grads, mean_loss)


LANES = 128
EXTRA = 2
FACTS = 16
WIDE_FIRST = 256
WIDE_SECOND = 256
KERNEL_VMEM = 16 * 2**20


def fits(queries, page_vectors, devices):
    tokens, features = queries.shape[1:]
    lanes = devices * tokens
    return (
        queries.shape[0] == 1
        and tokens == FACTS
        and features == LANES
        and page_vectors.shape[1] == LANES
        and page_vectors.shape[0] <= FACTS - 3
        and lanes % LANES == 0
        and lanes // LANES <= 8
        and lax.axis_size("blk") % 2 == 0
    )


def segment_sum(values, width):
    lanes = values.shape[1]
    lane = lax.broadcasted_iota(jnp.int32, values.shape, 1)
    step = 1
    while step < width:
        ahead = pltpu.roll(values, lanes - step, 1)
        behind = pltpu.roll(values, step, 1)
        values = values + jnp.where((lane & step) == 0, ahead, behind)
        step *= 2
    return values


def spread_runs(line, width):
    lane = lax.broadcasted_iota(jnp.int32, (8, LANES), 1)
    row = lax.broadcasted_iota(jnp.int32, (8, LANES), 0)
    return jnp.take_along_axis(jnp.broadcast_to(line, (8, LANES)), lane // width * width + row, axis=1)


def split_half(value):
    scaled = value * 8193.0
    high = scaled - (scaled - value)
    return high, value - high


def first_kernel(target_ref, queries_ref, query_mask_ref, page_mask_ref, out_ref, *scratch):
    queries, query_mask, page_mask, sems = scratch
    devices = out_ref.shape[0]
    tokens = queries_ref.shape[1]
    loads = [
        pltpu.make_async_copy(src, dst, sems.at[i])
        for i, (src, dst) in enumerate(
            (
                (queries_ref, queries),
                (query_mask_ref, query_mask),
                (page_mask_ref, page_mask),
            )
        )
    ]
    for load in loads:
        load.start()
    for load in loads:
        load.wait()
    alive = jnp.sum(query_mask[...].astype(jnp.float32), axis=1, keepdims=True)
    kind = lax.broadcasted_iota(jnp.int32, (EXTRA, LANES), 1) % FACTS
    number = target_ref[...].reshape(1, 1)
    facts = jnp.where(kind == 0, alive, 0.0)
    facts = jnp.where(kind == 1, (number >> 8).astype(jnp.float32), facts)
    facts = jnp.where(kind == 2, (number & 255).astype(jnp.float32), facts)
    for page in range(page_mask.shape[0]):
        count = jnp.sum(page_mask[page : page + 1, :].astype(jnp.float32), axis=1, keepdims=True)
        facts = jnp.where(kind == 3 + page, count, facts)
    out_rows = out_ref.reshape(devices, tokens + EXTRA, LANES)
    for device in range(devices):
        out_rows[device, 0:tokens, :] = queries[0]
    out_ref[:, tokens // 2] = jnp.broadcast_to(facts.astype(jnp.bfloat16)[None], (devices, EXTRA, LANES))


def middle_kernel(tokens, sent_ref, own_ref, other_ref, out_ref, power_ref, stat_ref, rows_ref, other_power_ref):
    sources = sent_ref.shape[0]
    lanes = sources * tokens
    chunks = lanes // LANES
    per_chunk = LANES // tokens
    local_pages = own_ref.shape[0]
    blk = lax.axis_index("blk")
    group = lax.axis_index("group")
    members = lax.axis_size("group")
    homes = [blk * members + group, (blk ^ 1) * members + group]
    sends_sum = (blk & 1) == 0

    counts, ids, vectors, powers_refs = [], [], [], []
    for vectors_ref, kept_ref, home in ((own_ref, power_ref, homes[0]), (other_ref, other_power_ref, homes[1])):
        facts = sent_ref[home, tokens // 2].astype(jnp.float32)
        for number in range(local_pages):
            counts.append(facts[0:1, 3 + number : 4 + number])
            ids.append(home * local_pages + number)
            vectors.append(vectors_ref[number])
            powers_refs.append(kept_ref.at[number])
    slot = lax.broadcasted_iota(jnp.int32, (1, LANES), 1) // tokens
    spot = lax.broadcasted_iota(jnp.int32, (1, LANES), 1) % tokens
    sent_rows = sent_ref.reshape(sources, tokens + EXTRA, LANES)
    out_rows = out_ref.reshape(sources, tokens + EXTRA, LANES)
    steep = 1.0 / (relaxation_scale_factor * math.log(2.0))

    scales = []
    high_line = jnp.zeros((1, LANES), jnp.float32)
    low_line = jnp.zeros((1, LANES), jnp.float32)
    wide_first = math.gcd(WIDE_FIRST, lanes)
    for start in range(0, lanes, wide_first):
        columns = pl.ds(start, wide_first)
        facts = []
        for c in range(start // LANES, (start + wide_first) // LANES):
            told = jnp.zeros((1, LANES), jnp.float32)
            for i in range(per_chunk):
                told = jnp.where(
                    slot == i, sent_ref[c * per_chunk + i, tokens // 2, 0:1, :].astype(jnp.float32), told
                )
            facts.append(spread_runs(told, tokens))
        facts = jnp.concatenate(facts, axis=1)
        spots = lax.broadcasted_iota(jnp.int32, (1, wide_first), 1) % tokens
        alive = (spots.astype(jnp.float32) < facts[0:1]).astype(jnp.float32)
        target = (facts[1:2] * 256.0 + facts[2:3]).astype(jnp.int32)
        first, last = start // tokens, (start + wide_first) // tokens
        for source in range(first, last):
            rows_ref[source * tokens : (source + 1) * tokens, :] = sent_rows[source, 0:tokens, :]
        rows_q = rows_ref[columns, :]

        softened, inverses = [], []
        patch = lax.broadcasted_iota(jnp.int32, (LANES, wide_first), 0).astype(jnp.float32)
        for page in range(2 * local_pages):
            similarity = lax.dot_general(
                vectors[page], rows_q, (((1,), (1,)), ((), ())), preferred_element_type=jnp.float32
            )
            masked = jnp.where(patch < counts[page], similarity, guarded_floor_entry)
            highest = jnp.max(masked, axis=0, keepdims=True)
            powers = jnp.exp2((masked - highest) * steep)
            powers_refs[page][:, columns] = powers
            total = jnp.sum(powers, axis=0, keepdims=True)
            lse = highest * (1.0 / relaxation_scale_factor) + jnp.log(total)
            softened.append(alive * (relaxation_scale_factor * (lse - jnp.log(counts[page]))))
            inverses.append(alive / total)
        scores = segment_sum(jnp.concatenate(softened, axis=0), tokens)
        top = jnp.max(scores, axis=0, keepdims=True)
        chip_lse = top + jnp.log(jnp.sum(jnp.exp(scores - top), axis=0, keepdims=True))

        picked = jnp.zeros((1, wide_first), jnp.float32)
        chunk_scales = []
        for page in range(2 * local_pages):
            score = scores[page : page + 1]
            hit = target == ids[page]
            picked = picked + jnp.where(hit, score, 0.0)
            share = jnp.where(sends_sum, jnp.exp(score - chip_lse), hit.astype(jnp.float32))
            chunk_scales.append(inverses[page] * share)
            if page < local_pages:
                for row, value in enumerate((score, hit.astype(jnp.float32), inverses[page])):
                    stat_ref[row * local_pages + page : row * local_pages + page + 1, columns] = value
        scales.append(chunk_scales)
        high, low = split_half(jnp.where(sends_sum, chip_lse, picked))
        for offset in range(0, wide_first, LANES):
            c = (start + offset) // LANES
            high_line = jnp.where(spot == c, high[:, offset : offset + LANES], high_line)
            low_line = jnp.where(spot == c, low[:, offset : offset + LANES], low_line)

    scales = [jnp.concatenate([part[page] for part in scales], axis=1) for page in range(2 * local_pages)]
    flipped = jnp.concatenate(vectors, axis=0).T
    wide_second = math.gcd(WIDE_SECOND, lanes)
    for start in range(0, lanes, wide_second):
        highs, lows = [], []
        for page in range(2 * local_pages):
            term = powers_refs[page][:, pl.ds(start, wide_second)] * scales[page][:, start : start + wide_second]
            high = term.astype(jnp.bfloat16)
            highs.append(high)
            lows.append((term - high.astype(jnp.float32)).astype(jnp.bfloat16))
        mixed = jnp.dot(flipped, jnp.concatenate(highs, axis=0), preferred_element_type=jnp.float32) + jnp.dot(
            flipped, jnp.concatenate(lows, axis=0), preferred_element_type=jnp.float32
        )
        mixed = mixed.T
        for source in range(start // tokens, (start + wide_second) // tokens):
            out_rows[source, 0:tokens, :] = mixed[source * tokens - start : (source + 1) * tokens - start, :]
    lines = jnp.concatenate([high_line, low_line], axis=0)
    out_ref[:, tokens // 2] = jnp.broadcast_to(lines[None], (sources, EXTRA, LANES))


def last_kernel(tokens, got_ref, rows_ref, power_ref, stat_ref, grad_q_out, grad_p_out, loss_out, *scratch):
    grad_q_ref, grad_p_ref, loss_ref, sems = scratch
    sources = got_ref.shape[0]
    lanes = sources * tokens
    chunks = lanes // LANES
    per_chunk = LANES // tokens
    local_pages = power_ref.shape[0]
    blk = lax.axis_index("blk")
    group = lax.axis_index("group")
    members = lax.axis_size("group")
    me = blk * members + group
    even = [s for s in range(sources) if (s // members) % 2 == 0]
    odd = [s for s in range(sources) if (s // members) % 2 == 1]

    def stats(source):
        return got_ref[source, tokens // 2, 0:1, :] + got_ref[source, tokens // 2, 1:2, :]

    def tree(combine, values):
        while len(values) > 1:
            values = [combine(*values[i : i + 2]) if i + 1 < len(values) else values[i] for i in range(0, len(values), 2)]
        return values[0]

    chip_lse = [stats(s) for s in even]
    top = tree(jnp.maximum, chip_lse)
    page_lse = top + jnp.log(tree(jnp.add, [jnp.exp(c - top) for c in chip_lse]))
    spread = spread_runs(page_lse, tokens)
    flat = jnp.concatenate([spread[c : c + 1] for c in range(chunks)], axis=1)
    rows_q = rows_ref[...]
    copies = []
    for page in range(local_pages):
        score, hit, inverse = (
            stat_ref[row * local_pages + page : row * local_pages + page + 1, :] for row in range(3)
        )
        coefficient = (jnp.exp(score - flat) - hit) * inverse
        factor = (coefficient * power_ref[page]).astype(jnp.bfloat16)
        grad_p_ref[page] = jnp.dot(factor, rows_q, preferred_element_type=jnp.float32)
        copies.append(pltpu.make_async_copy(grad_p_ref.at[page], grad_p_out.at[page], sems.at[page]))
        copies[-1].start()

    lane = lax.broadcasted_iota(jnp.int32, (1, LANES), 1)
    mine = lane == (me % per_chunk) * tokens + me // per_chunk
    ratios = jnp.concatenate([jnp.where(mine, jnp.exp(c - page_lse), 0.0) for c in chip_lse], axis=0)
    ratios = jnp.broadcast_to(jnp.sum(ratios, axis=1, keepdims=True), ratios.shape)
    got_rows = got_ref.reshape(sources, tokens + EXTRA, LANES)
    terms = [ratios[i : i + 1, :] * got_rows[s, 0:tokens, :] for i, s in enumerate(even)]
    grad_q_ref[0] = tree(jnp.add, terms) - tree(jnp.add, [got_rows[s, 0:tokens, :] for s in odd])
    copies.append(pltpu.make_async_copy(grad_q_ref, grad_q_out, sems.at[local_pages]))
    copies[-1].start()

    picked = tree(jnp.add, [stats(s) for s in odd])
    difference = jnp.where(lane % tokens < chunks, page_lse - picked, 0.0)
    loss_ref[...] = jnp.sum(difference, axis=1, keepdims=True) * (1.0 / sources)
    copies.append(pltpu.make_async_copy(loss_ref, loss_out, sems.at[local_pages + 1]))
    copies[-1].start()
    for copy in copies:
        copy.wait()


def exchange(blocks_to_all):
    return lax.all_to_all(blocks_to_all, ("blk", "group"), 0, 0, tiled=True)


def two_exchanges(queries, query_mask, positive, page_vectors, page_mask):
    tokens = queries.shape[1]
    local_pages = page_vectors.shape[0]
    devices = lax.axis_size("blk") * lax.axis_size("group")
    lanes = devices * tokens
    blocks = lax.axis_size("blk")
    pairs = (tokens + EXTRA) // 2
    swap = [(b, b ^ 1) for b in range(blocks)]
    other_vectors = lax.ppermute(page_vectors, "blk", swap)

    vmem = pl.BlockSpec(memory_space=pltpu.VMEM)
    anywhere = pl.BlockSpec(memory_space=pl.ANY)
    params = pltpu.CompilerParams(vmem_limit_bytes=KERNEL_VMEM)
    message = pl.pallas_call(
        first_kernel,
        out_shape=jax.ShapeDtypeStruct((devices, pairs, 2, LANES), jnp.bfloat16),
        in_specs=[vmem] + [pl.BlockSpec(memory_space=pltpu.HBM)] * 3,
        out_specs=vmem,
        compiler_params=params,
        scratch_shapes=[
            pltpu.VMEM(queries.shape, jnp.bfloat16),
            pltpu.VMEM(query_mask.shape, jnp.int32),
            pltpu.VMEM(page_mask.shape, jnp.int32),
            pltpu.SemaphoreType.DMA((3,)),
        ],
    )(positive, *[pltpu.with_memory_space_constraint(a, pltpu.HBM) for a in (queries, query_mask, page_mask)])
    message, other_vectors = lax.optimization_barrier((message, other_vectors))
    sent = exchange(message)
    out, powers, stats, rows_q = pl.pallas_call(
        functools.partial(middle_kernel, tokens),
        out_shape=(
            jax.ShapeDtypeStruct((devices, pairs, 2, LANES), jnp.float32),
            jax.ShapeDtypeStruct((local_pages, LANES, lanes), jnp.float32),
            jax.ShapeDtypeStruct((3 * local_pages, lanes), jnp.float32),
            jax.ShapeDtypeStruct((lanes, LANES), jnp.bfloat16),
        ),
        in_specs=[vmem] * 3,
        out_specs=(vmem,) * 4,
        scratch_shapes=[pltpu.VMEM((local_pages, LANES, lanes), jnp.float32)],
        compiler_params=params,
    )(sent, page_vectors, other_vectors)
    got = exchange(out.astype(jnp.float16)).astype(jnp.float32)
    grad_q, grad_p, loss = pl.pallas_call(
        functools.partial(last_kernel, tokens),
        out_shape=(
            jax.ShapeDtypeStruct(queries.shape, jnp.float32),
            jax.ShapeDtypeStruct(page_vectors.shape, jnp.float32),
            jax.ShapeDtypeStruct((1, 1), jnp.float32),
        ),
        in_specs=[vmem] * 4,
        out_specs=(anywhere,) * 3,
        scratch_shapes=[
            pltpu.VMEM(queries.shape, jnp.float32),
            pltpu.VMEM(page_vectors.shape, jnp.float32),
            pltpu.VMEM((1, 1), jnp.float32),
            pltpu.SemaphoreType.DMA((local_pages + 2,)),
        ],
        compiler_params=params,
    )(got, rows_q, powers, stats)
    return (grad_q, grad_p, loss[0, 0])


def on_device(queries, query_mask, positive, page_vectors, page_mask):
    devices = lax.axis_size("blk") * lax.axis_size("group")
    chosen = two_exchanges if fits(queries, page_vectors, devices) else general_path
    return chosen(queries, query_mask, positive, page_vectors, page_mask)


def solution(mesh):
    in_specs = (
        P(("blk", "group"), None, None),
        P(("blk", "group"), None),
        P(("blk", "group")),
        P(("blk", "group"), None, None),
        P(("blk", "group"), None),
    )
    out_specs = (P(("blk", "group"), None, None), P(("blk", "group"), None, None), P())
    return jax.shard_map(
        on_device, mesh=mesh, in_specs=in_specs, out_specs=out_specs, check_vma=False
    )
```

```python
import functools
import math

import jax
import jax.numpy as jnp
from jax import lax
from jax.experimental import pallas as pl
from jax.experimental.pallas import tpu as pltpu
from jax.sharding import PartitionSpec as P

relaxation_scale_factor = 0.5
guarded_floor_entry = -1e30


def combined_all(part, axis, combine):
    gathered = jax.tree.map(lambda a: lax.all_gather(a, axis), part)

    def take(source):
        return jax.tree.map(lambda a: lax.dynamic_index_in_dim(a, source, 0, False), gathered)

    return lax.fori_loop(
        1, lax.axis_size(axis), lambda source, state: combine(state, take(source)), take(0)
    )


def from_behind(value, axis, steps):
    count = lax.axis_size(axis)
    pairs = [(source, (source + steps) % count) for source in range(count)]
    return lax.ppermute(value, axis, pairs)


def masked_logits(row_block, lone_document, live_image_embeddings):
    similarity_matrix = lax.dot_general(
        row_block, lone_document, (((1,), (1,)), ((), ())), preferred_element_type=jnp.float32
    )
    return jnp.where(
        live_image_embeddings[None, :] > 0,
        similarity_matrix / relaxation_scale_factor,
        guarded_floor_entry,
    )


def combine_parts(earlier, later):
    highest = jnp.maximum(earlier[0], later[0])
    totals = earlier[1] * jnp.exp(earlier[0] - highest) + later[1] * jnp.exp(later[0] - highest)
    return (highest, totals, earlier[2] + later[2])


def general_path(queries, query_mask, positive, page_vectors, page_mask):
    tokens = queries.shape[1]
    features = queries.shape[2]
    local_pages = page_vectors.shape[0]
    blocks = lax.axis_size("blk")
    members = lax.axis_size("group")
    bundle_size = queries.shape[0] * members
    total_queries = bundle_size * blocks
    natural_logarithm_lengths = jnp.log(jnp.sum(page_mask.astype(jnp.float32), axis=1))
    bundle_vectors, bundle_masks, bundle_targets = (
        lax.all_gather(queries, "group", axis=0, tiled=True),
        lax.all_gather(query_mask, "group", axis=0, tiled=True),
        lax.all_gather(positive, "group", axis=0, tiled=True),
    )

    def forward_piece(folded, shard_in, root_row):
        scores, lse_rows, live_all, owners, kept = folded
        vectors, token_masks, targets = shard_in
        amount = vectors.shape[0]
        stride = math.gcd(amount, max(1, 512 // tokens))

        def run_block(number, current):
            scores, lse_rows = current
            offset = number * stride
            slab_rows = lax.dynamic_slice_in_dim(vectors, offset, stride, 0).reshape(
                stride * tokens, features
            )
            alive = lax.dynamic_slice_in_dim(token_masks, offset, stride, 0).astype(jnp.float32)
            found_sums = []
            for index_page in range(local_pages):
                masked = masked_logits(slab_rows, page_vectors[index_page], page_mask[index_page])
                highest = jnp.max(masked, axis=1, keepdims=True)
                found_sums.append(
                    highest[:, 0] + jnp.log(jnp.sum(jnp.exp(masked - highest), axis=1))
                )
            logsumexp_results = jnp.stack(found_sums, axis=1).reshape(stride, tokens, local_pages)
            softened_supremum = relaxation_scale_factor * (
                logsumexp_results - natural_logarithm_lengths
            )
            page_score = jnp.sum(alive[:, :, None] * softened_supremum, axis=1)
            scores = lax.dynamic_update_slice_in_dim(scores, page_score, offset, 0)
            lse_rows = lax.dynamic_update_slice_in_dim(lse_rows, logsumexp_results, offset, 0)
            return (scores, lse_rows)

        scores, lse_rows = lax.fori_loop(0, amount // stride, run_block, (scores, lse_rows))
        live_all = lax.dynamic_update_slice_in_dim(live_all, token_masks, root_row, 0)
        owners = lax.dynamic_update_slice_in_dim(owners, targets, root_row, 0)
        kept = vectors
        return (scores, lse_rows, live_all, owners, kept)

    starting = (
        jnp.zeros((total_queries, local_pages), jnp.float32),
        jnp.zeros((total_queries, tokens, local_pages), jnp.float32),
        jnp.zeros((total_queries, tokens), jnp.int32),
        jnp.zeros((total_queries,), jnp.int32),
        jnp.zeros((total_queries, tokens, features), jnp.bfloat16),
    )
    scores, lse_rows, live_all, owners, kept = forward_piece(
        starting,
        (
            lax.all_gather(bundle_vectors, "blk", axis=0, tiled=True),
            lax.all_gather(bundle_masks, "blk", axis=0, tiled=True),
            lax.all_gather(bundle_targets, "blk", axis=0, tiled=True),
        ),
        jnp.int32(0),
    )
    position = lax.axis_index(("blk", "group"))
    page_ids = position * local_pages + jnp.arange(local_pages, dtype=jnp.int32)
    chosen = owners[:, None] == page_ids[None, :]
    picked_local = jnp.sum(jnp.where(chosen, scores, 0.0))
    local_top = jnp.max(scores, axis=1)
    local_total = jnp.sum(jnp.exp(scores - local_top[:, None]), axis=1)
    highest, totals, picked = combined_all(
        (local_top, local_total, picked_local), ("blk", "group"), combine_parts
    )
    page_lse = highest + jnp.log(totals)
    mean_loss = (jnp.sum(page_lse) - picked) / total_queries
    coefficient = jnp.exp(scores - page_lse[:, None]) - chosen.astype(jnp.float32)
    factor_scale = coefficient[:, None, :] * live_all.astype(jnp.float32)[:, :, None]

    def slice_rows(root_row, amount):
        sums = lax.dynamic_slice_in_dim(lse_rows, root_row, amount, 0).reshape(
            amount * tokens, local_pages
        )
        scales = lax.dynamic_slice_in_dim(factor_scale, root_row, amount, 0).reshape(
            amount * tokens, local_pages
        )
        return (sums, scales)

    def gradient_terms(row_block, logsumexp_results, scales, page_grads):
        partial_value = jnp.zeros(row_block.shape, jnp.float32)
        for number in range(local_pages):
            masked = masked_logits(row_block, page_vectors[number], page_mask[number])
            weights = jnp.exp(masked - logsumexp_results[:, number : number + 1])
            factor = (scales[:, number : number + 1] * weights).astype(jnp.bfloat16)
            partial_value = partial_value + jnp.dot(
                factor, page_vectors[number], preferred_element_type=jnp.float32
            )
            update = lax.dot_general(
                factor, row_block, (((0,), (0,)), ((), ())), preferred_element_type=jnp.float32
            )
            page_grads = page_grads.at[number].add(update)
        return (partial_value, page_grads)

    home = lax.axis_index("blk")
    page_grads = jnp.zeros(page_vectors.shape, jnp.float32)

    def visit_one(moving, collected, page_grads, lap_index):
        root_row = (home - lap_index) % blocks * bundle_size
        sums, scales = slice_rows(root_row, bundle_size)
        partial_value, page_grads = gradient_terms(
            moving.reshape(bundle_size * tokens, features), sums, scales, page_grads
        )
        return (collected + partial_value.reshape(bundle_size, tokens, features), page_grads)

    def pass_one(collected):
        return from_behind(collected, "blk", 1)

    def turn_one(lap_index, current):
        moving, collected, page_grads = current
        collected, page_grads = visit_one(moving, collected, page_grads, lap_index)
        moving = from_behind(moving, "blk", 1)
        return (moving, pass_one(collected), page_grads)

    empty_whole = jnp.zeros((bundle_size, tokens, features), jnp.float32)
    moving, collected, page_grads = lax.fori_loop(
        0, blocks - 1, turn_one, (bundle_vectors, empty_whole, page_grads)
    )
    collected, page_grads = visit_one(moving, collected, page_grads, blocks - 1)
    collected = pass_one(collected)
    grad_queries = lax.psum_scatter(collected, "group", scatter_dimension=0, tiled=True)
    return (grad_queries, page_grads, mean_loss)


LANES = 128
EXTRA = 2
FACTS = 16
KERNEL_VMEM = 16 * 2**20


def fits(queries, page_vectors, devices):
    tokens, features = queries.shape[1:]
    lanes = devices * tokens
    return (
        queries.shape[0] == 1
        and tokens == FACTS
        and features == LANES
        and page_vectors.shape[1] == LANES
        and page_vectors.shape[0] <= FACTS - 3
        and lanes % LANES == 0
        and lanes // LANES <= 8
        and lax.axis_size("blk") % 2 == 0
    )


def segment_sum(values, width):
    lanes = values.shape[1]
    lane = lax.broadcasted_iota(jnp.int32, values.shape, 1)
    step = 1
    while step < width:
        ahead = pltpu.roll(values, lanes - step, 1)
        behind = pltpu.roll(values, step, 1)
        values = values + jnp.where((lane & step) == 0, ahead, behind)
        step *= 2
    return values


def spread_runs(line, width):
    lane = lax.broadcasted_iota(jnp.int32, (8, LANES), 1)
    row = lax.broadcasted_iota(jnp.int32, (8, LANES), 0)
    return jnp.take_along_axis(jnp.broadcast_to(line, (8, LANES)), lane // width * width + row, axis=1)


def split_half(value):
    scaled = value * 8193.0
    high = scaled - (scaled - value)
    return high, value - high


def first_kernel(target_ref, queries_ref, query_mask_ref, page_mask_ref, out_ref, *scratch):
    queries, query_mask, page_mask, sems = scratch
    devices = out_ref.shape[0]
    half = queries_ref.shape[1] // 2
    members = lax.axis_size("group")
    loads = [
        pltpu.make_async_copy(src, dst, sems.at[i])
        for i, (src, dst) in enumerate(
            (
                (queries_ref, queries),
                (query_mask_ref, query_mask),
                (page_mask_ref, page_mask),
            )
        )
    ]
    for load in loads:
        load.start()
    for load in loads:
        load.wait()
    alive = jnp.sum(query_mask[...].astype(jnp.float32), axis=1, keepdims=True)
    kind = lax.broadcasted_iota(jnp.int32, (EXTRA, LANES), 1) % half
    number = target_ref[...].reshape(1, 1)
    facts = jnp.where(kind == 0, alive, 0.0)
    facts = jnp.where(kind == 1, (number >> 8).astype(jnp.float32), facts)
    facts = jnp.where(kind == 2, (number & 255).astype(jnp.float32), facts)
    for page in range(page_mask.shape[0]):
        count = jnp.sum(page_mask[page : page + 1, :].astype(jnp.float32), axis=1, keepdims=True)
        facts = jnp.where(kind == 3 + page, count, facts)
    out_rows = out_ref.reshape(devices, half + EXTRA, LANES)
    for device in range(devices):
        begin = (device // members) % 2 * half
        out_rows[device, 0:half, :] = queries[0, begin : begin + half, :]
    out_ref[:, half // 2] = jnp.broadcast_to(facts.astype(jnp.bfloat16)[None], (devices, EXTRA, LANES))


def measure_pages(rows_q, vectors, flips, counts, alive, powers_ref=None):
    width = rows_q.shape[0]
    patch = lax.broadcasted_iota(jnp.int32, (LANES, width), 0).astype(jnp.float32)
    steep = 1.0 / (relaxation_scale_factor * math.log(2.0))
    softened, inverses, mixes = [], [], []
    for page, (block, flipped, count) in enumerate(zip(vectors, flips, counts)):
        similarity = lax.dot_general(
            block, rows_q, (((1,), (1,)), ((), ())), preferred_element_type=jnp.float32
        )
        masked = jnp.where(patch < count, similarity, guarded_floor_entry)
        highest = jnp.max(masked, axis=0, keepdims=True)
        powers = jnp.exp2((masked - highest) * steep)
        if powers_ref is not None:
            powers_ref[page] = powers
        high = powers.astype(jnp.bfloat16)
        low = (powers - high.astype(jnp.float32)).astype(jnp.bfloat16)
        mixes.append(
            jnp.dot(
                jnp.concatenate([flipped, flipped], axis=1),
                jnp.concatenate([high, low], axis=0),
                preferred_element_type=jnp.float32,
            )
        )
        total = jnp.sum(powers, axis=0, keepdims=True)
        lse = highest * (1.0 / relaxation_scale_factor) + jnp.log(total)
        softened.append(alive * (relaxation_scale_factor * (lse - jnp.log(count))))
        inverses.append(alive / total)
    return softened, inverses, mixes


def gather_rows(from_ref, to_ref):
    sources = from_ref.shape[0]
    half = 2 * (from_ref.shape[1] - 1)
    view = from_ref.reshape(sources, half + EXTRA, LANES)
    for source in range(sources):
        to_ref[source * half : (source + 1) * half, :] = view[source, 0:half, :]


def page_counts(sent_ref, home, local_pages):
    facts = sent_ref[home, sent_ref.shape[1] - 1].astype(jnp.float32)
    return [facts[0:1, 3 + number : 4 + number] for number in range(local_pages)]


def near_kernel(sent_ref, own_ref, rows_ref, power_ref, soft_ref, inverse_ref, facts_ref, mix_ref, flip_ref):
    sources = sent_ref.shape[0]
    half = 2 * (sent_ref.shape[1] - 1)
    part = sources * half
    per_chunk = LANES // half
    local_pages = own_ref.shape[0]
    blk = lax.axis_index("blk")
    home = blk * lax.axis_size("group") + lax.axis_index("group")
    slot = lax.broadcasted_iota(jnp.int32, (1, LANES), 1) // half
    facts = []
    for c in range(part // LANES):
        told = jnp.zeros((1, LANES), jnp.float32)
        for i in range(per_chunk):
            told = jnp.where(slot == i, sent_ref[c * per_chunk + i, half // 2, 0:1, :].astype(jnp.float32), told)
        facts.append(spread_runs(told, half))
    facts = jnp.concatenate(facts, axis=1)
    facts_ref[...] = facts
    token = lax.broadcasted_iota(jnp.int32, (1, part), 1) % half + (blk & 1) * half
    alive = (token.astype(jnp.float32) < facts[0:1]).astype(jnp.float32)
    gather_rows(sent_ref, rows_ref)
    vectors = [own_ref[page] for page in range(local_pages)]
    flips = [block.T for block in vectors]
    softened, inverses, mixes = measure_pages(
        rows_ref[...], vectors, flips, page_counts(sent_ref, home, local_pages), alive, power_ref
    )
    for page in range(local_pages):
        mix_ref[page] = mixes[page]
        flip_ref[page] = flips[page]
        soft_ref[page : page + 1, :] = softened[page]
        inverse_ref[page : page + 1, :] = inverses[page]


def far_kernel(*refs):
    sent_ref, swapped_ref, own_ref, other_ref, near_rows_ref, near_mix_ref, near_soft_ref, near_inverse_ref = refs[:8]
    facts_ref, flip_ref, out_ref, power_ref, score_ref, inverse_ref, rows_ref = refs[8:]
    sources = sent_ref.shape[0]
    half = 2 * (sent_ref.shape[1] - 1)
    part = sources * half
    local_pages = own_ref.shape[0]
    blk = lax.axis_index("blk")
    group = lax.axis_index("group")
    members = lax.axis_size("group")
    homes = [blk * members + group, (blk ^ 1) * members + group]
    side = blk & 1
    sends_sum = side == 0
    own_range = range(local_pages)
    ids = [home * local_pages + page for home in homes for page in own_range]
    own = [own_ref[page] for page in own_range]
    other = [other_ref[page] for page in own_range]
    own_flips = [flip_ref[page] for page in own_range]
    other_flips = [block.T for block in other]
    own_counts = page_counts(sent_ref, homes[0], local_pages)
    other_counts = page_counts(sent_ref, homes[1], local_pages)

    facts = facts_ref[...]
    target = (facts[1:2] * 256.0 + facts[2:3]).astype(jnp.int32)
    spot = lax.broadcasted_iota(jnp.int32, (1, part), 1) % half
    near_alive = ((spot + side * half).astype(jnp.float32) < facts[0:1]).astype(jnp.float32)
    far_alive = ((spot + (1 - side) * half).astype(jnp.float32) < facts[0:1]).astype(jnp.float32)
    other_soft, other_inverse, other_mix = measure_pages(near_rows_ref[...], other, other_flips, other_counts, near_alive)
    gather_rows(swapped_ref, rows_ref)
    rows_q = rows_ref[...]
    far_soft, far_inverse, far_mix = measure_pages(rows_q, own, own_flips, own_counts, far_alive, power_ref)
    cross_soft, cross_inverse, cross_mix = measure_pages(rows_q, other, other_flips, other_counts, far_alive)
    near_mix = [near_mix_ref[page] for page in own_range]
    near_soft = [near_soft_ref[page : page + 1, :] for page in own_range]
    near_inverse = [near_inverse_ref[page : page + 1, :] for page in own_range]
    for page in own_range:
        inverse_ref[page : page + 1, :] = far_inverse[page]
    softened = [a + b for a, b in zip(near_soft + other_soft, far_soft + cross_soft)]
    scores = segment_sum(jnp.concatenate(softened, axis=0), half)
    top = jnp.max(scores, axis=0, keepdims=True)
    chip_lse = top + jnp.log(jnp.sum(jnp.exp(scores - top), axis=0, keepdims=True))

    picked = jnp.zeros((1, part), jnp.float32)
    shares = []
    for page, name in enumerate(ids):
        score = scores[page : page + 1]
        hit = target == name
        picked = picked + jnp.where(hit, score, 0.0)
        shares.append(jnp.where(sends_sum, jnp.exp(score - chip_lse), hit.astype(jnp.float32)))
        if page < local_pages:
            score_ref[page : page + 1, :] = score
            score_ref[local_pages + page : local_pages + page + 1, :] = hit.astype(jnp.float32)
    high, low = split_half(jnp.where(sends_sum, chip_lse, picked))
    high_line = jnp.zeros((1, LANES), jnp.float32)
    low_line = jnp.zeros((1, LANES), jnp.float32)
    for c in range(part // LANES):
        high_line = jnp.where(spot[:, 0:LANES] == c, high[:, c * LANES : (c + 1) * LANES], high_line)
        low_line = jnp.where(spot[:, 0:LANES] == c, low[:, c * LANES : (c + 1) * LANES], low_line)
    lines = jnp.concatenate([high_line, low_line], axis=0)
    out_ref[:, half] = jnp.broadcast_to(lines[None], (sources, EXTRA, LANES))

    out_rows = out_ref.reshape(sources, 2 * half + EXTRA, LANES)
    for position, (mixes, inverses) in enumerate(
        ((near_mix + other_mix, near_inverse + other_inverse), (far_mix + cross_mix, far_inverse + cross_inverse))
    ):
        mixed = sum(mix * (inverse * share) for mix, inverse, share in zip(mixes, inverses, shares))
        mixed = mixed.T
        for source in range(sources):
            out_rows[source, position * half : (position + 1) * half, :] = mixed[
                source * half : (source + 1) * half, :
            ]


def last_kernel(tokens, got_ref, score_ref, *rest):
    near, far, results = rest[0:3], rest[3:6], rest[6:]
    grad_q_out, grad_p_out, loss_out, grad_q_ref, grad_p_ref, loss_ref, sems = results
    sources = got_ref.shape[0]
    half = tokens // 2
    chunks = sources * half // LANES
    per_chunk = LANES // half
    local_pages = grad_p_ref.shape[0]
    blk = lax.axis_index("blk")
    group = lax.axis_index("group")
    members = lax.axis_size("group")
    me = blk * members + group
    even = [s for s in range(sources) if (s // members) % 2 == 0]
    odd = [s for s in range(sources) if (s // members) % 2 == 1]

    def stats(source):
        return got_ref[source, tokens // 2, 0:1, :] + got_ref[source, tokens // 2, 1:2, :]

    def tree(combine, values):
        while len(values) > 1:
            values = [combine(*values[i : i + 2]) if i + 1 < len(values) else values[i] for i in range(0, len(values), 2)]
        return values[0]

    chip_lse = [stats(s) for s in even]
    top = tree(jnp.maximum, chip_lse)
    page_lse = top + jnp.log(tree(jnp.add, [jnp.exp(c - top) for c in chip_lse]))
    spread = spread_runs(page_lse, half)
    flat = jnp.concatenate([spread[c : c + 1] for c in range(chunks)], axis=1)
    copies = []
    for page in range(local_pages):
        score = score_ref[page : page + 1, :]
        hit = score_ref[local_pages + page : local_pages + page + 1, :]
        coefficient = jnp.exp(score - flat) - hit
        grad_p = jnp.zeros((LANES, LANES), jnp.float32)
        for rows_ref, power_ref, inverse_ref in (near, far):
            factor = (coefficient * inverse_ref[page : page + 1, :] * power_ref[page]).astype(jnp.bfloat16)
            grad_p += jnp.dot(factor, rows_ref[...], preferred_element_type=jnp.float32)
        grad_p_ref[page] = grad_p
        copies.append(pltpu.make_async_copy(grad_p_ref.at[page], grad_p_out.at[page], sems.at[page]))
        copies[-1].start()

    lane = lax.broadcasted_iota(jnp.int32, (1, LANES), 1)
    mine = lane == (me % per_chunk) * half + me // per_chunk
    ratios = jnp.concatenate([jnp.where(mine, jnp.exp(c - page_lse), 0.0) for c in chip_lse], axis=0)
    ratios = jnp.broadcast_to(jnp.sum(ratios, axis=1, keepdims=True), ratios.shape)
    got_rows = got_ref.reshape(sources, tokens + EXTRA, LANES)
    terms = [ratios[i : i + 1, :] * got_rows[s, 0:tokens, :] for i, s in enumerate(even)]
    sums = tree(jnp.add, terms)
    single = tree(jnp.add, [got_rows[s, 0:tokens, :] for s in odd])
    grad_q_ref[0, 0:half, :] = sums[0:half] - single[half:tokens]
    grad_q_ref[0, half:tokens, :] = sums[half:tokens] - single[0:half]
    copies.append(pltpu.make_async_copy(grad_q_ref, grad_q_out, sems.at[local_pages]))
    copies[-1].start()

    picked = tree(jnp.add, [stats(s) for s in odd])
    difference = jnp.where(lane % half < chunks, page_lse - picked, 0.0)
    loss_ref[...] = jnp.sum(difference, axis=1, keepdims=True) * (1.0 / sources)
    copies.append(pltpu.make_async_copy(loss_ref, loss_out, sems.at[local_pages + 1]))
    copies[-1].start()
    for copy in copies:
        copy.wait()


def exchange(blocks_to_all):
    return lax.all_to_all(blocks_to_all, ("blk", "group"), 0, 0, tiled=True)


def two_exchanges(queries, query_mask, positive, page_vectors, page_mask):
    tokens = queries.shape[1]
    local_pages = page_vectors.shape[0]
    devices = lax.axis_size("blk") * lax.axis_size("group")
    lanes = devices * tokens
    blocks = lax.axis_size("blk")
    half = tokens // 2
    pairs = (tokens + EXTRA) // 2
    swap = [(b, b ^ 1) for b in range(blocks)]

    vmem = pl.BlockSpec(memory_space=pltpu.VMEM)
    anywhere = pl.BlockSpec(memory_space=pl.ANY)
    params = pltpu.CompilerParams(vmem_limit_bytes=KERNEL_VMEM)
    message = pl.pallas_call(
        first_kernel,
        out_shape=jax.ShapeDtypeStruct((devices, (half + EXTRA) // 2, 2, LANES), jnp.bfloat16),
        in_specs=[vmem] + [pl.BlockSpec(memory_space=pltpu.HBM)] * 3,
        out_specs=vmem,
        compiler_params=params,
        scratch_shapes=[
            pltpu.VMEM(queries.shape, jnp.bfloat16),
            pltpu.VMEM(query_mask.shape, jnp.int32),
            pltpu.VMEM(page_mask.shape, jnp.int32),
            pltpu.SemaphoreType.DMA((3,)),
        ],
    )(positive, *[pltpu.with_memory_space_constraint(a, pltpu.HBM) for a in (queries, query_mask, page_mask)])
    sent = exchange(message)
    sent, page_vectors = lax.optimization_barrier((sent, page_vectors))
    swapped = lax.ppermute(sent, "blk", swap)
    other_vectors = lax.ppermute(page_vectors, "blk", swap)
    part = lanes // 2
    kept = (
        jax.ShapeDtypeStruct((part, LANES), jnp.bfloat16),
        jax.ShapeDtypeStruct((local_pages, LANES, part), jnp.float32),
        jax.ShapeDtypeStruct((local_pages, part), jnp.float32),
    )
    near_rows, near_powers, near_soft, near_inverses, facts, near_mix, flips = pl.pallas_call(
        near_kernel,
        out_shape=kept + (kept[2], jax.ShapeDtypeStruct((8, part), jnp.float32), kept[1], jax.ShapeDtypeStruct(page_vectors.shape, jnp.bfloat16)),
        in_specs=[vmem] * 2,
        out_specs=(vmem,) * 7,
        compiler_params=params,
        cost_estimate=pl.CostEstimate(flops=4 * part * LANES * LANES, bytes_accessed=2**20, transcendentals=part * LANES),
    )(sent, page_vectors)
    out, far_powers, scores, far_inverses, far_rows = pl.pallas_call(
        far_kernel,
        out_shape=(
            jax.ShapeDtypeStruct((devices, pairs, 2, LANES), jnp.float32),
            kept[1],
            jax.ShapeDtypeStruct((2 * local_pages, part), jnp.float32),
            kept[2],
            kept[0],
        ),
        in_specs=[vmem] * 10,
        out_specs=(vmem,) * 5,
        compiler_params=params,
    )(sent, swapped, page_vectors, other_vectors, near_rows, near_mix, near_soft, near_inverses, facts, flips)
    got = exchange(out.astype(jnp.float16)).astype(jnp.float32)
    grad_q, grad_p, loss = pl.pallas_call(
        functools.partial(last_kernel, tokens),
        out_shape=(
            jax.ShapeDtypeStruct(queries.shape, jnp.float32),
            jax.ShapeDtypeStruct(page_vectors.shape, jnp.float32),
            jax.ShapeDtypeStruct((1, 1), jnp.float32),
        ),
        in_specs=[vmem] * 8,
        out_specs=(anywhere,) * 3,
        scratch_shapes=[
            pltpu.VMEM(queries.shape, jnp.float32),
            pltpu.VMEM(page_vectors.shape, jnp.float32),
            pltpu.VMEM((1, 1), jnp.float32),
            pltpu.SemaphoreType.DMA((local_pages + 2,)),
        ],
        compiler_params=params,
    )(got, scores, near_rows, near_powers, near_inverses, far_rows, far_powers, far_inverses)
    return (grad_q, grad_p, loss[0, 0])


def on_device(queries, query_mask, positive, page_vectors, page_mask):
    devices = lax.axis_size("blk") * lax.axis_size("group")
    chosen = two_exchanges if fits(queries, page_vectors, devices) else general_path
    return chosen(queries, query_mask, positive, page_vectors, page_mask)


def solution(mesh):
    in_specs = (
        P(("blk", "group"), None, None),
        P(("blk", "group"), None),
        P(("blk", "group")),
        P(("blk", "group"), None, None),
        P(("blk", "group"), None),
    )
    out_specs = (P(("blk", "group"), None, None), P(("blk", "group"), None, None), P())
    return jax.shard_map(
        on_device, mesh=mesh, in_specs=in_specs, out_specs=out_specs, check_vma=False
    )
```

```python
import functools
import math

import jax
import jax.numpy as jnp
from jax import lax
from jax.experimental import pallas as pl
from jax.experimental.pallas import tpu as pltpu
from jax.sharding import PartitionSpec as P

relaxation_scale_factor = 0.5
guarded_floor_entry = -1e30


def combined_all(part, axis, combine):
    gathered = jax.tree.map(lambda a: lax.all_gather(a, axis), part)

    def take(source):
        return jax.tree.map(lambda a: lax.dynamic_index_in_dim(a, source, 0, False), gathered)

    return lax.fori_loop(
        1, lax.axis_size(axis), lambda source, state: combine(state, take(source)), take(0)
    )


def from_behind(value, axis, steps):
    count = lax.axis_size(axis)
    pairs = [(source, (source + steps) % count) for source in range(count)]
    return lax.ppermute(value, axis, pairs)


def masked_logits(row_block, lone_document, live_image_embeddings):
    similarity_matrix = lax.dot_general(
        row_block, lone_document, (((1,), (1,)), ((), ())), preferred_element_type=jnp.float32
    )
    return jnp.where(
        live_image_embeddings[None, :] > 0,
        similarity_matrix / relaxation_scale_factor,
        guarded_floor_entry,
    )


def combine_parts(earlier, later):
    highest = jnp.maximum(earlier[0], later[0])
    totals = earlier[1] * jnp.exp(earlier[0] - highest) + later[1] * jnp.exp(later[0] - highest)
    return (highest, totals, earlier[2] + later[2])


def general_path(queries, query_mask, positive, page_vectors, page_mask):
    tokens = queries.shape[1]
    features = queries.shape[2]
    local_pages = page_vectors.shape[0]
    blocks = lax.axis_size("blk")
    members = lax.axis_size("group")
    bundle_size = queries.shape[0] * members
    total_queries = bundle_size * blocks
    natural_logarithm_lengths = jnp.log(jnp.sum(page_mask.astype(jnp.float32), axis=1))
    bundle_vectors, bundle_masks, bundle_targets = (
        lax.all_gather(queries, "group", axis=0, tiled=True),
        lax.all_gather(query_mask, "group", axis=0, tiled=True),
        lax.all_gather(positive, "group", axis=0, tiled=True),
    )

    def forward_piece(folded, shard_in, root_row):
        scores, lse_rows, live_all, owners, kept = folded
        vectors, token_masks, targets = shard_in
        amount = vectors.shape[0]
        stride = math.gcd(amount, max(1, 512 // tokens))

        def run_block(number, current):
            scores, lse_rows = current
            offset = number * stride
            slab_rows = lax.dynamic_slice_in_dim(vectors, offset, stride, 0).reshape(
                stride * tokens, features
            )
            alive = lax.dynamic_slice_in_dim(token_masks, offset, stride, 0).astype(jnp.float32)
            found_sums = []
            for index_page in range(local_pages):
                masked = masked_logits(slab_rows, page_vectors[index_page], page_mask[index_page])
                highest = jnp.max(masked, axis=1, keepdims=True)
                found_sums.append(
                    highest[:, 0] + jnp.log(jnp.sum(jnp.exp(masked - highest), axis=1))
                )
            logsumexp_results = jnp.stack(found_sums, axis=1).reshape(stride, tokens, local_pages)
            softened_supremum = relaxation_scale_factor * (
                logsumexp_results - natural_logarithm_lengths
            )
            page_score = jnp.sum(alive[:, :, None] * softened_supremum, axis=1)
            scores = lax.dynamic_update_slice_in_dim(scores, page_score, offset, 0)
            lse_rows = lax.dynamic_update_slice_in_dim(lse_rows, logsumexp_results, offset, 0)
            return (scores, lse_rows)

        scores, lse_rows = lax.fori_loop(0, amount // stride, run_block, (scores, lse_rows))
        live_all = lax.dynamic_update_slice_in_dim(live_all, token_masks, root_row, 0)
        owners = lax.dynamic_update_slice_in_dim(owners, targets, root_row, 0)
        kept = vectors
        return (scores, lse_rows, live_all, owners, kept)

    starting = (
        jnp.zeros((total_queries, local_pages), jnp.float32),
        jnp.zeros((total_queries, tokens, local_pages), jnp.float32),
        jnp.zeros((total_queries, tokens), jnp.int32),
        jnp.zeros((total_queries,), jnp.int32),
        jnp.zeros((total_queries, tokens, features), jnp.bfloat16),
    )
    scores, lse_rows, live_all, owners, kept = forward_piece(
        starting,
        (
            lax.all_gather(bundle_vectors, "blk", axis=0, tiled=True),
            lax.all_gather(bundle_masks, "blk", axis=0, tiled=True),
            lax.all_gather(bundle_targets, "blk", axis=0, tiled=True),
        ),
        jnp.int32(0),
    )
    position = lax.axis_index(("blk", "group"))
    page_ids = position * local_pages + jnp.arange(local_pages, dtype=jnp.int32)
    chosen = owners[:, None] == page_ids[None, :]
    picked_local = jnp.sum(jnp.where(chosen, scores, 0.0))
    local_top = jnp.max(scores, axis=1)
    local_total = jnp.sum(jnp.exp(scores - local_top[:, None]), axis=1)
    highest, totals, picked = combined_all(
        (local_top, local_total, picked_local), ("blk", "group"), combine_parts
    )
    page_lse = highest + jnp.log(totals)
    mean_loss = (jnp.sum(page_lse) - picked) / total_queries
    coefficient = jnp.exp(scores - page_lse[:, None]) - chosen.astype(jnp.float32)
    factor_scale = coefficient[:, None, :] * live_all.astype(jnp.float32)[:, :, None]

    def slice_rows(root_row, amount):
        sums = lax.dynamic_slice_in_dim(lse_rows, root_row, amount, 0).reshape(
            amount * tokens, local_pages
        )
        scales = lax.dynamic_slice_in_dim(factor_scale, root_row, amount, 0).reshape(
            amount * tokens, local_pages
        )
        return (sums, scales)

    def gradient_terms(row_block, logsumexp_results, scales, page_grads):
        partial_value = jnp.zeros(row_block.shape, jnp.float32)
        for number in range(local_pages):
            masked = masked_logits(row_block, page_vectors[number], page_mask[number])
            weights = jnp.exp(masked - logsumexp_results[:, number : number + 1])
            factor = (scales[:, number : number + 1] * weights).astype(jnp.bfloat16)
            partial_value = partial_value + jnp.dot(
                factor, page_vectors[number], preferred_element_type=jnp.float32
            )
            update = lax.dot_general(
                factor, row_block, (((0,), (0,)), ((), ())), preferred_element_type=jnp.float32
            )
            page_grads = page_grads.at[number].add(update)
        return (partial_value, page_grads)

    home = lax.axis_index("blk")
    page_grads = jnp.zeros(page_vectors.shape, jnp.float32)

    def visit_one(moving, collected, page_grads, lap_index):
        root_row = (home - lap_index) % blocks * bundle_size
        sums, scales = slice_rows(root_row, bundle_size)
        partial_value, page_grads = gradient_terms(
            moving.reshape(bundle_size * tokens, features), sums, scales, page_grads
        )
        return (collected + partial_value.reshape(bundle_size, tokens, features), page_grads)

    def pass_one(collected):
        return from_behind(collected, "blk", 1)

    def turn_one(lap_index, current):
        moving, collected, page_grads = current
        collected, page_grads = visit_one(moving, collected, page_grads, lap_index)
        moving = from_behind(moving, "blk", 1)
        return (moving, pass_one(collected), page_grads)

    empty_whole = jnp.zeros((bundle_size, tokens, features), jnp.float32)
    moving, collected, page_grads = lax.fori_loop(
        0, blocks - 1, turn_one, (bundle_vectors, empty_whole, page_grads)
    )
    collected, page_grads = visit_one(moving, collected, page_grads, blocks - 1)
    collected = pass_one(collected)
    grad_queries = lax.psum_scatter(collected, "group", scatter_dimension=0, tiled=True)
    return (grad_queries, page_grads, mean_loss)


LANES = 128
EXTRA = 2
FACTS = 16
KERNEL_VMEM = 16 * 2**20
HALF_SCALE = 2.0**14


def fits(queries, page_vectors, devices):
    tokens, features = queries.shape[1:]
    lanes = devices * tokens
    return (
        queries.shape[0] == 1
        and tokens == FACTS
        and features == LANES
        and page_vectors.shape[1] == LANES
        and page_vectors.shape[0] <= FACTS - 3
        and lanes % LANES == 0
        and lanes // LANES <= 8
        and lax.axis_size("blk") % 2 == 0
    )


def segment_sum(values, width):
    lanes = values.shape[1]
    lane = lax.broadcasted_iota(jnp.int32, values.shape, 1)
    step = 1
    while step < width:
        ahead = pltpu.roll(values, lanes - step, 1)
        behind = pltpu.roll(values, step, 1)
        values = values + jnp.where((lane & step) == 0, ahead, behind)
        step *= 2
    return values


def spread_runs(line, width):
    lane = lax.broadcasted_iota(jnp.int32, (8, LANES), 1)
    row = lax.broadcasted_iota(jnp.int32, (8, LANES), 0)
    return jnp.take_along_axis(jnp.broadcast_to(line, (8, LANES)), lane // width * width + row, axis=1)


def split_half(value):
    scaled = value * 8193.0
    high = scaled - (scaled - value)
    return high, value - high


def first_kernel(target_ref, queries_ref, query_mask_ref, page_mask_ref, out_ref, *scratch):
    queries, query_mask, page_mask, sems = scratch
    devices = out_ref.shape[0]
    half = queries_ref.shape[1] // 2
    members = lax.axis_size("group")
    loads = [
        pltpu.make_async_copy(src, dst, sems.at[i])
        for i, (src, dst) in enumerate(
            (
                (queries_ref, queries),
                (query_mask_ref, query_mask),
                (page_mask_ref, page_mask),
            )
        )
    ]
    for load in loads:
        load.start()
    for load in loads:
        load.wait()
    alive = jnp.sum(query_mask[...].astype(jnp.float32), axis=1, keepdims=True)
    kind = lax.broadcasted_iota(jnp.int32, (EXTRA, LANES), 1) % half
    number = target_ref[...].reshape(1, 1)
    facts = jnp.where(kind == 0, alive, 0.0)
    facts = jnp.where(kind == 1, (number >> 8).astype(jnp.float32), facts)
    facts = jnp.where(kind == 2, (number & 255).astype(jnp.float32), facts)
    for page in range(page_mask.shape[0]):
        count = jnp.sum(page_mask[page : page + 1, :].astype(jnp.float32), axis=1, keepdims=True)
        facts = jnp.where(kind == 3 + page, count, facts)
    out_rows = out_ref.reshape(devices, half + EXTRA, LANES)
    for device in range(devices):
        begin = (device // members) % 2 * half
        out_rows[device, 0:half, :] = queries[0, begin : begin + half, :]
    out_ref[:, half // 2] = jnp.broadcast_to(facts.astype(jnp.bfloat16)[None], (devices, EXTRA, LANES))


def measure_pages(rows_q, vectors, flips, counts, alive, powers_ref=None):
    width = rows_q.shape[0]
    patch = lax.broadcasted_iota(jnp.int32, (LANES, width), 0).astype(jnp.float32)
    steep = 1.0 / (relaxation_scale_factor * math.log(2.0))
    softened, inverses, mixes = [], [], []
    for page, (block, flipped, count) in enumerate(zip(vectors, flips, counts)):
        similarity = lax.dot_general(
            block, rows_q, (((1,), (1,)), ((), ())), preferred_element_type=jnp.float32
        )
        masked = jnp.where(patch < count, similarity, guarded_floor_entry)
        highest = jnp.max(masked, axis=0, keepdims=True)
        powers = jnp.exp2((masked - highest) * steep)
        if powers_ref is not None:
            powers_ref[page] = powers
        high = powers.astype(jnp.bfloat16)
        low = (powers - high.astype(jnp.float32)).astype(jnp.bfloat16)
        mixes.append(
            jnp.dot(
                jnp.concatenate([flipped, flipped], axis=1),
                jnp.concatenate([high, low], axis=0),
                preferred_element_type=jnp.float32,
            )
        )
        total = jnp.sum(powers, axis=0, keepdims=True)
        lse = highest * (1.0 / relaxation_scale_factor) + jnp.log(total)
        softened.append(alive * (relaxation_scale_factor * (lse - jnp.log(count))))
        inverses.append(alive / total)
    return softened, inverses, mixes


def gather_rows(from_ref, to_ref):
    sources = from_ref.shape[0]
    half = 2 * (from_ref.shape[1] - 1)
    view = from_ref.reshape(sources, half + EXTRA, LANES)
    for source in range(sources):
        to_ref[source * half : (source + 1) * half, :] = view[source, 0:half, :]


def page_counts(sent_ref, home, local_pages):
    facts = sent_ref[home, sent_ref.shape[1] - 1].astype(jnp.float32)
    return [facts[0:1, 3 + number : 4 + number] for number in range(local_pages)]


def near_kernel(sent_ref, own_ref, rows_ref, power_ref, soft_ref, inverse_ref, facts_ref, mix_ref, flip_ref):
    sources = sent_ref.shape[0]
    half = 2 * (sent_ref.shape[1] - 1)
    part = sources * half
    per_chunk = LANES // half
    local_pages = own_ref.shape[0]
    blk = lax.axis_index("blk")
    home = blk * lax.axis_size("group") + lax.axis_index("group")
    slot = lax.broadcasted_iota(jnp.int32, (1, LANES), 1) // half
    facts = []
    for c in range(part // LANES):
        told = jnp.zeros((1, LANES), jnp.float32)
        for i in range(per_chunk):
            told = jnp.where(slot == i, sent_ref[c * per_chunk + i, half // 2, 0:1, :].astype(jnp.float32), told)
        facts.append(spread_runs(told, half))
    facts = jnp.concatenate(facts, axis=1)
    facts_ref[...] = facts
    token = lax.broadcasted_iota(jnp.int32, (1, part), 1) % half + (blk & 1) * half
    alive = (token.astype(jnp.float32) < facts[0:1]).astype(jnp.float32)
    gather_rows(sent_ref, rows_ref)
    vectors = [own_ref[page] for page in range(local_pages)]
    flips = [block.T for block in vectors]
    softened, inverses, mixes = measure_pages(
        rows_ref[...], vectors, flips, page_counts(sent_ref, home, local_pages), alive, power_ref
    )
    for page in range(local_pages):
        mix_ref[page] = mixes[page]
        flip_ref[page] = flips[page]
        soft_ref[page : page + 1, :] = softened[page]
        inverse_ref[page : page + 1, :] = inverses[page]


def far_kernel(*refs):
    sent_ref, swapped_ref, own_ref, other_ref, near_rows_ref, near_mix_ref, near_soft_ref, near_inverse_ref = refs[:8]
    facts_ref, flip_ref, out_ref, power_ref, score_ref, inverse_ref, rows_ref = refs[8:]
    sources = sent_ref.shape[0]
    half = 2 * (sent_ref.shape[1] - 1)
    part = sources * half
    local_pages = own_ref.shape[0]
    blk = lax.axis_index("blk")
    group = lax.axis_index("group")
    members = lax.axis_size("group")
    homes = [blk * members + group, (blk ^ 1) * members + group]
    side = blk & 1
    sends_sum = side == 0
    own_range = range(local_pages)
    ids = [home * local_pages + page for home in homes for page in own_range]
    own = [own_ref[page] for page in own_range]
    other = [other_ref[page] for page in own_range]
    own_flips = [flip_ref[page] for page in own_range]
    other_flips = [block.T for block in other]
    own_counts = page_counts(sent_ref, homes[0], local_pages)
    other_counts = page_counts(sent_ref, homes[1], local_pages)

    facts = facts_ref[...]
    target = (facts[1:2] * 256.0 + facts[2:3]).astype(jnp.int32)
    spot = lax.broadcasted_iota(jnp.int32, (1, part), 1) % half
    near_alive = ((spot + side * half).astype(jnp.float32) < facts[0:1]).astype(jnp.float32)
    far_alive = ((spot + (1 - side) * half).astype(jnp.float32) < facts[0:1]).astype(jnp.float32)
    other_soft, other_inverse, other_mix = measure_pages(near_rows_ref[...], other, other_flips, other_counts, near_alive)
    gather_rows(swapped_ref, rows_ref)
    rows_q = rows_ref[...]
    far_soft, far_inverse, far_mix = measure_pages(rows_q, own, own_flips, own_counts, far_alive, power_ref)
    cross_soft, cross_inverse, cross_mix = measure_pages(rows_q, other, other_flips, other_counts, far_alive)
    near_mix = [near_mix_ref[page] for page in own_range]
    near_soft = [near_soft_ref[page : page + 1, :] for page in own_range]
    near_inverse = [near_inverse_ref[page : page + 1, :] for page in own_range]
    for page in own_range:
        inverse_ref[page : page + 1, :] = far_inverse[page]
    softened = [a + b for a, b in zip(near_soft + other_soft, far_soft + cross_soft)]
    scores = segment_sum(jnp.concatenate(softened, axis=0), half)
    top = jnp.max(scores, axis=0, keepdims=True)
    chip_lse = top + jnp.log(jnp.sum(jnp.exp(scores - top), axis=0, keepdims=True))

    picked = jnp.zeros((1, part), jnp.float32)
    shares = []
    for page, name in enumerate(ids):
        score = scores[page : page + 1]
        hit = target == name
        picked = picked + jnp.where(hit, score, 0.0)
        shares.append(jnp.where(sends_sum, jnp.exp(score - chip_lse), hit.astype(jnp.float32)))
        if page < local_pages:
            score_ref[page : page + 1, :] = score
            score_ref[local_pages + page : local_pages + page + 1, :] = hit.astype(jnp.float32)
    high, low = split_half(jnp.where(sends_sum, chip_lse, picked))
    high_line = jnp.zeros((1, LANES), jnp.float32)
    low_line = jnp.zeros((1, LANES), jnp.float32)
    for c in range(part // LANES):
        high_line = jnp.where(spot[:, 0:LANES] == c, high[:, c * LANES : (c + 1) * LANES], high_line)
        low_line = jnp.where(spot[:, 0:LANES] == c, low[:, c * LANES : (c + 1) * LANES], low_line)
    lines = jnp.concatenate([high_line, low_line], axis=0)
    out_ref[:, half] = jnp.broadcast_to(lines[None], (sources, EXTRA, LANES))

    out_rows = out_ref.reshape(sources, 2 * half + EXTRA, LANES)
    for position, (mixes, inverses) in enumerate(
        ((near_mix + other_mix, near_inverse + other_inverse), (far_mix + cross_mix, far_inverse + cross_inverse))
    ):
        mixed = sum(mix * (inverse * (share * HALF_SCALE)) for mix, inverse, share in zip(mixes, inverses, shares))
        mixed = mixed.T
        for source in range(sources):
            out_rows[source, position * half : (position + 1) * half, :] = mixed[
                source * half : (source + 1) * half, :
            ]


def last_kernel(tokens, got_ref, score_ref, *rest):
    near, far, results = rest[0:3], rest[3:6], rest[6:]
    grad_q_out, grad_p_out, loss_out, grad_q_ref, grad_p_ref, loss_ref, sems = results
    sources = got_ref.shape[0]
    half = tokens // 2
    chunks = sources * half // LANES
    per_chunk = LANES // half
    local_pages = grad_p_ref.shape[0]
    blk = lax.axis_index("blk")
    group = lax.axis_index("group")
    members = lax.axis_size("group")
    me = blk * members + group
    even = [s for s in range(sources) if (s // members) % 2 == 0]
    odd = [s for s in range(sources) if (s // members) % 2 == 1]

    def stats(source):
        return got_ref[source, tokens // 2, 0:1, :] + got_ref[source, tokens // 2, 1:2, :]

    def tree(combine, values):
        while len(values) > 1:
            values = [combine(*values[i : i + 2]) if i + 1 < len(values) else values[i] for i in range(0, len(values), 2)]
        return values[0]

    chip_lse = [stats(s) for s in even]
    top = tree(jnp.maximum, chip_lse)
    page_lse = top + jnp.log(tree(jnp.add, [jnp.exp(c - top) for c in chip_lse]))
    spread = spread_runs(page_lse, half)
    flat = jnp.concatenate([spread[c : c + 1] for c in range(chunks)], axis=1)
    copies = []
    for page in range(local_pages):
        score = score_ref[page : page + 1, :]
        hit = score_ref[local_pages + page : local_pages + page + 1, :]
        coefficient = jnp.exp(score - flat) - hit
        grad_p = jnp.zeros((LANES, LANES), jnp.float32)
        for rows_ref, power_ref, inverse_ref in (near, far):
            factor = (coefficient * inverse_ref[page : page + 1, :] * power_ref[page]).astype(jnp.bfloat16)
            grad_p += jnp.dot(factor, rows_ref[...], preferred_element_type=jnp.float32)
        grad_p_ref[page] = grad_p
        copies.append(pltpu.make_async_copy(grad_p_ref.at[page], grad_p_out.at[page], sems.at[page]))
        copies[-1].start()

    lane = lax.broadcasted_iota(jnp.int32, (1, LANES), 1)
    mine = lane == (me % per_chunk) * half + me // per_chunk
    ratios = jnp.concatenate([jnp.where(mine, jnp.exp(c - page_lse), 0.0) for c in chip_lse], axis=0)
    ratios = jnp.sum(ratios, axis=1, keepdims=True) * (1.0 / HALF_SCALE)
    ratios = jnp.broadcast_to(ratios, ratios.shape[:1] + (LANES,))
    got_rows = got_ref.reshape(sources, tokens + EXTRA, LANES)
    terms = [ratios[i : i + 1, :] * got_rows[s, 0:tokens, :] for i, s in enumerate(even)]
    sums = tree(jnp.add, terms)
    single = tree(jnp.add, [got_rows[s, 0:tokens, :] for s in odd]) * (1.0 / HALF_SCALE)
    grad_q_ref[0, 0:half, :] = sums[0:half] - single[half:tokens]
    grad_q_ref[0, half:tokens, :] = sums[half:tokens] - single[0:half]
    copies.append(pltpu.make_async_copy(grad_q_ref, grad_q_out, sems.at[local_pages]))
    copies[-1].start()

    picked = tree(jnp.add, [stats(s) for s in odd])
    difference = jnp.where(lane % half < chunks, page_lse - picked, 0.0)
    loss_ref[...] = jnp.sum(difference, axis=1, keepdims=True) * (1.0 / sources)
    copies.append(pltpu.make_async_copy(loss_ref, loss_out, sems.at[local_pages + 1]))
    copies[-1].start()
    for copy in copies:
        copy.wait()


def exchange(blocks_to_all):
    return lax.all_to_all(blocks_to_all, ("blk", "group"), 0, 0, tiled=True)


def two_exchanges(queries, query_mask, positive, page_vectors, page_mask):
    tokens = queries.shape[1]
    local_pages = page_vectors.shape[0]
    devices = lax.axis_size("blk") * lax.axis_size("group")
    lanes = devices * tokens
    blocks = lax.axis_size("blk")
    half = tokens // 2
    pairs = (tokens + EXTRA) // 2
    swap = [(b, b ^ 1) for b in range(blocks)]

    vmem = pl.BlockSpec(memory_space=pltpu.VMEM)
    anywhere = pl.BlockSpec(memory_space=pl.ANY)
    params = pltpu.CompilerParams(vmem_limit_bytes=KERNEL_VMEM)
    message = pl.pallas_call(
        first_kernel,
        out_shape=jax.ShapeDtypeStruct((devices, (half + EXTRA) // 2, 2, LANES), jnp.bfloat16),
        in_specs=[vmem] + [pl.BlockSpec(memory_space=pltpu.HBM)] * 3,
        out_specs=vmem,
        compiler_params=params,
        scratch_shapes=[
            pltpu.VMEM(queries.shape, jnp.bfloat16),
            pltpu.VMEM(query_mask.shape, jnp.int32),
            pltpu.VMEM(page_mask.shape, jnp.int32),
            pltpu.SemaphoreType.DMA((3,)),
        ],
    )(positive, *[pltpu.with_memory_space_constraint(a, pltpu.HBM) for a in (queries, query_mask, page_mask)])
    sent = exchange(message)
    sent, page_vectors = lax.optimization_barrier((sent, page_vectors))
    swapped = lax.ppermute(sent, "blk", swap)
    other_vectors = lax.ppermute(page_vectors, "blk", swap)
    part = lanes // 2
    kept = (
        jax.ShapeDtypeStruct((part, LANES), jnp.bfloat16),
        jax.ShapeDtypeStruct((local_pages, LANES, part), jnp.float32),
        jax.ShapeDtypeStruct((local_pages, part), jnp.float32),
    )
    near_rows, near_powers, near_soft, near_inverses, facts, near_mix, flips = pl.pallas_call(
        near_kernel,
        out_shape=kept + (kept[2], jax.ShapeDtypeStruct((8, part), jnp.float32), kept[1], jax.ShapeDtypeStruct(page_vectors.shape, jnp.bfloat16)),
        in_specs=[vmem] * 2,
        out_specs=(vmem,) * 7,
        compiler_params=params,
        cost_estimate=pl.CostEstimate(flops=4 * part * LANES * LANES, bytes_accessed=2**20, transcendentals=part * LANES),
    )(sent, page_vectors)
    out, far_powers, scores, far_inverses, far_rows = pl.pallas_call(
        far_kernel,
        out_shape=(
            jax.ShapeDtypeStruct((devices, pairs, 2, LANES), jnp.float32),
            kept[1],
            jax.ShapeDtypeStruct((2 * local_pages, part), jnp.float32),
            kept[2],
            kept[0],
        ),
        in_specs=[vmem] * 10,
        out_specs=(vmem,) * 5,
        compiler_params=params,
    )(sent, swapped, page_vectors, other_vectors, near_rows, near_mix, near_soft, near_inverses, facts, flips)
    got = exchange(out.astype(jnp.float16)).astype(jnp.float32)
    grad_q, grad_p, loss = pl.pallas_call(
        functools.partial(last_kernel, tokens),
        out_shape=(
            jax.ShapeDtypeStruct(queries.shape, jnp.float32),
            jax.ShapeDtypeStruct(page_vectors.shape, jnp.float32),
            jax.ShapeDtypeStruct((1, 1), jnp.float32),
        ),
        in_specs=[vmem] * 8,
        out_specs=(anywhere,) * 3,
        scratch_shapes=[
            pltpu.VMEM(queries.shape, jnp.float32),
            pltpu.VMEM(page_vectors.shape, jnp.float32),
            pltpu.VMEM((1, 1), jnp.float32),
            pltpu.SemaphoreType.DMA((local_pages + 2,)),
        ],
        compiler_params=params,
    )(got, scores, near_rows, near_powers, near_inverses, far_rows, far_powers, far_inverses)
    return (grad_q, grad_p, loss[0, 0])


def on_device(queries, query_mask, positive, page_vectors, page_mask):
    devices = lax.axis_size("blk") * lax.axis_size("group")
    chosen = two_exchanges if fits(queries, page_vectors, devices) else general_path
    return chosen(queries, query_mask, positive, page_vectors, page_mask)


def solution(mesh):
    in_specs = (
        P(("blk", "group"), None, None),
        P(("blk", "group"), None),
        P(("blk", "group")),
        P(("blk", "group"), None, None),
        P(("blk", "group"), None),
    )
    out_specs = (P(("blk", "group"), None, None), P(("blk", "group"), None, None), P())
    return jax.shard_map(
        on_device, mesh=mesh, in_specs=in_specs, out_specs=out_specs, check_vma=False
    )
```

```python
import functools
import math

import jax
import jax.numpy as jnp
from jax import lax
from jax.experimental import pallas as pl
from jax.experimental.pallas import tpu as pltpu
from jax.sharding import PartitionSpec as P

relaxation_scale_factor = 0.5
guarded_floor_entry = -1e30


def combined_all(part, axis, combine):
    gathered = jax.tree.map(lambda a: lax.all_gather(a, axis), part)

    def take(source):
        return jax.tree.map(lambda a: lax.dynamic_index_in_dim(a, source, 0, False), gathered)

    return lax.fori_loop(
        1, lax.axis_size(axis), lambda source, state: combine(state, take(source)), take(0)
    )


def from_behind(value, axis, steps):
    count = lax.axis_size(axis)
    pairs = [(source, (source + steps) % count) for source in range(count)]
    return lax.ppermute(value, axis, pairs)


def masked_logits(row_block, lone_document, live_image_embeddings):
    similarity_matrix = lax.dot_general(
        row_block, lone_document, (((1,), (1,)), ((), ())), preferred_element_type=jnp.float32
    )
    return jnp.where(
        live_image_embeddings[None, :] > 0,
        similarity_matrix / relaxation_scale_factor,
        guarded_floor_entry,
    )


def combine_parts(earlier, later):
    highest = jnp.maximum(earlier[0], later[0])
    totals = earlier[1] * jnp.exp(earlier[0] - highest) + later[1] * jnp.exp(later[0] - highest)
    return (highest, totals, earlier[2] + later[2])


def general_path(queries, query_mask, positive, page_vectors, page_mask):
    tokens = queries.shape[1]
    features = queries.shape[2]
    local_pages = page_vectors.shape[0]
    blocks = lax.axis_size("blk")
    members = lax.axis_size("group")
    bundle_size = queries.shape[0] * members
    total_queries = bundle_size * blocks
    natural_logarithm_lengths = jnp.log(jnp.sum(page_mask.astype(jnp.float32), axis=1))
    bundle_vectors, bundle_masks, bundle_targets = (
        lax.all_gather(queries, "group", axis=0, tiled=True),
        lax.all_gather(query_mask, "group", axis=0, tiled=True),
        lax.all_gather(positive, "group", axis=0, tiled=True),
    )

    def forward_piece(folded, shard_in, root_row):
        scores, lse_rows, live_all, owners, kept = folded
        vectors, token_masks, targets = shard_in
        amount = vectors.shape[0]
        stride = math.gcd(amount, max(1, 512 // tokens))

        def run_block(number, current):
            scores, lse_rows = current
            offset = number * stride
            slab_rows = lax.dynamic_slice_in_dim(vectors, offset, stride, 0).reshape(
                stride * tokens, features
            )
            alive = lax.dynamic_slice_in_dim(token_masks, offset, stride, 0).astype(jnp.float32)
            found_sums = []
            for index_page in range(local_pages):
                masked = masked_logits(slab_rows, page_vectors[index_page], page_mask[index_page])
                highest = jnp.max(masked, axis=1, keepdims=True)
                found_sums.append(
                    highest[:, 0] + jnp.log(jnp.sum(jnp.exp(masked - highest), axis=1))
                )
            logsumexp_results = jnp.stack(found_sums, axis=1).reshape(stride, tokens, local_pages)
            softened_supremum = relaxation_scale_factor * (
                logsumexp_results - natural_logarithm_lengths
            )
            page_score = jnp.sum(alive[:, :, None] * softened_supremum, axis=1)
            scores = lax.dynamic_update_slice_in_dim(scores, page_score, offset, 0)
            lse_rows = lax.dynamic_update_slice_in_dim(lse_rows, logsumexp_results, offset, 0)
            return (scores, lse_rows)

        scores, lse_rows = lax.fori_loop(0, amount // stride, run_block, (scores, lse_rows))
        live_all = lax.dynamic_update_slice_in_dim(live_all, token_masks, root_row, 0)
        owners = lax.dynamic_update_slice_in_dim(owners, targets, root_row, 0)
        kept = vectors
        return (scores, lse_rows, live_all, owners, kept)

    starting = (
        jnp.zeros((total_queries, local_pages), jnp.float32),
        jnp.zeros((total_queries, tokens, local_pages), jnp.float32),
        jnp.zeros((total_queries, tokens), jnp.int32),
        jnp.zeros((total_queries,), jnp.int32),
        jnp.zeros((total_queries, tokens, features), jnp.bfloat16),
    )
    scores, lse_rows, live_all, owners, kept = forward_piece(
        starting,
        (
            lax.all_gather(bundle_vectors, "blk", axis=0, tiled=True),
            lax.all_gather(bundle_masks, "blk", axis=0, tiled=True),
            lax.all_gather(bundle_targets, "blk", axis=0, tiled=True),
        ),
        jnp.int32(0),
    )
    position = lax.axis_index(("blk", "group"))
    page_ids = position * local_pages + jnp.arange(local_pages, dtype=jnp.int32)
    chosen = owners[:, None] == page_ids[None, :]
    picked_local = jnp.sum(jnp.where(chosen, scores, 0.0))
    local_top = jnp.max(scores, axis=1)
    local_total = jnp.sum(jnp.exp(scores - local_top[:, None]), axis=1)
    highest, totals, picked = combined_all(
        (local_top, local_total, picked_local), ("blk", "group"), combine_parts
    )
    page_lse = highest + jnp.log(totals)
    mean_loss = (jnp.sum(page_lse) - picked) / total_queries
    coefficient = jnp.exp(scores - page_lse[:, None]) - chosen.astype(jnp.float32)
    factor_scale = coefficient[:, None, :] * live_all.astype(jnp.float32)[:, :, None]

    def slice_rows(root_row, amount):
        sums = lax.dynamic_slice_in_dim(lse_rows, root_row, amount, 0).reshape(
            amount * tokens, local_pages
        )
        scales = lax.dynamic_slice_in_dim(factor_scale, root_row, amount, 0).reshape(
            amount * tokens, local_pages
        )
        return (sums, scales)

    def gradient_terms(row_block, logsumexp_results, scales, page_grads):
        partial_value = jnp.zeros(row_block.shape, jnp.float32)
        for number in range(local_pages):
            masked = masked_logits(row_block, page_vectors[number], page_mask[number])
            weights = jnp.exp(masked - logsumexp_results[:, number : number + 1])
            factor = (scales[:, number : number + 1] * weights).astype(jnp.bfloat16)
            partial_value = partial_value + jnp.dot(
                factor, page_vectors[number], preferred_element_type=jnp.float32
            )
            update = lax.dot_general(
                factor, row_block, (((0,), (0,)), ((), ())), preferred_element_type=jnp.float32
            )
            page_grads = page_grads.at[number].add(update)
        return (partial_value, page_grads)

    home = lax.axis_index("blk")
    page_grads = jnp.zeros(page_vectors.shape, jnp.float32)

    def visit_one(moving, collected, page_grads, lap_index):
        root_row = (home - lap_index) % blocks * bundle_size
        sums, scales = slice_rows(root_row, bundle_size)
        partial_value, page_grads = gradient_terms(
            moving.reshape(bundle_size * tokens, features), sums, scales, page_grads
        )
        return (collected + partial_value.reshape(bundle_size, tokens, features), page_grads)

    def pass_one(collected):
        return from_behind(collected, "blk", 1)

    def turn_one(lap_index, current):
        moving, collected, page_grads = current
        collected, page_grads = visit_one(moving, collected, page_grads, lap_index)
        moving = from_behind(moving, "blk", 1)
        return (moving, pass_one(collected), page_grads)

    empty_whole = jnp.zeros((bundle_size, tokens, features), jnp.float32)
    moving, collected, page_grads = lax.fori_loop(
        0, blocks - 1, turn_one, (bundle_vectors, empty_whole, page_grads)
    )
    collected, page_grads = visit_one(moving, collected, page_grads, blocks - 1)
    collected = pass_one(collected)
    grad_queries = lax.psum_scatter(collected, "group", scatter_dimension=0, tiled=True)
    return (grad_queries, page_grads, mean_loss)


LANES = 128
EXTRA = 2
FACTS = 16
KERNEL_VMEM = 16 * 2**20
HALF_SCALE = 2.0**14


def fits(queries, page_vectors, devices):
    tokens, features = queries.shape[1:]
    lanes = devices * tokens
    return (
        queries.shape[0] == 1
        and tokens == FACTS
        and features == LANES
        and page_vectors.shape[1] == LANES
        and page_vectors.shape[0] <= FACTS - 3
        and lanes % LANES == 0
        and lanes // LANES <= 8
        and lax.axis_size("blk") % 2 == 0
    )


def segment_sum(values, width):
    lanes = values.shape[1]
    lane = lax.broadcasted_iota(jnp.int32, values.shape, 1)
    step = 1
    while step < width:
        ahead = pltpu.roll(values, lanes - step, 1)
        behind = pltpu.roll(values, step, 1)
        values = values + jnp.where((lane & step) == 0, ahead, behind)
        step *= 2
    return values


def spread_runs(line, width):
    lane = lax.broadcasted_iota(jnp.int32, (8, LANES), 1)
    row = lax.broadcasted_iota(jnp.int32, (8, LANES), 0)
    return jnp.take_along_axis(jnp.broadcast_to(line, (8, LANES)), lane // width * width + row, axis=1)


def split_half(value):
    scaled = value * 8193.0
    high = scaled - (scaled - value)
    return high, value - high


def facts_kernel(target_ref, query_mask_ref, page_mask_ref, facts_ref):
    half = query_mask_ref.shape[1] // 2
    alive = jnp.sum(query_mask_ref[...].astype(jnp.float32), axis=1, keepdims=True)
    kind = lax.broadcasted_iota(jnp.int32, (EXTRA, LANES), 1) % half
    number = target_ref[...].reshape(1, 1)
    facts = jnp.where(kind == 0, alive, 0.0)
    facts = jnp.where(kind == 1, (number >> 8).astype(jnp.float32), facts)
    facts = jnp.where(kind == 2, (number & 255).astype(jnp.float32), facts)
    for page in range(page_mask_ref.shape[0]):
        count = jnp.sum(page_mask_ref[page : page + 1, :].astype(jnp.float32), axis=1, keepdims=True)
        facts = jnp.where(kind == 3 + page, count, facts)
    facts_ref[...] = facts


def message_kernel(facts_ref, queries_ref, out_ref):
    devices = out_ref.shape[0]
    half = queries_ref.shape[1] // 2
    members = lax.axis_size("group")
    out_rows = out_ref.reshape(devices, half + EXTRA, LANES)
    for device in range(devices):
        begin = (device // members) % 2 * half
        out_rows[device, 0:half, :] = queries_ref[0, begin : begin + half, :]
    out_ref[:, half // 2] = jnp.broadcast_to(facts_ref[...].astype(jnp.bfloat16)[None], (devices, EXTRA, LANES))


def measure_pages(rows_q, vectors, flips, counts, alive, powers_ref=None):
    width = rows_q.shape[0]
    patch = lax.broadcasted_iota(jnp.int32, (LANES, width), 0).astype(jnp.float32)
    steep = 1.0 / (relaxation_scale_factor * math.log(2.0))
    softened, inverses, mixes = [], [], []
    stack = jnp.concatenate(vectors, axis=0)
    similarities = lax.dot_general(stack, rows_q, (((1,), (1,)), ((), ())), preferred_element_type=jnp.float32)
    for page, (flipped, count) in enumerate(zip(flips, counts)):
        similarity = similarities[page * LANES : (page + 1) * LANES]
        masked = jnp.where(patch < count, similarity, guarded_floor_entry)
        highest = jnp.max(masked, axis=0, keepdims=True)
        powers = jnp.exp2((masked - highest) * steep)
        if powers_ref is not None:
            powers_ref[page] = powers
        high = powers.astype(jnp.bfloat16)
        low = (powers - high.astype(jnp.float32)).astype(jnp.bfloat16)
        mixes.append(
            jnp.dot(
                jnp.concatenate([flipped, flipped], axis=1),
                jnp.concatenate([high, low], axis=0),
                preferred_element_type=jnp.float32,
            )
        )
        total = jnp.sum(powers, axis=0, keepdims=True)
        lse = highest * (1.0 / relaxation_scale_factor) + jnp.log(total)
        softened.append(alive * (relaxation_scale_factor * (lse - jnp.log(count))))
        inverses.append(alive / total)
    return softened, inverses, mixes


def gather_rows(from_ref, to_ref):
    sources = from_ref.shape[0]
    half = 2 * (from_ref.shape[1] - 1)
    view = from_ref.reshape(sources, half + EXTRA, LANES)
    for source in range(sources):
        to_ref[source * half : (source + 1) * half, :] = view[source, 0:half, :]


def page_counts(sent_ref, home, local_pages):
    facts = sent_ref[home, sent_ref.shape[1] - 1].astype(jnp.float32)
    return [facts[0:1, 3 + number : 4 + number] for number in range(local_pages)]


def near_kernel(sent_ref, own_ref, rows_ref, power_ref, soft_ref, inverse_ref, facts_ref, mix_ref, flip_ref):
    sources = sent_ref.shape[0]
    half = 2 * (sent_ref.shape[1] - 1)
    part = sources * half
    per_chunk = LANES // half
    local_pages = own_ref.shape[0]
    blk = lax.axis_index("blk")
    home = blk * lax.axis_size("group") + lax.axis_index("group")
    slot = lax.broadcasted_iota(jnp.int32, (1, LANES), 1) // half
    facts = []
    for c in range(part // LANES):
        told = jnp.zeros((1, LANES), jnp.float32)
        for i in range(per_chunk):
            told = jnp.where(slot == i, sent_ref[c * per_chunk + i, half // 2, 0:1, :].astype(jnp.float32), told)
        facts.append(spread_runs(told, half))
    facts = jnp.concatenate(facts, axis=1)
    facts_ref[...] = facts
    token = lax.broadcasted_iota(jnp.int32, (1, part), 1) % half + (blk & 1) * half
    alive = (token.astype(jnp.float32) < facts[0:1]).astype(jnp.float32)
    gather_rows(sent_ref, rows_ref)
    vectors = [own_ref[page] for page in range(local_pages)]
    flips = [block.T for block in vectors]
    softened, inverses, mixes = measure_pages(
        rows_ref[...], vectors, flips, page_counts(sent_ref, home, local_pages), alive, power_ref
    )
    for page in range(local_pages):
        mix_ref[page] = mixes[page]
        flip_ref[page] = flips[page]
        soft_ref[page : page + 1, :] = softened[page]
        inverse_ref[page : page + 1, :] = inverses[page]


def far_kernel(*refs):
    sent_ref, swapped_ref, own_ref, other_ref, near_rows_ref, near_mix_ref, near_soft_ref, near_inverse_ref = refs[:8]
    facts_ref, flip_ref, out_ref, power_ref, score_ref, inverse_ref, rows_ref = refs[8:]
    sources = sent_ref.shape[0]
    half = 2 * (sent_ref.shape[1] - 1)
    part = sources * half
    local_pages = own_ref.shape[0]
    blk = lax.axis_index("blk")
    group = lax.axis_index("group")
    members = lax.axis_size("group")
    homes = [blk * members + group, (blk ^ 1) * members + group]
    side = blk & 1
    sends_sum = side == 0
    own_range = range(local_pages)
    ids = [home * local_pages + page for home in homes for page in own_range]
    own = [own_ref[page] for page in own_range]
    other = [other_ref[page] for page in own_range]
    own_flips = [flip_ref[page] for page in own_range]
    other_flips = [block.T for block in other]
    own_counts = page_counts(sent_ref, homes[0], local_pages)
    other_counts = page_counts(sent_ref, homes[1], local_pages)

    facts = facts_ref[...]
    target = (facts[1:2] * 256.0 + facts[2:3]).astype(jnp.int32)
    spot = lax.broadcasted_iota(jnp.int32, (1, part), 1) % half
    near_alive = ((spot + side * half).astype(jnp.float32) < facts[0:1]).astype(jnp.float32)
    far_alive = ((spot + (1 - side) * half).astype(jnp.float32) < facts[0:1]).astype(jnp.float32)
    other_soft, other_inverse, other_mix = measure_pages(near_rows_ref[...], other, other_flips, other_counts, near_alive)
    gather_rows(swapped_ref, rows_ref)
    rows_q = rows_ref[...]
    far_soft, far_inverse, far_mix = measure_pages(rows_q, own, own_flips, own_counts, far_alive, power_ref)
    cross_soft, cross_inverse, cross_mix = measure_pages(rows_q, other, other_flips, other_counts, far_alive)
    near_mix = [near_mix_ref[page] for page in own_range]
    near_soft = [near_soft_ref[page : page + 1, :] for page in own_range]
    near_inverse = [near_inverse_ref[page : page + 1, :] for page in own_range]
    for page in own_range:
        inverse_ref[page : page + 1, :] = far_inverse[page]
    softened = [a + b for a, b in zip(near_soft + other_soft, far_soft + cross_soft)]
    scores = segment_sum(jnp.concatenate(softened, axis=0), half)
    top = jnp.max(scores, axis=0, keepdims=True)
    chip_lse = top + jnp.log(jnp.sum(jnp.exp(scores - top), axis=0, keepdims=True))

    picked = jnp.zeros((1, part), jnp.float32)
    shares = []
    for page, name in enumerate(ids):
        score = scores[page : page + 1]
        hit = target == name
        picked = picked + jnp.where(hit, score, 0.0)
        shares.append(jnp.where(sends_sum, jnp.exp(score - chip_lse), hit.astype(jnp.float32)))
        if page < local_pages:
            score_ref[page : page + 1, :] = score
            score_ref[local_pages + page : local_pages + page + 1, :] = hit.astype(jnp.float32)
    high, low = split_half(jnp.where(sends_sum, chip_lse, picked))
    high_line = jnp.zeros((1, LANES), jnp.float32)
    low_line = jnp.zeros((1, LANES), jnp.float32)
    for c in range(part // LANES):
        high_line = jnp.where(spot[:, 0:LANES] == c, high[:, c * LANES : (c + 1) * LANES], high_line)
        low_line = jnp.where(spot[:, 0:LANES] == c, low[:, c * LANES : (c + 1) * LANES], low_line)
    lines = jnp.concatenate([high_line, low_line], axis=0)
    out_ref[:, half] = jnp.broadcast_to(lines[None], (sources, EXTRA, LANES))

    out_rows = out_ref.reshape(sources, 2 * half + EXTRA, LANES)
    for position, (mixes, inverses) in enumerate(
        ((near_mix + other_mix, near_inverse + other_inverse), (far_mix + cross_mix, far_inverse + cross_inverse))
    ):
        mixed = sum(mix * (inverse * (share * HALF_SCALE)) for mix, inverse, share in zip(mixes, inverses, shares))
        mixed = mixed.T
        for source in range(sources):
            out_rows[source, position * half : (position + 1) * half, :] = mixed[
                source * half : (source + 1) * half, :
            ]


def last_kernel(tokens, got_ref, score_ref, *rest):
    near, far, results = rest[0:3], rest[3:6], rest[6:]
    grad_q_out, grad_p_out, loss_out, grad_q_ref, grad_p_ref, loss_ref, sems = results
    sources = got_ref.shape[0]
    half = tokens // 2
    chunks = sources * half // LANES
    per_chunk = LANES // half
    local_pages = grad_p_ref.shape[0]
    blk = lax.axis_index("blk")
    group = lax.axis_index("group")
    members = lax.axis_size("group")
    me = blk * members + group
    even = [s for s in range(sources) if (s // members) % 2 == 0]
    odd = [s for s in range(sources) if (s // members) % 2 == 1]

    def stats(source):
        return got_ref[source, tokens // 2, 0:1, :] + got_ref[source, tokens // 2, 1:2, :]

    def tree(combine, values):
        while len(values) > 1:
            values = [combine(*values[i : i + 2]) if i + 1 < len(values) else values[i] for i in range(0, len(values), 2)]
        return values[0]

    chip_lse = [stats(s) for s in even]
    top = tree(jnp.maximum, chip_lse)
    page_lse = top + jnp.log(tree(jnp.add, [jnp.exp(c - top) for c in chip_lse]))
    spread = spread_runs(page_lse, half)
    flat = jnp.concatenate([spread[c : c + 1] for c in range(chunks)], axis=1)
    copies = []
    for page in range(local_pages):
        score = score_ref[page : page + 1, :]
        hit = score_ref[local_pages + page : local_pages + page + 1, :]
        coefficient = jnp.exp(score - flat) - hit
        grad_p = jnp.zeros((LANES, LANES), jnp.float32)
        for rows_ref, power_ref, inverse_ref in (near, far):
            factor = (coefficient * inverse_ref[page : page + 1, :] * power_ref[page]).astype(jnp.bfloat16)
            grad_p += jnp.dot(factor, rows_ref[...], preferred_element_type=jnp.float32)
        grad_p_ref[page] = grad_p
        copies.append(pltpu.make_async_copy(grad_p_ref.at[page], grad_p_out.at[page], sems.at[page]))
        copies[-1].start()

    lane = lax.broadcasted_iota(jnp.int32, (1, LANES), 1)
    mine = lane == (me % per_chunk) * half + me // per_chunk
    ratios = jnp.concatenate([jnp.where(mine, jnp.exp(c - page_lse), 0.0) for c in chip_lse], axis=0)
    ratios = jnp.sum(ratios, axis=1, keepdims=True) * (1.0 / HALF_SCALE)
    ratios = jnp.broadcast_to(ratios, ratios.shape[:1] + (LANES,))
    got_rows = got_ref.reshape(sources, tokens + EXTRA, LANES)
    terms = [ratios[i : i + 1, :] * got_rows[s, 0:tokens, :] for i, s in enumerate(even)]
    sums = tree(jnp.add, terms)
    single = tree(jnp.add, [got_rows[s, 0:tokens, :] for s in odd]) * (1.0 / HALF_SCALE)
    grad_q_ref[0, 0:half, :] = sums[0:half] - single[half:tokens]
    grad_q_ref[0, half:tokens, :] = sums[half:tokens] - single[0:half]
    copies.append(pltpu.make_async_copy(grad_q_ref, grad_q_out, sems.at[local_pages]))
    copies[-1].start()

    picked = tree(jnp.add, [stats(s) for s in odd])
    difference = jnp.where(lane % half < chunks, page_lse - picked, 0.0)
    loss_ref[...] = jnp.sum(difference, axis=1, keepdims=True) * (1.0 / sources)
    copies.append(pltpu.make_async_copy(loss_ref, loss_out, sems.at[local_pages + 1]))
    copies[-1].start()
    for copy in copies:
        copy.wait()


def exchange(blocks_to_all):
    return lax.all_to_all(blocks_to_all, ("blk", "group"), 0, 0, tiled=True)


def two_exchanges(queries, query_mask, positive, page_vectors, page_mask):
    tokens = queries.shape[1]
    local_pages = page_vectors.shape[0]
    devices = lax.axis_size("blk") * lax.axis_size("group")
    lanes = devices * tokens
    blocks = lax.axis_size("blk")
    half = tokens // 2
    pairs = (tokens + EXTRA) // 2
    swap = [(b, b ^ 1) for b in range(blocks)]

    vmem = pl.BlockSpec(memory_space=pltpu.VMEM)
    anywhere = pl.BlockSpec(memory_space=pl.ANY)
    params = pltpu.CompilerParams(vmem_limit_bytes=KERNEL_VMEM)
    told = pl.pallas_call(
        facts_kernel,
        out_shape=jax.ShapeDtypeStruct((EXTRA, LANES), jnp.float32),
        in_specs=[vmem] * 3,
        out_specs=vmem,
        compiler_params=params,
        cost_estimate=pl.CostEstimate(flops=1000000, bytes_accessed=10000, transcendentals=0),
    )(positive, query_mask, page_mask)
    message = pl.pallas_call(
        message_kernel,
        out_shape=jax.ShapeDtypeStruct((devices, (half + EXTRA) // 2, 2, LANES), jnp.bfloat16),
        in_specs=[vmem] * 2,
        out_specs=vmem,
        compiler_params=params,
    )(told, queries)
    sent = exchange(message)
    sent, page_vectors = lax.optimization_barrier((sent, page_vectors))
    swapped = lax.ppermute(sent, "blk", swap)
    other_vectors = lax.ppermute(page_vectors, "blk", swap)
    part = lanes // 2
    kept = (
        jax.ShapeDtypeStruct((part, LANES), jnp.bfloat16),
        jax.ShapeDtypeStruct((local_pages, LANES, part), jnp.float32),
        jax.ShapeDtypeStruct((local_pages, part), jnp.float32),
    )
    near_rows, near_powers, near_soft, near_inverses, facts, near_mix, flips = pl.pallas_call(
        near_kernel,
        out_shape=kept + (kept[2], jax.ShapeDtypeStruct((8, part), jnp.float32), kept[1], jax.ShapeDtypeStruct(page_vectors.shape, jnp.bfloat16)),
        in_specs=[vmem] * 2,
        out_specs=(vmem,) * 7,
        compiler_params=params,
        cost_estimate=pl.CostEstimate(flops=4 * part * LANES * LANES, bytes_accessed=2**20, transcendentals=part * LANES),
    )(sent, page_vectors)
    out, far_powers, scores, far_inverses, far_rows = pl.pallas_call(
        far_kernel,
        out_shape=(
            jax.ShapeDtypeStruct((devices, pairs, 2, LANES), jnp.float32),
            kept[1],
            jax.ShapeDtypeStruct((2 * local_pages, part), jnp.float32),
            kept[2],
            kept[0],
        ),
        in_specs=[vmem] * 10,
        out_specs=(vmem,) * 5,
        compiler_params=params,
    )(sent, swapped, page_vectors, other_vectors, near_rows, near_mix, near_soft, near_inverses, facts, flips)
    got = exchange(out.astype(jnp.float16)).astype(jnp.float32)
    grad_q, grad_p, loss = pl.pallas_call(
        functools.partial(last_kernel, tokens),
        out_shape=(
            jax.ShapeDtypeStruct(queries.shape, jnp.float32),
            jax.ShapeDtypeStruct(page_vectors.shape, jnp.float32),
            jax.ShapeDtypeStruct((1, 1), jnp.float32),
        ),
        in_specs=[vmem] * 8,
        out_specs=(anywhere,) * 3,
        scratch_shapes=[
            pltpu.VMEM(queries.shape, jnp.float32),
            pltpu.VMEM(page_vectors.shape, jnp.float32),
            pltpu.VMEM((1, 1), jnp.float32),
            pltpu.SemaphoreType.DMA((local_pages + 2,)),
        ],
        compiler_params=params,
    )(got, scores, near_rows, near_powers, near_inverses, far_rows, far_powers, far_inverses)
    return (grad_q, grad_p, loss[0, 0])


def on_device(queries, query_mask, positive, page_vectors, page_mask):
    devices = lax.axis_size("blk") * lax.axis_size("group")
    chosen = two_exchanges if fits(queries, page_vectors, devices) else general_path
    return chosen(queries, query_mask, positive, page_vectors, page_mask)


def solution(mesh):
    in_specs = (
        P(("blk", "group"), None, None),
        P(("blk", "group"), None),
        P(("blk", "group")),
        P(("blk", "group"), None, None),
        P(("blk", "group"), None),
    )
    out_specs = (P(("blk", "group"), None, None), P(("blk", "group"), None, None), P())
    return jax.shard_map(
        on_device, mesh=mesh, in_specs=in_specs, out_specs=out_specs, check_vma=False
    )
```

```python
import functools
import math

import jax
import jax.numpy as jnp
from jax import lax
from jax.experimental import pallas as pl
from jax.experimental.pallas import tpu as pltpu
from jax.sharding import PartitionSpec as P

relaxation_scale_factor = 0.5
guarded_floor_entry = -1e30


def combined_all(part, axis, combine):
    gathered = jax.tree.map(lambda a: lax.all_gather(a, axis), part)

    def take(source):
        return jax.tree.map(lambda a: lax.dynamic_index_in_dim(a, source, 0, False), gathered)

    return lax.fori_loop(
        1, lax.axis_size(axis), lambda source, state: combine(state, take(source)), take(0)
    )


def from_behind(value, axis, steps):
    count = lax.axis_size(axis)
    pairs = [(source, (source + steps) % count) for source in range(count)]
    return lax.ppermute(value, axis, pairs)


def masked_logits(row_block, lone_document, live_image_embeddings):
    similarity_matrix = lax.dot_general(
        row_block, lone_document, (((1,), (1,)), ((), ())), preferred_element_type=jnp.float32
    )
    return jnp.where(
        live_image_embeddings[None, :] > 0,
        similarity_matrix / relaxation_scale_factor,
        guarded_floor_entry,
    )


def combine_parts(earlier, later):
    highest = jnp.maximum(earlier[0], later[0])
    totals = earlier[1] * jnp.exp(earlier[0] - highest) + later[1] * jnp.exp(later[0] - highest)
    return (highest, totals, earlier[2] + later[2])


def general_path(queries, query_mask, positive, page_vectors, page_mask):
    tokens = queries.shape[1]
    features = queries.shape[2]
    local_pages = page_vectors.shape[0]
    blocks = lax.axis_size("blk")
    members = lax.axis_size("group")
    bundle_size = queries.shape[0] * members
    total_queries = bundle_size * blocks
    natural_logarithm_lengths = jnp.log(jnp.sum(page_mask.astype(jnp.float32), axis=1))
    bundle_vectors, bundle_masks, bundle_targets = (
        lax.all_gather(queries, "group", axis=0, tiled=True),
        lax.all_gather(query_mask, "group", axis=0, tiled=True),
        lax.all_gather(positive, "group", axis=0, tiled=True),
    )

    def forward_piece(folded, shard_in, root_row):
        scores, lse_rows, live_all, owners, kept = folded
        vectors, token_masks, targets = shard_in
        amount = vectors.shape[0]
        stride = math.gcd(amount, max(1, 512 // tokens))

        def run_block(number, current):
            scores, lse_rows = current
            offset = number * stride
            slab_rows = lax.dynamic_slice_in_dim(vectors, offset, stride, 0).reshape(
                stride * tokens, features
            )
            alive = lax.dynamic_slice_in_dim(token_masks, offset, stride, 0).astype(jnp.float32)
            found_sums = []
            for index_page in range(local_pages):
                masked = masked_logits(slab_rows, page_vectors[index_page], page_mask[index_page])
                highest = jnp.max(masked, axis=1, keepdims=True)
                found_sums.append(
                    highest[:, 0] + jnp.log(jnp.sum(jnp.exp(masked - highest), axis=1))
                )
            logsumexp_results = jnp.stack(found_sums, axis=1).reshape(stride, tokens, local_pages)
            softened_supremum = relaxation_scale_factor * (
                logsumexp_results - natural_logarithm_lengths
            )
            page_score = jnp.sum(alive[:, :, None] * softened_supremum, axis=1)
            scores = lax.dynamic_update_slice_in_dim(scores, page_score, offset, 0)
            lse_rows = lax.dynamic_update_slice_in_dim(lse_rows, logsumexp_results, offset, 0)
            return (scores, lse_rows)

        scores, lse_rows = lax.fori_loop(0, amount // stride, run_block, (scores, lse_rows))
        live_all = lax.dynamic_update_slice_in_dim(live_all, token_masks, root_row, 0)
        owners = lax.dynamic_update_slice_in_dim(owners, targets, root_row, 0)
        kept = vectors
        return (scores, lse_rows, live_all, owners, kept)

    starting = (
        jnp.zeros((total_queries, local_pages), jnp.float32),
        jnp.zeros((total_queries, tokens, local_pages), jnp.float32),
        jnp.zeros((total_queries, tokens), jnp.int32),
        jnp.zeros((total_queries,), jnp.int32),
        jnp.zeros((total_queries, tokens, features), jnp.bfloat16),
    )
    scores, lse_rows, live_all, owners, kept = forward_piece(
        starting,
        (
            lax.all_gather(bundle_vectors, "blk", axis=0, tiled=True),
            lax.all_gather(bundle_masks, "blk", axis=0, tiled=True),
            lax.all_gather(bundle_targets, "blk", axis=0, tiled=True),
        ),
        jnp.int32(0),
    )
    position = lax.axis_index(("blk", "group"))
    page_ids = position * local_pages + jnp.arange(local_pages, dtype=jnp.int32)
    chosen = owners[:, None] == page_ids[None, :]
    picked_local = jnp.sum(jnp.where(chosen, scores, 0.0))
    local_top = jnp.max(scores, axis=1)
    local_total = jnp.sum(jnp.exp(scores - local_top[:, None]), axis=1)
    highest, totals, picked = combined_all(
        (local_top, local_total, picked_local), ("blk", "group"), combine_parts
    )
    page_lse = highest + jnp.log(totals)
    mean_loss = (jnp.sum(page_lse) - picked) / total_queries
    coefficient = jnp.exp(scores - page_lse[:, None]) - chosen.astype(jnp.float32)
    factor_scale = coefficient[:, None, :] * live_all.astype(jnp.float32)[:, :, None]

    def slice_rows(root_row, amount):
        sums = lax.dynamic_slice_in_dim(lse_rows, root_row, amount, 0).reshape(
            amount * tokens, local_pages
        )
        scales = lax.dynamic_slice_in_dim(factor_scale, root_row, amount, 0).reshape(
            amount * tokens, local_pages
        )
        return (sums, scales)

    def gradient_terms(row_block, logsumexp_results, scales, page_grads):
        partial_value = jnp.zeros(row_block.shape, jnp.float32)
        for number in range(local_pages):
            masked = masked_logits(row_block, page_vectors[number], page_mask[number])
            weights = jnp.exp(masked - logsumexp_results[:, number : number + 1])
            factor = (scales[:, number : number + 1] * weights).astype(jnp.bfloat16)
            partial_value = partial_value + jnp.dot(
                factor, page_vectors[number], preferred_element_type=jnp.float32
            )
            update = lax.dot_general(
                factor, row_block, (((0,), (0,)), ((), ())), preferred_element_type=jnp.float32
            )
            page_grads = page_grads.at[number].add(update)
        return (partial_value, page_grads)

    home = lax.axis_index("blk")
    page_grads = jnp.zeros(page_vectors.shape, jnp.float32)

    def visit_one(moving, collected, page_grads, lap_index):
        root_row = (home - lap_index) % blocks * bundle_size
        sums, scales = slice_rows(root_row, bundle_size)
        partial_value, page_grads = gradient_terms(
            moving.reshape(bundle_size * tokens, features), sums, scales, page_grads
        )
        return (collected + partial_value.reshape(bundle_size, tokens, features), page_grads)

    def pass_one(collected):
        return from_behind(collected, "blk", 1)

    def turn_one(lap_index, current):
        moving, collected, page_grads = current
        collected, page_grads = visit_one(moving, collected, page_grads, lap_index)
        moving = from_behind(moving, "blk", 1)
        return (moving, pass_one(collected), page_grads)

    empty_whole = jnp.zeros((bundle_size, tokens, features), jnp.float32)
    moving, collected, page_grads = lax.fori_loop(
        0, blocks - 1, turn_one, (bundle_vectors, empty_whole, page_grads)
    )
    collected, page_grads = visit_one(moving, collected, page_grads, blocks - 1)
    collected = pass_one(collected)
    grad_queries = lax.psum_scatter(collected, "group", scatter_dimension=0, tiled=True)
    return (grad_queries, page_grads, mean_loss)


LANES = 128
EXTRA = 2
FACTS = 16
KERNEL_VMEM = 16 * 2**20
HALF_SCALE = 2.0**14


def fits(queries, page_vectors, devices):
    tokens, features = queries.shape[1:]
    lanes = devices * tokens
    return (
        queries.shape[0] == 1
        and tokens == FACTS
        and features == LANES
        and page_vectors.shape[1] == LANES
        and page_vectors.shape[0] <= FACTS - 3
        and lanes % LANES == 0
        and lanes // LANES <= 8
        and lax.axis_size("blk") % 2 == 0
    )


def segment_sum(values, width):
    lanes = values.shape[1]
    lane = lax.broadcasted_iota(jnp.int32, values.shape, 1)
    step = 1
    while step < width:
        ahead = pltpu.roll(values, lanes - step, 1)
        behind = pltpu.roll(values, step, 1)
        values = values + jnp.where((lane & step) == 0, ahead, behind)
        step *= 2
    return values


def spread_runs(line, width):
    lane = lax.broadcasted_iota(jnp.int32, (8, LANES), 1)
    row = lax.broadcasted_iota(jnp.int32, (8, LANES), 0)
    return jnp.take_along_axis(jnp.broadcast_to(line, (8, LANES)), lane // width * width + row, axis=1)


def split_half(value):
    scaled = value * 8193.0
    high = scaled - (scaled - value)
    return high, value - high


def facts_kernel(target_ref, query_mask_ref, page_mask_ref, facts_ref):
    half = query_mask_ref.shape[1] // 2
    alive = jnp.sum(query_mask_ref[...].astype(jnp.float32), axis=1, keepdims=True)
    kind = lax.broadcasted_iota(jnp.int32, (EXTRA, LANES), 1) % half
    number = target_ref[...].reshape(1, 1)
    facts = jnp.where(kind == 0, alive, 0.0)
    facts = jnp.where(kind == 1, (number >> 8).astype(jnp.float32), facts)
    facts = jnp.where(kind == 2, (number & 255).astype(jnp.float32), facts)
    for page in range(page_mask_ref.shape[0]):
        count = jnp.sum(page_mask_ref[page : page + 1, :].astype(jnp.float32), axis=1, keepdims=True)
        facts = jnp.where(kind == 3 + page, count, facts)
    facts_ref[...] = facts


def message_kernel(facts_ref, queries_ref, out_ref):
    devices = out_ref.shape[0]
    half = queries_ref.shape[1] // 2
    members = lax.axis_size("group")
    out_rows = out_ref.reshape(devices, half + EXTRA, LANES)
    for device in range(devices):
        begin = (device // members) % 2 * half
        out_rows[device, 0:half, :] = queries_ref[0, begin : begin + half, :]
    out_ref[:, half // 2] = jnp.broadcast_to(facts_ref[...].astype(jnp.bfloat16)[None], (devices, EXTRA, LANES))


def measure_pages(rows_q, vectors, flips, counts, alive, powers_ref=None):
    width = rows_q.shape[0]
    patch = lax.broadcasted_iota(jnp.int32, (LANES, width), 0).astype(jnp.float32)
    steep = 1.0 / (relaxation_scale_factor * math.log(2.0))
    softened, inverses, mixes = [], [], []
    stack = jnp.concatenate(vectors, axis=0)
    similarities = lax.dot_general(stack, rows_q, (((1,), (1,)), ((), ())), preferred_element_type=jnp.float32)
    for page, (flipped, count) in enumerate(zip(flips, counts)):
        similarity = similarities[page * LANES : (page + 1) * LANES]
        masked = jnp.where(patch < count, similarity, guarded_floor_entry)
        highest = jnp.max(masked, axis=0, keepdims=True)
        powers = jnp.exp2((masked - highest) * steep)
        if powers_ref is not None:
            powers_ref[page] = powers
        high = powers.astype(jnp.bfloat16)
        low = (powers - high.astype(jnp.float32)).astype(jnp.bfloat16)
        mixes.append(
            jnp.dot(
                jnp.concatenate([flipped, flipped], axis=1),
                jnp.concatenate([high, low], axis=0),
                preferred_element_type=jnp.float32,
            )
        )
        total = jnp.sum(powers, axis=0, keepdims=True)
        lse = highest * (1.0 / relaxation_scale_factor) + jnp.log(total)
        softened.append(alive * (relaxation_scale_factor * (lse - jnp.log(count))))
        inverses.append(alive / total)
    return softened, inverses, mixes


def gather_rows(from_ref, to_ref):
    sources = from_ref.shape[0]
    half = 2 * (from_ref.shape[1] - 1)
    view = from_ref.reshape(sources, half + EXTRA, LANES)
    for source in range(sources):
        to_ref[source * half : (source + 1) * half, :] = view[source, 0:half, :]


def page_counts(sent_ref, home, local_pages):
    facts = sent_ref[home, sent_ref.shape[1] - 1].astype(jnp.float32)
    return [facts[0:1, 3 + number : 4 + number] for number in range(local_pages)]


def near_kernel(sent_ref, own_ref, rows_ref, power_ref, soft_ref, inverse_ref, facts_ref, mix_ref, flip_ref):
    sources = sent_ref.shape[0]
    half = 2 * (sent_ref.shape[1] - 1)
    part = sources * half
    per_chunk = LANES // half
    local_pages = own_ref.shape[0]
    blk = lax.axis_index("blk")
    home = blk * lax.axis_size("group") + lax.axis_index("group")
    slot = lax.broadcasted_iota(jnp.int32, (1, LANES), 1) // half
    facts = []
    for c in range(part // LANES):
        told = jnp.zeros((1, LANES), jnp.float32)
        for i in range(per_chunk):
            told = jnp.where(slot == i, sent_ref[c * per_chunk + i, half // 2, 0:1, :].astype(jnp.float32), told)
        facts.append(spread_runs(told, half))
    facts = jnp.concatenate(facts, axis=1)
    facts_ref[...] = facts
    token = lax.broadcasted_iota(jnp.int32, (1, part), 1) % half + (blk & 1) * half
    alive = (token.astype(jnp.float32) < facts[0:1]).astype(jnp.float32)
    gather_rows(sent_ref, rows_ref)
    vectors = [own_ref[page] for page in range(local_pages)]
    flips = [block.T for block in vectors]
    softened, inverses, mixes = measure_pages(
        rows_ref[...], vectors, flips, page_counts(sent_ref, home, local_pages), alive, power_ref
    )
    for page in range(local_pages):
        mix_ref[page] = mixes[page]
        flip_ref[page] = flips[page]
        soft_ref[page : page + 1, :] = softened[page]
        inverse_ref[page : page + 1, :] = inverses[page]


def far_kernel(*refs):
    sent_ref, swapped_ref, own_ref, other_ref, near_rows_ref, near_mix_ref, near_soft_ref, near_inverse_ref = refs[:8]
    facts_ref, flip_ref, out_ref, power_ref, score_ref, inverse_ref, rows_ref = refs[8:]
    sources = sent_ref.shape[0]
    half = 2 * (sent_ref.shape[1] - 1)
    part = sources * half
    local_pages = own_ref.shape[0]
    blk = lax.axis_index("blk")
    group = lax.axis_index("group")
    members = lax.axis_size("group")
    homes = [blk * members + group, (blk ^ 1) * members + group]
    side = blk & 1
    sends_sum = side == 0
    own_range = range(local_pages)
    ids = [home * local_pages + page for home in homes for page in own_range]
    own = [own_ref[page] for page in own_range]
    other = [other_ref[page] for page in own_range]
    own_flips = [flip_ref[page] for page in own_range]
    other_flips = [block.T for block in other]
    own_counts = page_counts(sent_ref, homes[0], local_pages)
    other_counts = page_counts(sent_ref, homes[1], local_pages)

    facts = facts_ref[...]
    target = (facts[1:2] * 256.0 + facts[2:3]).astype(jnp.int32)
    spot = lax.broadcasted_iota(jnp.int32, (1, part), 1) % half
    near_alive = ((spot + side * half).astype(jnp.float32) < facts[0:1]).astype(jnp.float32)
    far_alive = ((spot + (1 - side) * half).astype(jnp.float32) < facts[0:1]).astype(jnp.float32)
    other_soft, other_inverse, other_mix = measure_pages(near_rows_ref[...], other, other_flips, other_counts, near_alive)
    gather_rows(swapped_ref, rows_ref)
    rows_q = rows_ref[...]
    far_soft, far_inverse, far_mix = measure_pages(rows_q, own, own_flips, own_counts, far_alive, power_ref)
    cross_soft, cross_inverse, cross_mix = measure_pages(rows_q, other, other_flips, other_counts, far_alive)
    near_mix = [near_mix_ref[page] for page in own_range]
    near_soft = [near_soft_ref[page : page + 1, :] for page in own_range]
    near_inverse = [near_inverse_ref[page : page + 1, :] for page in own_range]
    for page in own_range:
        inverse_ref[page : page + 1, :] = far_inverse[page]
    softened = [a + b for a, b in zip(near_soft + other_soft, far_soft + cross_soft)]
    scores = segment_sum(jnp.concatenate(softened, axis=0), half)
    top = jnp.max(scores, axis=0, keepdims=True)
    chip_lse = top + jnp.log(jnp.sum(jnp.exp(scores - top), axis=0, keepdims=True))

    picked = jnp.zeros((1, part), jnp.float32)
    shares = []
    for page, name in enumerate(ids):
        score = scores[page : page + 1]
        hit = target == name
        picked = picked + jnp.where(hit, score, 0.0)
        shares.append(jnp.where(sends_sum, jnp.exp(score - chip_lse), hit.astype(jnp.float32)))
        if page < local_pages:
            score_ref[page : page + 1, :] = score
            score_ref[local_pages + page : local_pages + page + 1, :] = hit.astype(jnp.float32)
    high, low = split_half(jnp.where(sends_sum, chip_lse, picked))
    high_line = jnp.zeros((1, LANES), jnp.float32)
    low_line = jnp.zeros((1, LANES), jnp.float32)
    for c in range(part // LANES):
        high_line = jnp.where(spot[:, 0:LANES] == c, high[:, c * LANES : (c + 1) * LANES], high_line)
        low_line = jnp.where(spot[:, 0:LANES] == c, low[:, c * LANES : (c + 1) * LANES], low_line)
    lines = jnp.concatenate([high_line, low_line], axis=0)
    out_ref[:, half] = jnp.broadcast_to(lines[None], (sources, EXTRA, LANES))

    out_rows = out_ref.reshape(sources, 2 * half + EXTRA, LANES)
    for position, (mixes, inverses) in enumerate(
        ((near_mix + other_mix, near_inverse + other_inverse), (far_mix + cross_mix, far_inverse + cross_inverse))
    ):
        mixed = sum(mix * (inverse * (share * HALF_SCALE)) for mix, inverse, share in zip(mixes, inverses, shares))
        mixed = mixed.T
        for source in range(sources):
            out_rows[source, position * half : (position + 1) * half, :] = mixed[
                source * half : (source + 1) * half, :
            ]


def last_kernel(tokens, got_ref, score_ref, *rest):
    near, far, results = rest[0:3], rest[3:6], rest[6:]
    grad_q_out, grad_p_out, loss_out, grad_q_ref, grad_p_ref, loss_ref, sems = results
    sources = got_ref.shape[0]
    half = tokens // 2
    chunks = sources * half // LANES
    per_chunk = LANES // half
    local_pages = grad_p_ref.shape[0]
    blk = lax.axis_index("blk")
    group = lax.axis_index("group")
    members = lax.axis_size("group")
    me = blk * members + group
    even = [s for s in range(sources) if (s // members) % 2 == 0]
    odd = [s for s in range(sources) if (s // members) % 2 == 1]

    def stats(source):
        return got_ref[source, tokens // 2, 0:1, :] + got_ref[source, tokens // 2, 1:2, :]

    def tree(combine, values):
        while len(values) > 1:
            values = [combine(*values[i : i + 2]) if i + 1 < len(values) else values[i] for i in range(0, len(values), 2)]
        return values[0]

    chip_lse = [stats(s) for s in even]
    top = tree(jnp.maximum, chip_lse)
    page_lse = top + jnp.log(tree(jnp.add, [jnp.exp(c - top) for c in chip_lse]))
    spread = spread_runs(page_lse, half)
    flat = jnp.concatenate([spread[c : c + 1] for c in range(chunks)], axis=1)
    copies = []
    for page in range(local_pages):
        score = score_ref[page : page + 1, :]
        hit = score_ref[local_pages + page : local_pages + page + 1, :]
        coefficient = jnp.exp(score - flat) - hit
        grad_p = jnp.zeros((LANES, LANES), jnp.float32)
        for rows_ref, power_ref, inverse_ref in (near, far):
            factor = (coefficient * inverse_ref[page : page + 1, :] * power_ref[page]).astype(jnp.bfloat16)
            grad_p += jnp.dot(factor, rows_ref[...], preferred_element_type=jnp.float32)
        grad_p_ref[page] = grad_p
        copies.append(pltpu.make_async_copy(grad_p_ref.at[page], grad_p_out.at[page], sems.at[page]))
        copies[-1].start()

    lane = lax.broadcasted_iota(jnp.int32, (1, LANES), 1)
    mine = lane == (me % per_chunk) * half + me // per_chunk
    ratios = jnp.concatenate([jnp.where(mine, jnp.exp(c - page_lse), 0.0) for c in chip_lse], axis=0)
    ratios = jnp.sum(ratios, axis=1, keepdims=True) * (1.0 / HALF_SCALE)
    ratios = jnp.broadcast_to(ratios, ratios.shape[:1] + (LANES,))
    got_rows = got_ref.reshape(sources, tokens + EXTRA, LANES)
    terms = [ratios[i : i + 1, :] * got_rows[s, 0:tokens, :] for i, s in enumerate(even)]
    sums = tree(jnp.add, terms)
    single = tree(jnp.add, [got_rows[s, 0:tokens, :] for s in odd]) * (1.0 / HALF_SCALE)
    grad_q_ref[0, 0:half, :] = sums[0:half] - single[half:tokens]
    grad_q_ref[0, half:tokens, :] = sums[half:tokens] - single[0:half]
    copies.append(pltpu.make_async_copy(grad_q_ref, grad_q_out, sems.at[local_pages]))
    copies[-1].start()

    picked = tree(jnp.add, [stats(s) for s in odd])
    difference = jnp.where(lane % half < chunks, page_lse - picked, 0.0)
    loss_ref[...] = jnp.sum(difference, axis=1, keepdims=True) * (1.0 / sources)
    copies.append(pltpu.make_async_copy(loss_ref, loss_out, sems.at[local_pages + 1]))
    copies[-1].start()
    for copy in copies:
        copy.wait()


def exchange(blocks_to_all):
    return lax.all_to_all(blocks_to_all, ("blk", "group"), 0, 0, tiled=True)


def two_exchanges(queries, query_mask, positive, page_vectors, page_mask):
    tokens = queries.shape[1]
    local_pages = page_vectors.shape[0]
    devices = lax.axis_size("blk") * lax.axis_size("group")
    lanes = devices * tokens
    blocks = lax.axis_size("blk")
    half = tokens // 2
    pairs = (tokens + EXTRA) // 2
    swap = [(b, b ^ 1) for b in range(blocks)]

    vmem = pl.BlockSpec(memory_space=pltpu.VMEM)
    anywhere = pl.BlockSpec(memory_space=pl.ANY)
    params = pltpu.CompilerParams(vmem_limit_bytes=KERNEL_VMEM)
    told = pl.pallas_call(
        facts_kernel,
        out_shape=jax.ShapeDtypeStruct((EXTRA, LANES), jnp.float32),
        in_specs=[vmem] * 3,
        out_specs=vmem,
        compiler_params=params,
        cost_estimate=pl.CostEstimate(flops=1000000, bytes_accessed=10000, transcendentals=0),
    )(positive, query_mask, page_mask)
    message = pl.pallas_call(
        message_kernel,
        out_shape=jax.ShapeDtypeStruct((devices, (half + EXTRA) // 2, 2, LANES), jnp.bfloat16),
        in_specs=[vmem] * 2,
        out_specs=vmem,
        compiler_params=params,
    )(told, queries)
    sent = exchange(message)
    sent, page_vectors = lax.optimization_barrier((sent, page_vectors))
    other_vectors = lax.ppermute(page_vectors, "blk", swap)
    swapped = lax.ppermute(sent, "blk", swap)
    part = lanes // 2
    kept = (
        jax.ShapeDtypeStruct((part, LANES), jnp.bfloat16),
        jax.ShapeDtypeStruct((local_pages, LANES, part), jnp.float32),
        jax.ShapeDtypeStruct((local_pages, part), jnp.float32),
    )
    near_rows, near_powers, near_soft, near_inverses, facts, near_mix, flips = pl.pallas_call(
        near_kernel,
        out_shape=kept + (kept[2], jax.ShapeDtypeStruct((8, part), jnp.float32), kept[1], jax.ShapeDtypeStruct(page_vectors.shape, jnp.bfloat16)),
        in_specs=[vmem] * 2,
        out_specs=(vmem,) * 7,
        compiler_params=params,
        cost_estimate=pl.CostEstimate(flops=4 * part * LANES * LANES, bytes_accessed=2**20, transcendentals=part * LANES),
    )(sent, page_vectors)
    out, far_powers, scores, far_inverses, far_rows = pl.pallas_call(
        far_kernel,
        out_shape=(
            jax.ShapeDtypeStruct((devices, pairs, 2, LANES), jnp.float32),
            kept[1],
            jax.ShapeDtypeStruct((2 * local_pages, part), jnp.float32),
            kept[2],
            kept[0],
        ),
        in_specs=[vmem] * 10,
        out_specs=(vmem,) * 5,
        compiler_params=pltpu.CompilerParams(
            vmem_limit_bytes=KERNEL_VMEM
        ),
    )(sent, swapped, page_vectors, other_vectors, near_rows, near_mix, near_soft, near_inverses, facts, flips)
    got = exchange(out.astype(jnp.float16)).astype(jnp.float32)
    grad_q, grad_p, loss = pl.pallas_call(
        functools.partial(last_kernel, tokens),
        out_shape=(
            jax.ShapeDtypeStruct(queries.shape, jnp.float32),
            jax.ShapeDtypeStruct(page_vectors.shape, jnp.float32),
            jax.ShapeDtypeStruct((1, 1), jnp.float32),
        ),
        in_specs=[vmem] * 8,
        out_specs=(anywhere,) * 3,
        scratch_shapes=[
            pltpu.VMEM(queries.shape, jnp.float32),
            pltpu.VMEM(page_vectors.shape, jnp.float32),
            pltpu.VMEM((1, 1), jnp.float32),
            pltpu.SemaphoreType.DMA((local_pages + 2,)),
        ],
        compiler_params=params,
    )(got, scores, near_rows, near_powers, near_inverses, far_rows, far_powers, far_inverses)
    return (grad_q, grad_p, loss[0, 0])


def on_device(queries, query_mask, positive, page_vectors, page_mask):
    devices = lax.axis_size("blk") * lax.axis_size("group")
    chosen = two_exchanges if fits(queries, page_vectors, devices) else general_path
    return chosen(queries, query_mask, positive, page_vectors, page_mask)


def solution(mesh):
    in_specs = (
        P(("blk", "group"), None, None),
        P(("blk", "group"), None),
        P(("blk", "group")),
        P(("blk", "group"), None, None),
        P(("blk", "group"), None),
    )
    out_specs = (P(("blk", "group"), None, None), P(("blk", "group"), None, None), P())
    return jax.shard_map(
        on_device, mesh=mesh, in_specs=in_specs, out_specs=out_specs, check_vma=False
    )
```

```python
import functools
import math

import jax
import jax.numpy as jnp
from jax import lax
from jax.experimental import pallas as pl
from jax.experimental.pallas import tpu as pltpu
from jax.sharding import PartitionSpec as P

relaxation_scale_factor = 0.5
guarded_floor_entry = -1e30


def combined_all(part, axis, combine):
    gathered = jax.tree.map(lambda a: lax.all_gather(a, axis), part)

    def take(source):
        return jax.tree.map(lambda a: lax.dynamic_index_in_dim(a, source, 0, False), gathered)

    return lax.fori_loop(
        1, lax.axis_size(axis), lambda source, state: combine(state, take(source)), take(0)
    )


def from_behind(value, axis, steps):
    count = lax.axis_size(axis)
    pairs = [(source, (source + steps) % count) for source in range(count)]
    return lax.ppermute(value, axis, pairs)


def masked_logits(row_block, lone_document, live_image_embeddings):
    similarity_matrix = lax.dot_general(
        row_block, lone_document, (((1,), (1,)), ((), ())), preferred_element_type=jnp.float32
    )
    return jnp.where(
        live_image_embeddings[None, :] > 0,
        similarity_matrix / relaxation_scale_factor,
        guarded_floor_entry,
    )


def combine_parts(earlier, later):
    highest = jnp.maximum(earlier[0], later[0])
    totals = earlier[1] * jnp.exp(earlier[0] - highest) + later[1] * jnp.exp(later[0] - highest)
    return (highest, totals, earlier[2] + later[2])


def general_path(queries, query_mask, positive, page_vectors, page_mask):
    tokens = queries.shape[1]
    features = queries.shape[2]
    local_pages = page_vectors.shape[0]
    blocks = lax.axis_size("blk")
    members = lax.axis_size("group")
    bundle_size = queries.shape[0] * members
    total_queries = bundle_size * blocks
    natural_logarithm_lengths = jnp.log(jnp.sum(page_mask.astype(jnp.float32), axis=1))
    bundle_vectors, bundle_masks, bundle_targets = (
        lax.all_gather(queries, "group", axis=0, tiled=True),
        lax.all_gather(query_mask, "group", axis=0, tiled=True),
        lax.all_gather(positive, "group", axis=0, tiled=True),
    )

    def forward_piece(folded, shard_in, root_row):
        scores, lse_rows, live_all, owners, kept = folded
        vectors, token_masks, targets = shard_in
        amount = vectors.shape[0]
        stride = math.gcd(amount, max(1, 512 // tokens))

        def run_block(number, current):
            scores, lse_rows = current
            offset = number * stride
            slab_rows = lax.dynamic_slice_in_dim(vectors, offset, stride, 0).reshape(
                stride * tokens, features
            )
            alive = lax.dynamic_slice_in_dim(token_masks, offset, stride, 0).astype(jnp.float32)
            found_sums = []
            for index_page in range(local_pages):
                masked = masked_logits(slab_rows, page_vectors[index_page], page_mask[index_page])
                highest = jnp.max(masked, axis=1, keepdims=True)
                found_sums.append(
                    highest[:, 0] + jnp.log(jnp.sum(jnp.exp(masked - highest), axis=1))
                )
            logsumexp_results = jnp.stack(found_sums, axis=1).reshape(stride, tokens, local_pages)
            softened_supremum = relaxation_scale_factor * (
                logsumexp_results - natural_logarithm_lengths
            )
            page_score = jnp.sum(alive[:, :, None] * softened_supremum, axis=1)
            scores = lax.dynamic_update_slice_in_dim(scores, page_score, offset, 0)
            lse_rows = lax.dynamic_update_slice_in_dim(lse_rows, logsumexp_results, offset, 0)
            return (scores, lse_rows)

        scores, lse_rows = lax.fori_loop(0, amount // stride, run_block, (scores, lse_rows))
        live_all = lax.dynamic_update_slice_in_dim(live_all, token_masks, root_row, 0)
        owners = lax.dynamic_update_slice_in_dim(owners, targets, root_row, 0)
        kept = vectors
        return (scores, lse_rows, live_all, owners, kept)

    starting = (
        jnp.zeros((total_queries, local_pages), jnp.float32),
        jnp.zeros((total_queries, tokens, local_pages), jnp.float32),
        jnp.zeros((total_queries, tokens), jnp.int32),
        jnp.zeros((total_queries,), jnp.int32),
        jnp.zeros((total_queries, tokens, features), jnp.bfloat16),
    )
    scores, lse_rows, live_all, owners, kept = forward_piece(
        starting,
        (
            lax.all_gather(bundle_vectors, "blk", axis=0, tiled=True),
            lax.all_gather(bundle_masks, "blk", axis=0, tiled=True),
            lax.all_gather(bundle_targets, "blk", axis=0, tiled=True),
        ),
        jnp.int32(0),
    )
    position = lax.axis_index(("blk", "group"))
    page_ids = position * local_pages + jnp.arange(local_pages, dtype=jnp.int32)
    chosen = owners[:, None] == page_ids[None, :]
    picked_local = jnp.sum(jnp.where(chosen, scores, 0.0))
    local_top = jnp.max(scores, axis=1)
    local_total = jnp.sum(jnp.exp(scores - local_top[:, None]), axis=1)
    highest, totals, picked = combined_all(
        (local_top, local_total, picked_local), ("blk", "group"), combine_parts
    )
    page_lse = highest + jnp.log(totals)
    mean_loss = (jnp.sum(page_lse) - picked) / total_queries
    coefficient = jnp.exp(scores - page_lse[:, None]) - chosen.astype(jnp.float32)
    factor_scale = coefficient[:, None, :] * live_all.astype(jnp.float32)[:, :, None]

    def slice_rows(root_row, amount):
        sums = lax.dynamic_slice_in_dim(lse_rows, root_row, amount, 0).reshape(
            amount * tokens, local_pages
        )
        scales = lax.dynamic_slice_in_dim(factor_scale, root_row, amount, 0).reshape(
            amount * tokens, local_pages
        )
        return (sums, scales)

    def gradient_terms(row_block, logsumexp_results, scales, page_grads):
        partial_value = jnp.zeros(row_block.shape, jnp.float32)
        for number in range(local_pages):
            masked = masked_logits(row_block, page_vectors[number], page_mask[number])
            weights = jnp.exp(masked - logsumexp_results[:, number : number + 1])
            factor = (scales[:, number : number + 1] * weights).astype(jnp.bfloat16)
            partial_value = partial_value + jnp.dot(
                factor, page_vectors[number], preferred_element_type=jnp.float32
            )
            update = lax.dot_general(
                factor, row_block, (((0,), (0,)), ((), ())), preferred_element_type=jnp.float32
            )
            page_grads = page_grads.at[number].add(update)
        return (partial_value, page_grads)

    home = lax.axis_index("blk")
    page_grads = jnp.zeros(page_vectors.shape, jnp.float32)

    def visit_one(moving, collected, page_grads, lap_index):
        root_row = (home - lap_index) % blocks * bundle_size
        sums, scales = slice_rows(root_row, bundle_size)
        partial_value, page_grads = gradient_terms(
            moving.reshape(bundle_size * tokens, features), sums, scales, page_grads
        )
        return (collected + partial_value.reshape(bundle_size, tokens, features), page_grads)

    def pass_one(collected):
        return from_behind(collected, "blk", 1)

    def turn_one(lap_index, current):
        moving, collected, page_grads = current
        collected, page_grads = visit_one(moving, collected, page_grads, lap_index)
        moving = from_behind(moving, "blk", 1)
        return (moving, pass_one(collected), page_grads)

    empty_whole = jnp.zeros((bundle_size, tokens, features), jnp.float32)
    moving, collected, page_grads = lax.fori_loop(
        0, blocks - 1, turn_one, (bundle_vectors, empty_whole, page_grads)
    )
    collected, page_grads = visit_one(moving, collected, page_grads, blocks - 1)
    collected = pass_one(collected)
    grad_queries = lax.psum_scatter(collected, "group", scatter_dimension=0, tiled=True)
    return (grad_queries, page_grads, mean_loss)


LANES = 128
EXTRA = 2
FACTS = 16
KERNEL_VMEM = 16 * 2**20
HALF_SCALE = 2.0**14


def fits(queries, page_vectors, devices):
    tokens, features = queries.shape[1:]
    lanes = devices * tokens
    return (
        queries.shape[0] == 1
        and tokens == FACTS
        and features == LANES
        and page_vectors.shape[1] == LANES
        and page_vectors.shape[0] <= FACTS - 3
        and lanes % LANES == 0
        and lanes // LANES <= 8
        and lax.axis_size("blk") % 2 == 0
    )


def segment_sum(values, width):
    lanes = values.shape[1]
    lane = lax.broadcasted_iota(jnp.int32, values.shape, 1)
    rows, pieces = values.shape[0], lanes // LANES
    if rows * pieces == 8:
        packed = jnp.concatenate([values[:, c * LANES : (c + 1) * LANES] for c in range(pieces)], axis=0)
        place = lax.broadcasted_iota(jnp.int32, packed.shape, 1)
        step = 1
        while step < width:
            packed = packed + jnp.take_along_axis(packed, place ^ step, axis=1)
            step *= 2
        return jnp.concatenate([packed[c * rows : (c + 1) * rows] for c in range(pieces)], axis=1)
    step = 1
    while step < width:
        ahead = pltpu.roll(values, lanes - step, 1)
        behind = pltpu.roll(values, step, 1)
        values = values + jnp.where((lane & step) == 0, ahead, behind)
        step *= 2
    return values


def spread_runs(line, width):
    lane = lax.broadcasted_iota(jnp.int32, (8, LANES), 1)
    row = lax.broadcasted_iota(jnp.int32, (8, LANES), 0)
    return jnp.take_along_axis(jnp.broadcast_to(line, (8, LANES)), lane // width * width + row, axis=1)


def split_half(value):
    scaled = value * 8193.0
    high = scaled - (scaled - value)
    return high, value - high


def facts_kernel(target_ref, query_mask_ref, page_mask_ref, facts_ref):
    half = query_mask_ref.shape[1] // 2
    alive = jnp.sum(query_mask_ref[...].astype(jnp.float32), axis=1, keepdims=True)
    kind = lax.broadcasted_iota(jnp.int32, (EXTRA, LANES), 1) % half
    number = target_ref[...].reshape(1, 1)
    facts = jnp.where(kind == 0, alive, 0.0)
    facts = jnp.where(kind == 1, (number >> 8).astype(jnp.float32), facts)
    facts = jnp.where(kind == 2, (number & 255).astype(jnp.float32), facts)
    for page in range(page_mask_ref.shape[0]):
        count = jnp.sum(page_mask_ref[page : page + 1, :].astype(jnp.float32), axis=1, keepdims=True)
        facts = jnp.where(kind == 3 + page, count, facts)
    facts_ref[...] = facts


def message_kernel(facts_ref, queries_ref, out_ref):
    devices = out_ref.shape[0]
    half = queries_ref.shape[1] // 2
    members = lax.axis_size("group")
    out_rows = out_ref.reshape(devices, half + EXTRA, LANES)
    for device in range(devices):
        begin = (device // members) % 2 * half
        out_rows[device, 0:half, :] = queries_ref[0, begin : begin + half, :]
    out_ref[:, half // 2] = jnp.broadcast_to(facts_ref[...].astype(jnp.bfloat16)[None], (devices, EXTRA, LANES))


def measure_pages(rows_q, vectors, flips, counts, alive, powers_ref=None):
    width = rows_q.shape[0]
    patch = lax.broadcasted_iota(jnp.int32, (LANES, width), 0).astype(jnp.float32)
    steep = 1.0 / (relaxation_scale_factor * math.log(2.0))
    softened, inverses, mixes = [], [], []
    stack = jnp.concatenate(vectors, axis=0)
    similarities = lax.dot_general(stack, rows_q, (((1,), (1,)), ((), ())), preferred_element_type=jnp.float32)
    for page, (flipped, count) in enumerate(zip(flips, counts)):
        similarity = similarities[page * LANES : (page + 1) * LANES]
        masked = jnp.where(patch < count, similarity, guarded_floor_entry)
        highest = jnp.max(masked, axis=0, keepdims=True)
        powers = jnp.exp2((masked - highest) * steep)
        if powers_ref is not None:
            powers_ref[page] = powers
        high = powers.astype(jnp.bfloat16)
        low = (powers - high.astype(jnp.float32)).astype(jnp.bfloat16)
        mixes.append(
            jnp.dot(
                jnp.concatenate([flipped, flipped], axis=1),
                jnp.concatenate([high, low], axis=0),
                preferred_element_type=jnp.float32,
            )
        )
        total = jnp.sum(powers, axis=0, keepdims=True)
        lse = highest * (1.0 / relaxation_scale_factor) + jnp.log(total)
        softened.append(alive * (relaxation_scale_factor * (lse - jnp.log(count))))
        inverses.append(alive / total)
    return softened, inverses, mixes


def gather_rows(from_ref, to_ref):
    sources = from_ref.shape[0]
    half = 2 * (from_ref.shape[1] - 1)
    view = from_ref.reshape(sources, half + EXTRA, LANES)
    for source in range(sources):
        to_ref[source * half : (source + 1) * half, :] = view[source, 0:half, :]


def page_counts(sent_ref, home, local_pages):
    facts = sent_ref[home, sent_ref.shape[1] - 1].astype(jnp.float32)
    return [facts[0:1, 3 + number : 4 + number] for number in range(local_pages)]


def near_kernel(sent_ref, own_ref, rows_ref, power_ref, soft_ref, inverse_ref, facts_ref, mix_ref, flip_ref):
    sources = sent_ref.shape[0]
    half = 2 * (sent_ref.shape[1] - 1)
    part = sources * half
    per_chunk = LANES // half
    local_pages = own_ref.shape[0]
    blk = lax.axis_index("blk")
    home = blk * lax.axis_size("group") + lax.axis_index("group")
    slot = lax.broadcasted_iota(jnp.int32, (1, LANES), 1) // half
    facts = []
    for c in range(part // LANES):
        told = jnp.zeros((1, LANES), jnp.float32)
        for i in range(per_chunk):
            told = jnp.where(slot == i, sent_ref[c * per_chunk + i, half // 2, 0:1, :].astype(jnp.float32), told)
        facts.append(spread_runs(told, half))
    facts = jnp.concatenate(facts, axis=1)
    facts_ref[...] = facts
    token = lax.broadcasted_iota(jnp.int32, (1, part), 1) % half + (blk & 1) * half
    alive = (token.astype(jnp.float32) < facts[0:1]).astype(jnp.float32)
    gather_rows(sent_ref, rows_ref)
    vectors = [own_ref[page] for page in range(local_pages)]
    flips = [block.T for block in vectors]
    softened, inverses, mixes = measure_pages(
        rows_ref[...], vectors, flips, page_counts(sent_ref, home, local_pages), alive, power_ref
    )
    for page in range(local_pages):
        mix_ref[page] = mixes[page]
        flip_ref[page] = flips[page]
        soft_ref[page : page + 1, :] = softened[page]
        inverse_ref[page : page + 1, :] = inverses[page]


def far_kernel(*refs):
    sent_ref, swapped_ref, own_ref, other_ref, near_rows_ref, near_mix_ref, near_soft_ref, near_inverse_ref = refs[:8]
    facts_ref, flip_ref, out_ref, power_ref, score_ref, inverse_ref, rows_ref = refs[8:]
    sources = sent_ref.shape[0]
    half = 2 * (sent_ref.shape[1] - 1)
    part = sources * half
    local_pages = own_ref.shape[0]
    blk = lax.axis_index("blk")
    group = lax.axis_index("group")
    members = lax.axis_size("group")
    homes = [blk * members + group, (blk ^ 1) * members + group]
    side = blk & 1
    sends_sum = side == 0
    own_range = range(local_pages)
    ids = [home * local_pages + page for home in homes for page in own_range]
    own = [own_ref[page] for page in own_range]
    other = [other_ref[page] for page in own_range]
    own_flips = [flip_ref[page] for page in own_range]
    other_flips = [block.T for block in other]
    own_counts = page_counts(sent_ref, homes[0], local_pages)
    other_counts = page_counts(sent_ref, homes[1], local_pages)

    facts = facts_ref[...]
    target = (facts[1:2] * 256.0 + facts[2:3]).astype(jnp.int32)
    spot = lax.broadcasted_iota(jnp.int32, (1, part), 1) % half
    near_alive = ((spot + side * half).astype(jnp.float32) < facts[0:1]).astype(jnp.float32)
    far_alive = ((spot + (1 - side) * half).astype(jnp.float32) < facts[0:1]).astype(jnp.float32)
    other_soft, other_inverse, other_mix = measure_pages(near_rows_ref[...], other, other_flips, other_counts, near_alive)
    gather_rows(swapped_ref, rows_ref)
    rows_q = rows_ref[...]
    far_soft, far_inverse, far_mix = measure_pages(rows_q, own, own_flips, own_counts, far_alive, power_ref)
    cross_soft, cross_inverse, cross_mix = measure_pages(rows_q, other, other_flips, other_counts, far_alive)
    near_mix = [near_mix_ref[page] for page in own_range]
    near_soft = [near_soft_ref[page : page + 1, :] for page in own_range]
    near_inverse = [near_inverse_ref[page : page + 1, :] for page in own_range]
    for page in own_range:
        inverse_ref[page : page + 1, :] = far_inverse[page]
    softened = [a + b for a, b in zip(near_soft + other_soft, far_soft + cross_soft)]
    scores = segment_sum(jnp.concatenate(softened, axis=0), half)
    top = jnp.max(scores, axis=0, keepdims=True)
    chip_lse = top + jnp.log(jnp.sum(jnp.exp(scores - top), axis=0, keepdims=True))

    picked = jnp.zeros((1, part), jnp.float32)
    shares = []
    for page, name in enumerate(ids):
        score = scores[page : page + 1]
        hit = target == name
        picked = picked + jnp.where(hit, score, 0.0)
        shares.append(jnp.where(sends_sum, jnp.exp(score - chip_lse), hit.astype(jnp.float32)))
        if page < local_pages:
            score_ref[page : page + 1, :] = score
            score_ref[local_pages + page : local_pages + page + 1, :] = hit.astype(jnp.float32)
    high, low = split_half(jnp.where(sends_sum, chip_lse, picked))
    high_line = jnp.zeros((1, LANES), jnp.float32)
    low_line = jnp.zeros((1, LANES), jnp.float32)
    for c in range(part // LANES):
        high_line = jnp.where(spot[:, 0:LANES] == c, high[:, c * LANES : (c + 1) * LANES], high_line)
        low_line = jnp.where(spot[:, 0:LANES] == c, low[:, c * LANES : (c + 1) * LANES], low_line)
    lines = jnp.concatenate([high_line, low_line], axis=0)
    out_ref[:, half] = jnp.broadcast_to(lines[None], (sources, EXTRA, LANES))

    out_rows = out_ref.reshape(sources, 2 * half + EXTRA, LANES)
    for position, (mixes, inverses) in enumerate(
        ((near_mix + other_mix, near_inverse + other_inverse), (far_mix + cross_mix, far_inverse + cross_inverse))
    ):
        mixed = sum(mix * (inverse * (share * HALF_SCALE)) for mix, inverse, share in zip(mixes, inverses, shares))
        mixed = mixed.T
        for source in range(sources):
            out_rows[source, position * half : (position + 1) * half, :] = mixed[
                source * half : (source + 1) * half, :
            ]


def last_kernel(tokens, got_ref, score_ref, *rest):
    near, far, results = rest[0:3], rest[3:6], rest[6:]
    grad_q_out, grad_p_out, loss_out, grad_q_ref, grad_p_ref, loss_ref, sems = results
    sources = got_ref.shape[0]
    half = tokens // 2
    chunks = sources * half // LANES
    per_chunk = LANES // half
    local_pages = grad_p_ref.shape[0]
    blk = lax.axis_index("blk")
    group = lax.axis_index("group")
    members = lax.axis_size("group")
    me = blk * members + group
    even = [s for s in range(sources) if (s // members) % 2 == 0]
    odd = [s for s in range(sources) if (s // members) % 2 == 1]

    def stats(source):
        return got_ref[source, tokens // 2, 0:1, :] + got_ref[source, tokens // 2, 1:2, :]

    def tree(combine, values):
        while len(values) > 1:
            values = [combine(*values[i : i + 2]) if i + 1 < len(values) else values[i] for i in range(0, len(values), 2)]
        return values[0]

    chip_lse = [stats(s) for s in even]
    top = tree(jnp.maximum, chip_lse)
    page_lse = top + jnp.log(tree(jnp.add, [jnp.exp(c - top) for c in chip_lse]))
    spread = spread_runs(page_lse, half)
    flat = jnp.concatenate([spread[c : c + 1] for c in range(chunks)], axis=1)
    copies = []
    for page in range(local_pages):
        score = score_ref[page : page + 1, :]
        hit = score_ref[local_pages + page : local_pages + page + 1, :]
        coefficient = jnp.exp(score - flat) - hit
        grad_p = jnp.zeros((LANES, LANES), jnp.float32)
        for rows_ref, power_ref, inverse_ref in (near, far):
            factor = (coefficient * inverse_ref[page : page + 1, :] * power_ref[page]).astype(jnp.bfloat16)
            grad_p += jnp.dot(factor, rows_ref[...], preferred_element_type=jnp.float32)
        grad_p_ref[page] = grad_p
        copies.append(pltpu.make_async_copy(grad_p_ref.at[page], grad_p_out.at[page], sems.at[page]))
        copies[-1].start()

    lane = lax.broadcasted_iota(jnp.int32, (1, LANES), 1)
    mine = lane == (me % per_chunk) * half + me // per_chunk
    ratios = jnp.concatenate([jnp.where(mine, jnp.exp(c - page_lse), 0.0) for c in chip_lse], axis=0)
    ratios = jnp.sum(ratios, axis=1, keepdims=True) * (1.0 / HALF_SCALE)
    ratios = jnp.broadcast_to(ratios, ratios.shape[:1] + (LANES,))
    got_rows = got_ref.reshape(sources, tokens + EXTRA, LANES)
    terms = [ratios[i : i + 1, :] * got_rows[s, 0:tokens, :] for i, s in enumerate(even)]
    sums = tree(jnp.add, terms)
    single = tree(jnp.add, [got_rows[s, 0:tokens, :] for s in odd]) * (1.0 / HALF_SCALE)
    grad_q_ref[0, 0:half, :] = sums[0:half] - single[half:tokens]
    grad_q_ref[0, half:tokens, :] = sums[half:tokens] - single[0:half]
    copies.append(pltpu.make_async_copy(grad_q_ref, grad_q_out, sems.at[local_pages]))
    copies[-1].start()

    picked = tree(jnp.add, [stats(s) for s in odd])
    difference = jnp.where(lane % half < chunks, page_lse - picked, 0.0)
    loss_ref[...] = jnp.sum(difference, axis=1, keepdims=True) * (1.0 / sources)
    copies.append(pltpu.make_async_copy(loss_ref, loss_out, sems.at[local_pages + 1]))
    copies[-1].start()
    for copy in copies:
        copy.wait()


def exchange(blocks_to_all):
    return lax.all_to_all(blocks_to_all, ("blk", "group"), 0, 0, tiled=True)


def two_exchanges(queries, query_mask, positive, page_vectors, page_mask):
    tokens = queries.shape[1]
    local_pages = page_vectors.shape[0]
    devices = lax.axis_size("blk") * lax.axis_size("group")
    lanes = devices * tokens
    blocks = lax.axis_size("blk")
    half = tokens // 2
    pairs = (tokens + EXTRA) // 2
    swap = [(b, b ^ 1) for b in range(blocks)]

    vmem = pl.BlockSpec(memory_space=pltpu.VMEM)
    anywhere = pl.BlockSpec(memory_space=pl.ANY)
    params = pltpu.CompilerParams(vmem_limit_bytes=KERNEL_VMEM)
    told = pl.pallas_call(
        facts_kernel,
        out_shape=jax.ShapeDtypeStruct((EXTRA, LANES), jnp.float32),
        in_specs=[vmem] * 3,
        out_specs=vmem,
        compiler_params=params,
        cost_estimate=pl.CostEstimate(flops=1000000, bytes_accessed=10000, transcendentals=0),
    )(positive, query_mask, page_mask)
    message = pl.pallas_call(
        message_kernel,
        out_shape=jax.ShapeDtypeStruct((devices, (half + EXTRA) // 2, 2, LANES), jnp.bfloat16),
        in_specs=[vmem] * 2,
        out_specs=vmem,
        compiler_params=params,
    )(told, queries)
    sent = exchange(message)
    sent, page_vectors = lax.optimization_barrier((sent, page_vectors))
    other_vectors = lax.ppermute(page_vectors, "blk", swap)
    swapped = lax.ppermute(sent, "blk", swap)
    part = lanes // 2
    kept = (
        jax.ShapeDtypeStruct((part, LANES), jnp.bfloat16),
        jax.ShapeDtypeStruct((local_pages, LANES, part), jnp.float32),
        jax.ShapeDtypeStruct((local_pages, part), jnp.float32),
    )
    near_rows, near_powers, near_soft, near_inverses, facts, near_mix, flips = pl.pallas_call(
        near_kernel,
        out_shape=kept + (kept[2], jax.ShapeDtypeStruct((8, part), jnp.float32), kept[1], jax.ShapeDtypeStruct(page_vectors.shape, jnp.bfloat16)),
        in_specs=[vmem] * 2,
        out_specs=(vmem,) * 7,
        compiler_params=params,
        cost_estimate=pl.CostEstimate(flops=4 * part * LANES * LANES, bytes_accessed=2**20, transcendentals=part * LANES),
    )(sent, page_vectors)
    out, far_powers, scores, far_inverses, far_rows = pl.pallas_call(
        far_kernel,
        out_shape=(
            jax.ShapeDtypeStruct((devices, pairs, 2, LANES), jnp.float32),
            kept[1],
            jax.ShapeDtypeStruct((2 * local_pages, part), jnp.float32),
            kept[2],
            kept[0],
        ),
        in_specs=[vmem] * 10,
        out_specs=(vmem,) * 5,
        compiler_params=pltpu.CompilerParams(
            vmem_limit_bytes=KERNEL_VMEM
        ),
    )(sent, swapped, page_vectors, other_vectors, near_rows, near_mix, near_soft, near_inverses, facts, flips)
    got = exchange(out.astype(jnp.float16)).astype(jnp.float32)
    grad_q, grad_p, loss = pl.pallas_call(
        functools.partial(last_kernel, tokens),
        out_shape=(
            jax.ShapeDtypeStruct(queries.shape, jnp.float32),
            jax.ShapeDtypeStruct(page_vectors.shape, jnp.float32),
            jax.ShapeDtypeStruct((1, 1), jnp.float32),
        ),
        in_specs=[vmem] * 8,
        out_specs=(anywhere,) * 3,
        scratch_shapes=[
            pltpu.VMEM(queries.shape, jnp.float32),
            pltpu.VMEM(page_vectors.shape, jnp.float32),
            pltpu.VMEM((1, 1), jnp.float32),
            pltpu.SemaphoreType.DMA((local_pages + 2,)),
        ],
        compiler_params=params,
    )(got, scores, near_rows, near_powers, near_inverses, far_rows, far_powers, far_inverses)
    return (grad_q, grad_p, loss[0, 0])


def on_device(queries, query_mask, positive, page_vectors, page_mask):
    devices = lax.axis_size("blk") * lax.axis_size("group")
    chosen = two_exchanges if fits(queries, page_vectors, devices) else general_path
    return chosen(queries, query_mask, positive, page_vectors, page_mask)


def solution(mesh):
    in_specs = (
        P(("blk", "group"), None, None),
        P(("blk", "group"), None),
        P(("blk", "group")),
        P(("blk", "group"), None, None),
        P(("blk", "group"), None),
    )
    out_specs = (P(("blk", "group"), None, None), P(("blk", "group"), None, None), P())
    return jax.shard_map(
        on_device, mesh=mesh, in_specs=in_specs, out_specs=out_specs, check_vma=False
    )
```
